32 devices in a mesh: band: 16 (over z, y, x), lev: 2 (over core).
Axes of the slice: x: 2, y: 2, z: 4, core: 2. Of those that a mesh axis runs over, the one named last changes fastest.
Arguments:
- spectral: bfloat16 [1280, 2, 2, 3, 1280], P('band', None, 'lev'), may hold values from -0.08984375 to 0.08984375
- legendre: bfloat16 [1280, 16, 1280], P('band'), may hold values from -0.15625 to 0.15625
- level_weights: float32 [2], P('lev'), may hold values from 0.1 to 0.6
- coupling: int32 [64, 128], P('band'), may hold values from 0 to 8191
- land_sea: int32 [64, 128], P('band'), may hold values 0 or 1
- spectra: bfloat16 [36, 36, 64, 128], P('lev', None, 'band'), may hold values from 0.049804688 to 2
- courant: float32 [36], P('lev'), may hold values from 0.1 to 0.65
- growth_rate: float32 [36], P('lev'), may hold values from 0.05 to 0.5
- breaking: float32 [36], P('lev'), may hold values from 0.1 to 1
Outputs:
- grid: float32 [16, 2, 3, 512], P('band', 'lev')
- spectra_out: float32 [36, 36, 64, 128], P('lev', None, 'band')
- charnock: float32 [64, 128], P('band')
The draws below stay inside these ranges and needn't reach their ends.
All inputs are finite; a program needn't handle non-finite values. No bound on the sum of `land_sea` on one device may be relied on, other than what follows from the above.
Results may differ from the reference program's by a relative error of at most 0.0029.
Values may be sent and summed in bfloat16 or wider, within the bound.
No kernel may reach another device: no remote copies, remote signals or barrier semaphores. Data moves between devices by JAX's collectives and lax.ppermute only.
A program may use at most 64 MiB of HBM per device.

```python
import math
import jax
import jax.numpy as jnp
from jax import lax

M = 1280
N = 1280
NLON = 5136
LON_W = 512
NF = 36
ND = 36
WC = 128
STEPS = 4
NLAT_W = 16
LEVELS = 2
WROWS = 64
N_BAND = 16


def touch_ends(values, stream_key, low, largest):
    longest = values.shape.index(max(values.shape))
    spots = []
    for shift in (0, 1):
        where = [jax.random.randint(jax.random.fold_in(stream_key, axis), (), 0, length) for axis, length in enumerate(values.shape)]
        where[longest] = (where[longest] + shift) % values.shape[longest]
        spots.append(tuple(where))
    return values.at[spots[0]].set(low).at[spots[1]].set(largest)


def block_levels(rng, dims, pieces, smallest, largest):
    def one(axis_at, parts):
        heights = jax.random.uniform(jax.random.fold_in(jax.random.fold_in(rng, 6), axis_at), (parts,), jnp.float32, smallest / len(pieces), largest / len(pieces))
        return jnp.repeat(jnp.exp(heights), dims[axis_at] // parts).reshape((-1,) + (1,) * (len(dims) - axis_at - 1))

    gain = one(*pieces[0])
    for cut in pieces[1:]:
        gain = gain * one(*cut)
    return gain


def bell_draw(own_key, shape, width, most, cuts=(), held_as=jnp.bfloat16):
    loudness = block_levels(own_key, shape, cuts, -0.22, 0.18) if cuts else 1.0
    entries = jax.random.normal(own_key, shape, jnp.float32) * width * loudness
    return jnp.minimum(jnp.maximum(entries, -most), most).astype(held_as)


def setup_inputs(seed: int = 0) -> dict:
    arg_keys = jax.random.split(jax.random.key(seed), 10)
    spectral = bell_draw(arg_keys[0], (M, 2, LEVELS, 3, N), 0.014, 0.08984375, ((0, 16), (2, 2)))
    legendre = bell_draw(arg_keys[1], (M, NLAT_W, N), N ** -0.5, 0.15625, ((0, 16),))
    level_weights = jnp.clip(jnp.exp(math.log(0.6) - 1.7917595 * jax.random.uniform(arg_keys[2], (LEVELS,), jnp.float32) ** block_levels(arg_keys[2], (LEVELS,), ((0, 2),), -0.2, 0.2)), 0.1, 0.6)
    coupling = touch_ends(jax.random.randint(arg_keys[3], (WROWS, WC), 0, NLAT_W * LON_W), jax.random.fold_in(arg_keys[3], 1), 0, (NLAT_W * LON_W) - 1).astype(jnp.int32)
    land_sea = touch_ends((jax.random.randint(arg_keys[4], (WROWS, WC), 0, 4) < 3).astype(jnp.int32), jax.random.fold_in(arg_keys[4], 1), 0, 1)
    spectra = jnp.clip(jnp.exp(math.log(2.0) - 3.6927934 * jax.random.uniform(arg_keys[5], (NF, ND, WROWS, WC), jnp.float32) ** block_levels(arg_keys[5], (NF, ND, WROWS, WC), ((0, 2), (2, 16)), -0.2, 0.2)), 0.049804688, 2.0).astype(jnp.bfloat16)
    courant = jnp.clip(jnp.exp(math.log(0.65) - 1.8718021 * jax.random.uniform(arg_keys[6], (NF,), jnp.float32) ** block_levels(arg_keys[6], (NF,), ((0, 2),), -0.2, 0.2)), 0.1, 0.65)
    growth_rate = jnp.clip(jnp.exp(math.log(0.5) - 2.3025851 * jax.random.uniform(arg_keys[7], (NF,), jnp.float32) ** block_levels(arg_keys[7], (NF,), ((0, 2),), -0.2, 0.2)), 0.05, 0.5)
    breaking = jnp.clip(jnp.exp(math.log(1.0) - 2.3025851 * jax.random.uniform(arg_keys[8], (NF,), jnp.float32) ** block_levels(arg_keys[8], (NF,), ((0, 2),), -0.2, 0.2)), 0.1, 1.0)
    return dict(spectral=spectral, legendre=legendre, level_weights=level_weights, coupling=coupling, land_sea=land_sea, spectra=spectra, courant=courant, growth_rate=growth_rate, breaking=breaking)


def fourier_basis(first, count):
    waves = first + jnp.arange(count, dtype=jnp.int32)
    columns = jnp.arange(LON_W, dtype=jnp.int32)
    remains = (waves[:, None] * columns[None, :]) % NLON
    angles = (2.0 * math.pi / NLON) * remains.astype(jnp.float32)
    weights = jnp.where(waves == 0, 1.0, 2.0).astype(jnp.float32)[:, None]
    return jnp.stack([weights * jnp.cos(angles), -weights * jnp.sin(angles)])


def advance(padded, east_speed, north_speed):
    centre = padded[..., 1:-1, :]
    below = padded[..., :-2, :]
    above = padded[..., 2:, :]
    west = jnp.roll(centre, 1, axis=-1)
    east = jnp.roll(centre, -1, axis=-1)
    return (centre - jnp.maximum(east_speed, 0.0) * (centre - west)
            - jnp.minimum(east_speed, 0.0) * (east - centre)
            - jnp.maximum(north_speed, 0.0) * (centre - below)
            - jnp.minimum(north_speed, 0.0) * (above - centre))


def reference(spectral, legendre, level_weights, coupling, land_sea, spectra, courant, growth_rate, breaking):
    blocks = N_BAND
    block_size = M // blocks
    table = legendre.reshape(blocks, block_size, NLAT_W, N)
    stacked = spectral.reshape(blocks, block_size, 2 * LEVELS * 3, N)

    def one_block(pair):
        return lax.dot_general(pair[1], pair[0], (((2,), (2,)), ((0,), (0,))),
                               preferred_element_type=jnp.float32).astype(jnp.bfloat16)

    legendre_out = lax.map(one_block, (table, stacked)).reshape(M, 2, LEVELS * 3, NLAT_W)
    legendre_out = lax.optimization_barrier(legendre_out)
    basis = fourier_basis(0, M)
    grid = jnp.einsum("mrfl,rmx->lfx", legendre_out.astype(jnp.float32), basis,
                      precision=lax.Precision.HIGHEST)
    grid = grid.reshape(NLAT_W, LEVELS, 3, LON_W)
    wind = jnp.sum(grid[:, :, 0:2, :] * level_weights[None, :, None, None], axis=1)
    wind_east = jnp.take(wind[:, 0, :].reshape(-1), coupling)
    wind_north = jnp.take(wind[:, 1, :].reshape(-1), coupling)

    theta = (2.0 * math.pi / ND) * (jnp.arange(ND).astype(jnp.float32) + 0.5)
    cosines = jnp.cos(theta)[:, None, None]
    sines = jnp.sin(theta)[:, None, None]
    push = jnp.maximum(cosines * wind_east[None] + sines * wind_north[None], 0.0)
    landmask = land_sea.astype(jnp.float32)
    energy = 1.0 + 2.0 * jnp.arange(NF).astype(jnp.float32) / (NF - 1)

    def one_frequency(items):
        field, speed, rate, damping, weight = items
        state = field.astype(jnp.float32)
        for step in range(STEPS):
            padded = jnp.pad(state, ((0, 0), (1, 1), (0, 0)))
            state = advance(padded, speed * cosines, speed * sines)
        growth = rate * push
        result = landmask * state * (1.0 + growth) / (1.0 + damping * state)
        partial_value = weight * jnp.sum(growth * state, axis=0) * landmask
        return result, partial_value

    spectra_out, partials = lax.map(one_frequency, (spectra, courant, growth_rate, breaking, energy))
    stress = jnp.sum(partials, axis=0) / (NF * ND)
    charnock = 0.011 + 0.5 * stress / (stress + 0.05 * (1.0 + wind_east * wind_east + wind_north * wind_north))
    return grid, spectra_out, charnock
```

```python
import functools
import math

import jax
import jax.numpy as jnp
from jax import lax
from jax.experimental import pallas as pl
from jax.experimental.pallas import tpu as pltpu
from jax.sharding import PartitionSpec as P

NLON = 5136
LON_W = 512
NF = 36
STEPS = 4
FIELDS = 3

VMEM = pl.BlockSpec(memory_space=pltpu.VMEM)
SMEM = pl.BlockSpec(memory_space=pltpu.SMEM)


def swapped(block, axis, apart):
    count = lax.axis_size(axis)
    return lax.ppermute(block, axis, [(i, i ^ (1 << apart)) for i in range(count)])


def bits_of(count):
    bits = count.bit_length() - 1
    return [*range(1, bits), 0] if bits else []


def angles_of(directions):
    return [2.0 * math.pi / directions * (d + 0.5) for d in range(directions)]


def halves(row_low, low, high):
    return jnp.where(row_low, low, high)


def advect_kernel(directions, courant, weight, breaking, own, below, above, land, damped, source):
    freqs = courant.shape[0]
    pairs = directions // 2
    half = pairs // 2
    theta = angles_of(directions)
    row_low = lax.broadcasted_iota(jnp.int32, (8, 128), 0) < 4
    source[...] = jnp.zeros_like(source)
    mask = land[...]

    def evolve(tile, d, speed):
        b = speed * abs(math.cos(theta[d]))
        c = speed * abs(math.sin(theta[d]))
        a = 1.0 - b - c
        dx = 1 if math.cos(theta[d]) > 0 else 127
        dy = 1 if math.sin(theta[d]) > 0 else 7
        for _ in range(STEPS):
            tile = a * tile + b * pltpu.roll(tile, dx, 1) + c * pltpu.roll(tile, dy, 0)
        return tile

    def body(f, carry):
        speed = courant[f]
        damp = breaking[f]
        gain = weight[f]
        for j in range(pairs):
            up = j < half
            inner = own[f * pairs + j].astype(jnp.float32)
            outer = (below if up else above)[f * half + j % half].astype(jnp.float32)
            inner4 = pltpu.roll(inner, 4, 0)
            outer4 = pltpu.roll(outer, 4, 0)
            if up:
                first = halves(row_low, outer, inner4)
                second = halves(row_low, outer4, inner)
            else:
                first = halves(row_low, inner, outer4)
                second = halves(row_low, inner4, outer)
            first = evolve(first, 2 * j, speed)
            second = evolve(second, 2 * j + 1, speed)
            if up:
                state = halves(row_low, pltpu.roll(first, 4, 0), second)
            else:
                state = halves(row_low, first, pltpu.roll(second, 4, 0))
            damped[f * pairs + j] = mask * state / (1.0 + damp * state)
            source[j] = source[j] + gain * state
        return carry

    lax.fori_loop(0, freqs, body, 0)


def basis_kernel(block_trig, wave_trig, coupling, chi, clo, shi, slo, pick):
    blocks = block_trig.shape[1]
    waves = wave_trig.shape[1]
    for q in range(blocks):
        rows = pl.ds(q * waves, waves)
        ca = block_trig[0, q : q + 1, :]
        sa = block_trig[1, q : q + 1, :]
        cb = wave_trig[0]
        sb = wave_trig[1]
        for value, high, low in ((ca * cb - sa * sb, chi, clo), (sa * cb + ca * sb, shi, slo)):
            top = value.astype(jnp.bfloat16)
            high[rows, :] = top
            low[rows, :] = (value - top.astype(jnp.float32)).astype(jnp.bfloat16)
    one_hot(coupling, pick)


def lanes_of(cells):
    return jnp.concatenate([cells[r : r + 1, :] for r in range(cells.shape[0])], axis=1)


def one_hot(coupling, pick):
    longitude = lanes_of(coupling[...]) % LON_W
    columns = lax.broadcasted_iota(jnp.int32, pick.shape, 0)
    pick[...] = (columns == longitude).astype(jnp.float32).astype(jnp.bfloat16)


def fourier_kernel(lats, share, band, level, legs, chi, clo, shi, slo, pick, coupling, grid, wind, hold):
    rows = FIELDS * lats
    turned = legs[...].T
    real = turned[:rows]
    imag = turned[rows:]
    dot = functools.partial(jnp.dot, preferred_element_type=jnp.float32)
    fields = (dot(real, chi[...]) + dot(imag, shi[...])) + (
        dot(real, clo[...]) + dot(imag, slo[...])
    )
    hold[...] = fields
    for f in range(FIELDS):
        grid[f] = hold[pl.ds(f * lats + band[0] * share, share), :]
    speed = fields[: 2 * lats] * level[0]
    top = speed.astype(jnp.bfloat16)
    low = (speed - top.astype(jnp.float32)).astype(jnp.bfloat16)
    found = dot(top, pick[...]) + dot(low, pick[...])
    latitude = lanes_of(coupling[...]) // LON_W
    here = lax.broadcasted_iota(jnp.int32, (lats, latitude.shape[1]), 0) == latitude
    for c in range(2):
        value = jnp.sum(
            jnp.where(here, found[c * lats : (c + 1) * lats], 0.0), axis=0, keepdims=True
        )
        for r in range(wind.shape[1]):
            wind[c, r : r + 1, :] = value[:, r * 128 : (r + 1) * 128]


def result_kernel(directions, parts, rate, damped, land, *refs):
    sources, winds, (result, charnock) = refs[:parts], refs[parts : 2 * parts], refs[2 * parts :]
    freqs = rate.shape[0]
    pairs = directions // 2
    theta = angles_of(directions)
    row_low = lax.broadcasted_iota(jnp.int32, (8, 128), 0) < 4

    def total(parts_of, index):
        value = parts_of[0][index]
        for part in parts_of[1:]:
            value = value + part[index]
        return value

    east4 = total(winds, 0)
    north4 = total(winds, 1)
    east = jnp.concatenate([east4, east4], axis=0)
    north = jnp.concatenate([north4, north4], axis=0)
    pushes = []
    stress = jnp.zeros((8, 128), jnp.float32)
    for j in range(pairs):
        cosines = halves(row_low, math.cos(theta[2 * j]), math.cos(theta[2 * j + 1]))
        sines = halves(row_low, math.sin(theta[2 * j]), math.sin(theta[2 * j + 1]))
        push = jnp.maximum(cosines * east + sines * north, 0.0)
        stress = stress + push * total(sources, j)
        pushes.append(push)
    for f in range(freqs):
        for j in range(pairs):
            value = damped[f * pairs + j]
            result[f * pairs + j] = value + value * (rate[f] * pushes[j])
    stress = (stress[0:4] + stress[4:8]) * (land[...] / (NF * directions))
    charnock[...] = 0.011 + 0.5 * stress / (
        stress + 0.05 * (1.0 + east4 * east4 + north4 * north4)
    )


def trig(waves):
    columns = jnp.arange(LON_W, dtype=jnp.int32)
    remains = waves[:, None] * columns[None, :] % NLON
    angles = 2.0 * math.pi / NLON * remains.astype(jnp.float32)
    return jnp.stack([jnp.cos(angles), -jnp.sin(angles)])


def split(value):
    top = value.astype(jnp.bfloat16)
    return top, (value - top.astype(jnp.float32)).astype(jnp.bfloat16)


def on_device(
    spectral, legendre, level_weights, coupling, land_sea, spectra, courant, growth_rate, breaking
):
    waves, lats, n_total = legendre.shape
    freqs, directions, tile_rows, tile_cols = spectra.shape
    bands = lax.axis_size("band")
    levs = lax.axis_size("lev")
    band = lax.axis_index("band")
    lev = lax.axis_index("lev")
    share = lats // bands
    pairs = directions // 2
    half = directions // 2

    below = lax.ppermute(spectra[:, :half], "band", [(i, i + 1) for i in range(bands - 1)])
    above = lax.ppermute(spectra[:, half:], "band", [(i + 1, i) for i in range(bands - 1)])

    stacked = spectral.reshape(waves, 2 * FIELDS, n_total)
    legs = lax.dot_general(
        stacked, legendre, (((2,), (2,)), ((0,), (0,))), preferred_element_type=jnp.float32
    ).astype(jnp.bfloat16)
    numbers = band * waves + jnp.arange(waves, dtype=jnp.int32)
    legs = legs.reshape(waves, 2 * FIELDS * lats)
    legs = legs * jnp.where(numbers == 0, 1.0, 2.0).astype(jnp.bfloat16)[:, None]

    order = [0]
    for bit in bits_of(bands):
        legs = jnp.concatenate([legs, swapped(legs, "band", bit)], axis=0)
        order = order + [q ^ (1 << bit) for q in order]
    blocks = band ^ jnp.asarray(order, dtype=jnp.int32)

    total = bands * waves
    points = tile_rows * tile_cols
    part = jax.ShapeDtypeStruct((total, LON_W), jnp.bfloat16)
    pick_shape = jax.ShapeDtypeStruct((LON_W, points), jnp.bfloat16)
    if waves % 16 == 0:
        chi, clo, shi, slo, pick = pl.pallas_call(
            basis_kernel,
            out_shape=[part] * 4 + [pick_shape],
            in_specs=[VMEM] * 3,
            out_specs=[VMEM] * 5,
            name="basis",
        )(trig(blocks * waves), trig(jnp.arange(waves, dtype=jnp.int32)), coupling)
    else:
        table = trig((blocks[:, None] * waves + jnp.arange(waves, dtype=jnp.int32)).reshape(-1))
        chi, clo = split(table[0])
        shi, slo = split(table[1])
        pick = pl.pallas_call(
            one_hot, out_shape=pick_shape, in_specs=[VMEM], out_specs=VMEM, name="pick"
        )(coupling)

    grid, wind = pl.pallas_call(
        functools.partial(fourier_kernel, lats, share),
        out_shape=[
            jax.ShapeDtypeStruct((FIELDS, share, LON_W), jnp.float32),
            jax.ShapeDtypeStruct((2, tile_rows, tile_cols), jnp.float32),
        ],
        in_specs=[SMEM, SMEM] + [VMEM] * 7,
        out_specs=[VMEM] * 2,
        scratch_shapes=[pltpu.VMEM((FIELDS * lats, LON_W), jnp.float32)],
        name="fourier",
    )(band.reshape(1), level_weights, legs, chi, clo, shi, slo, pick, coupling)
    grid = jnp.transpose(grid, (1, 0, 2)).reshape(share, 1, FIELDS, LON_W)

    numbers = lev * freqs + jnp.arange(freqs, dtype=jnp.int32)
    energy = 1.0 + 2.0 * numbers.astype(jnp.float32) / (NF - 1)
    land = land_sea.astype(jnp.float32)
    tiles = freqs * pairs
    damped, source = pl.pallas_call(
        functools.partial(advect_kernel, directions),
        out_shape=[
            jax.ShapeDtypeStruct((tiles, 8, 128), jnp.float32),
            jax.ShapeDtypeStruct((pairs, 8, 128), jnp.float32),
        ],
        in_specs=[SMEM] * 3 + [VMEM] * 4,
        out_specs=[VMEM] * 2,
        name="advect",
    )(
        courant,
        energy * growth_rate,
        breaking,
        spectra.reshape(tiles, 8, 128),
        below.reshape(tiles // 2, 8, 128),
        above.reshape(tiles // 2, 8, 128),
        jnp.concatenate([land, land], axis=0),
    )

    sources, winds = [source], [wind]
    bit = 0
    while 1 << bit < levs:
        sources = sources + [swapped(s, "lev", bit) for s in sources]
        winds = winds + [swapped(w, "lev", bit) for w in winds]
        bit += 1

    result, charnock = pl.pallas_call(
        functools.partial(result_kernel, directions, levs),
        out_shape=[
            jax.ShapeDtypeStruct((tiles, 8, 128), jnp.float32),
            jax.ShapeDtypeStruct((tile_rows, tile_cols), jnp.float32),
        ],
        in_specs=[SMEM] + [VMEM] * (2 + 2 * levs),
        out_specs=[VMEM] * 2,
        name="result",
    )(growth_rate, damped, land, *sources, *winds)
    return grid, result.reshape(freqs, directions, tile_rows, tile_cols), charnock


def solution(mesh):
    in_specs = (
        P("band", None, "lev", None, None),
        P("band", None, None),
        P("lev"),
        P("band", None),
        P("band", None),
        P("lev", None, "band", None),
        P("lev"),
        P("lev"),
        P("lev"),
    )
    out_specs = (P("band", "lev", None, None), P("lev", None, "band", None), P("band", None))
    return jax.shard_map(
        on_device, mesh=mesh, in_specs=in_specs, out_specs=out_specs, check_vma=False
    )
```

```python
import functools
import math

import jax
import jax.numpy as jnp
from jax import lax
from jax.experimental import pallas as pl
from jax.experimental.pallas import tpu as pltpu
from jax.sharding import PartitionSpec as P


NLON = 5136
LON_W = 512
NF = 36
STEPS = 4
FIELDS = 3

VMEM = pl.BlockSpec(memory_space=pltpu.VMEM)
SMEM = pl.BlockSpec(memory_space=pltpu.SMEM)


def swapped(block, axis, apart):
    count = lax.axis_size(axis)
    return lax.ppermute(block, axis, [(i, i ^ (1 << apart)) for i in range(count)])


def bits_of(count):
    bits = count.bit_length() - 1
    return [*range(1, bits), 0] if bits else []


def angles_of(directions):
    return [2.0 * math.pi / directions * (d + 0.5) for d in range(directions)]


def halves(row_low, low, high):
    return jnp.where(row_low, low, high)


def params(mib):
    return pltpu.CompilerParams(vmem_limit_bytes=mib * 2**20)


def pack_kernel(spectra, up, down, sems):
    half = up.shape[1]
    copies = [
        pltpu.make_async_copy(spectra.at[:, pl.ds(k * half, half)], out, sems.at[k])
        for k, out in enumerate((up, down))
    ]
    for copy in copies:
        copy.start()
    for copy in copies:
        copy.wait()


def by_sublane(table, group):
    rows = lax.broadcasted_iota(jnp.int32, (8, 128), 0)
    value = jnp.zeros((8, 128), jnp.float32)
    for s in range(8):
        if 8 * group + s < table.shape[0]:
            value = jnp.where(rows == s, table[8 * group + s], value)
    return value


def advect_kernel(
    directions, lev, angles, courant, rate, breaking, own, below, above, land,
    damped, source, own_f32, below_f32, above_f32, gains,
):
    freqs = courant.shape[0]
    groups = damped.shape[1]
    rows = damped.shape[2]
    half = directions // 2
    quarter = directions // 4

    for src, dst in ((own, own_f32), (below, below_f32), (above, above_f32)):
        def widen(i, carry, src=src, dst=dst):
            dst[pl.ds(8 * i, 8), :] = src[i].astype(jnp.float32)
            return carry

        lax.fori_loop(0, src.shape[0], widen, 0, unroll=9)

    speeds = [by_sublane(courant, g) for g in range(groups)]
    damps = [by_sublane(breaking, g) for g in range(groups)]
    sublane = lax.broadcasted_iota(jnp.int32, (8, 128), 0)
    weights = []
    for g in range(groups):
        number = (lev[0] * freqs + 8 * g + sublane).astype(jnp.float32)
        weights.append((1.0 + 2.0 * number / (NF - 1)) * by_sublane(rate, g))
    masks = [jnp.broadcast_to(land[r : r + 1, :].astype(jnp.float32), (8, 128)) for r in range(rows)]

    for quadrant in range(4):
        up = quadrant < 2
        shift = 1 if quadrant in (0, 3) else 127
        outer_f32 = below_f32 if up else above_f32

        def body(k, carry, quadrant=quadrant, up=up, shift=shift, outer_f32=outer_f32):
            d = quadrant * quarter + k
            east = angles[0, d]
            north = angles[1, d]
            total = [None] * rows
            for g in range(groups):
                b = speeds[g] * east
                c = speeds[g] * north
                a = 1.0 - b - c
                c2 = c * c
                terms = (4.0 * c, 6.0 * c2, 4.0 * c2 * c, c2 * c2)
                inner = [
                    own_f32[pl.ds(8 * g * rows * directions + d * rows + r, 8, rows * directions), :]
                    for r in range(rows)
                ]
                outer = [
                    outer_f32[pl.ds(8 * g * rows * half + (d % half) * rows + r, 8, rows * half), :]
                    for r in range(rows)
                ]
                column = outer + inner if up else (inner + outer)[::-1]
                for r in range(rows):
                    at = rows + r
                    state = column[at]
                    for j in range(STEPS):
                        state = a * state + b * pltpu.roll(state, shift, 1)
                        state = state + terms[j] * column[at - 1 - j]
                    row = r if up else rows - 1 - r
                    damped[d, g, row] = masks[row] * state / (1.0 + damps[g] * state)
                    part = weights[g] * state
                    if 8 * g + 8 > freqs:
                        part = jnp.where(sublane < freqs - 8 * g, part, 0.0)
                    total[row] = part if total[row] is None else total[row] + part
            for r in range(rows):
                gains[pl.ds(pl.multiple_of((d * rows + r) * 8, 8), 8), :] = total[r]
            return carry

        lax.fori_loop(0, quarter, body, 0)

    for i in range(source.shape[0]):
        value = gains[pl.ds(64 * i, 8, 8), :]
        for s in range(1, 8):
            value = value + gains[pl.ds(64 * i + s, 8, 8), :]
        source[i] = value


def basis_kernel(cosines, sines, coupling, cos_table, sin_table, pick, wave_cos, wave_sin):
    waves = wave_cos.shape[0]
    blocks = cos_table.shape[0] // waves
    tens = waves // 8
    for j in range(tens):
        ca, sa = cosines[blocks + j : blocks + j + 1, :], sines[blocks + j : blocks + j + 1, :]
        cb, sb = cosines[blocks + tens :, :], sines[blocks + tens :, :]
        wave_cos[8 * j : 8 * j + 8, :] = ca * cb - sa * sb
        wave_sin[8 * j : 8 * j + 8, :] = sa * cb + ca * sb

    def body(q, carry):
        ca, sa = cosines[pl.ds(q, 1), :], sines[pl.ds(q, 1), :]
        for j in range(0, waves, 16):
            cb, sb = wave_cos[j : j + 16, :], wave_sin[j : j + 16, :]
            rows = pl.ds(pl.multiple_of(q * waves + j, 16), 16)
            cos_table[rows, :] = (ca * cb - sa * sb).astype(jnp.bfloat16)
            sin_table[rows, :] = -(sa * cb + ca * sb).astype(jnp.bfloat16)
        return carry

    lax.fori_loop(0, blocks, body, 0)
    one_hot(coupling, pick)


def lanes_of(cells):
    return jnp.concatenate([cells[r : r + 1, :] for r in range(cells.shape[0])], axis=1)


def one_hot(coupling, pick):
    longitude = lanes_of(coupling[...]) % LON_W
    columns = lax.broadcasted_iota(jnp.int32, pick.shape, 0)
    pick[...] = (columns == longitude).astype(jnp.float32).astype(jnp.bfloat16)


def synthesis(parts, cos_table, sin_table, first, hold):
    at = 0
    for part in parts:
        count = part.shape[0]
        hold[at : at + count, :] = part[...]
        at += count
    turned = hold[...].T
    rows = turned.shape[0] // 2
    span = pl.ds(first, at)
    dot = functools.partial(jnp.dot, preferred_element_type=jnp.float32)
    return dot(turned[:rows], cos_table[span, :]) + dot(turned[rows:], sin_table[span, :])


def first_kernel(count, cos_table, sin_table, *refs):
    refs[count][...] = synthesis(refs[:count], cos_table, sin_table, 0, refs[count + 1])


def fourier_kernel(
    lats, share, band, level, early, last, cos_table, sin_table, pick, coupling, grid, wind, legs, hold
):
    first = cos_table.shape[0] - last.shape[0]
    fields = early[...] + synthesis([last], cos_table, sin_table, first, legs)
    hold[...] = fields
    for f in range(FIELDS):
        grid[f] = hold[pl.ds(f * lats + band[0] * share, share), :]
    speed = fields[: 2 * lats] * level[0]
    top = speed.astype(jnp.bfloat16)
    low = (speed - top.astype(jnp.float32)).astype(jnp.bfloat16)
    dot = functools.partial(jnp.dot, preferred_element_type=jnp.float32)
    found = dot(top, pick[...]) + dot(low, pick[...])
    latitude = lanes_of(coupling[...]) // LON_W
    here = lax.broadcasted_iota(jnp.int32, (lats, latitude.shape[1]), 0) == latitude
    for c in range(2):
        value = jnp.sum(
            jnp.where(here, found[c * lats : (c + 1) * lats], 0.0), axis=0, keepdims=True
        )
        for r in range(wind.shape[1]):
            wind[c, r : r + 1, :] = value[:, r * 128 : (r + 1) * 128]


def result_kernel(directions, parts, rate, damped, land, *refs):
    sources, winds = refs[:parts], refs[parts : 2 * parts]
    result, charnock, stage, sems = refs[2 * parts :]
    freqs = rate.shape[0]
    groups = damped.shape[1]
    rows = damped.shape[2]
    theta = angles_of(directions)
    span = rows * directions

    def total(parts_of, index):
        value = parts_of[0][index]
        for part in parts_of[1:]:
            value = value + part[index]
        return value

    east4 = total(winds, 0)
    north4 = total(winds, 1)
    east = [jnp.broadcast_to(east4[r : r + 1], (8, 128)) for r in range(rows)]
    north = [jnp.broadcast_to(north4[r : r + 1], (8, 128)) for r in range(rows)]
    copies = []
    for g in range(groups):
        rates = by_sublane(rate, g)
        for d in range(directions):
            for r in range(rows):
                push = jnp.maximum(
                    math.cos(theta[d]) * east[r] + math.sin(theta[d]) * north[r], 0.0
                )
                value = damped[d, g, r]
                stage[pl.ds(8 * g * span + d * rows + r, 8, span), :] = value + value * (rates * push)
        here = pl.ds(8 * g * span, min(8, freqs - 8 * g) * span)
        copies.append(pltpu.make_async_copy(stage.at[here], result.at[here], sems.at[g]))
        copies[-1].start()
    row_low = lax.broadcasted_iota(jnp.int32, (8, 128), 0) < 4
    east8 = jnp.concatenate([east4, east4], axis=0)
    north8 = jnp.concatenate([north4, north4], axis=0)
    stress = jnp.zeros((8, 128), jnp.float32)
    for j in range(directions // 2):
        cosines = halves(row_low, math.cos(theta[2 * j]), math.cos(theta[2 * j + 1]))
        sines = halves(row_low, math.sin(theta[2 * j]), math.sin(theta[2 * j + 1]))
        push = jnp.maximum(cosines * east8 + sines * north8, 0.0)
        stress = stress + push * total(sources, j)
    stress = (stress[0:4] + stress[4:8]) * (land[...].astype(jnp.float32) / (NF * directions))
    charnock[...] = 0.011 + 0.5 * stress / (
        stress + 0.05 * (1.0 + east4 * east4 + north4 * north4)
    )
    for copy in copies:
        copy.wait()


def trig(waves):
    columns = jnp.arange(LON_W, dtype=jnp.int32)
    remains = waves[:, None] * columns[None, :] % NLON
    angles = 2.0 * math.pi / NLON * remains.astype(jnp.float32)
    return jnp.cos(angles), jnp.sin(angles)


def on_device_(
    spectral, legendre, level_weights, coupling, land_sea, spectra, courant, growth_rate, breaking
):
    waves, lats, n_total = legendre.shape
    freqs, directions, tile_rows, tile_cols = spectra.shape
    bands = lax.axis_size("band")
    levs = lax.axis_size("lev")
    band = lax.axis_index("band")
    lev = lax.axis_index("lev")
    share = lats // bands
    pairs = directions // 2
    half = directions // 2

    half_shape = jax.ShapeDtypeStruct((freqs, half, tile_rows, tile_cols), jnp.bfloat16)
    up, down = pl.pallas_call(
        pack_kernel,
        out_shape=[half_shape] * 2,
        in_specs=[pl.BlockSpec(memory_space=pl.ANY)],
        out_specs=[pl.BlockSpec(memory_space=pl.ANY)] * 2,
        scratch_shapes=[pltpu.SemaphoreType.DMA((2,))],
        compiler_params=params(4),
        name="pack",
    )(spectra)
    below = lax.ppermute(up, "band", [(i, i + 1) for i in range(bands - 1)])
    above = lax.ppermute(down, "band", [(i + 1, i) for i in range(bands - 1)])

    spectral, up, down = lax.optimization_barrier((spectral, up, down))
    stacked = spectral.reshape(waves, 2 * FIELDS, n_total)
    legs = lax.dot_general(
        stacked, legendre, (((2,), (2,)), ((0,), (0,))), preferred_element_type=jnp.float32
    ).astype(jnp.bfloat16)
    numbers = band * waves + jnp.arange(waves, dtype=jnp.int32)
    legs = legs.reshape(waves, 2 * FIELDS * lats)
    legs = legs * jnp.where(numbers == 0, 1.0, 2.0).astype(jnp.bfloat16)[:, None]

    order = [0]
    parts = [legs]
    for bit in bits_of(bands):
        together = jnp.concatenate(parts, axis=0) if len(parts) > 1 else legs
        parts = parts + [swapped(together, "band", bit)]
        order = order + [q ^ (1 << bit) for q in order]
    blocks = band ^ jnp.asarray(order, dtype=jnp.int32)

    total = bands * waves
    points = tile_rows * tile_cols
    table = jax.ShapeDtypeStruct((total, LON_W), jnp.bfloat16)
    pick_shape = jax.ShapeDtypeStruct((LON_W, points), jnp.bfloat16)
    if waves % 16 == 0:
        tens = waves // 8
        listed = [blocks * waves, 8 * jnp.arange(tens, dtype=jnp.int32)]
        cos_rows, sin_rows = trig(jnp.concatenate(listed + [jnp.arange(8, dtype=jnp.int32)]))
        cos_table, sin_table, pick = pl.pallas_call(
            basis_kernel,
            out_shape=[table] * 2 + [pick_shape],
            in_specs=[VMEM] * 3,
            out_specs=[VMEM] * 3,
            scratch_shapes=[pltpu.VMEM((waves, LON_W), jnp.float32)] * 2,
            compiler_params=params(8),
            name="basis",
        )(cos_rows, sin_rows, coupling)
    else:
        cos_table, sin_table = trig(
            (blocks[:, None] * waves + jnp.arange(waves, dtype=jnp.int32)).reshape(-1)
        )
        cos_table, sin_table = cos_table.astype(jnp.bfloat16), -sin_table.astype(jnp.bfloat16)
        pick = pl.pallas_call(
            one_hot, out_shape=pick_shape, in_specs=[VMEM], out_specs=VMEM, name="pick"
        )(coupling)

    columns = 2 * FIELDS * lats
    size = 8 if lats <= 32 else 32
    fields_shape = jax.ShapeDtypeStruct((FIELDS * lats, LON_W), jnp.float32)
    early = pl.pallas_call(
        functools.partial(first_kernel, len(parts) - 1),
        out_shape=fields_shape,
        in_specs=[VMEM] * (len(parts) + 1),
        out_specs=VMEM,
        scratch_shapes=[pltpu.VMEM((total - parts[-1].shape[0], columns), jnp.bfloat16)],
        compiler_params=params(size),
        name="first",
    )(cos_table, sin_table, *parts[:-1])
    grid, wind = pl.pallas_call(
        functools.partial(fourier_kernel, lats, share),
        out_shape=[
            jax.ShapeDtypeStruct((FIELDS, share, LON_W), jnp.float32),
            jax.ShapeDtypeStruct((2, tile_rows, tile_cols), jnp.float32),
        ],
        in_specs=[SMEM, SMEM] + [VMEM] * 6,
        out_specs=[VMEM] * 2,
        scratch_shapes=[
            pltpu.VMEM((parts[-1].shape[0], columns), jnp.bfloat16),
            pltpu.VMEM((FIELDS * lats, LON_W), jnp.float32),
        ],
        compiler_params=params(size),
        name="fourier",
    )(band.reshape(1), level_weights, early, parts[-1], cos_table, sin_table, pick, coupling)
    grid = jnp.transpose(grid, (1, 0, 2)).reshape(share, 1, FIELDS, LON_W)

    tiles = freqs * pairs
    groups = -(-freqs // 8)
    theta = angles_of(directions)
    angles = jnp.asarray(
        [[abs(math.cos(t)) for t in theta], [abs(math.sin(t)) for t in theta]], jnp.float32
    )
    stage = 8 * groups * tile_rows
    damped, source = pl.pallas_call(
        functools.partial(advect_kernel, directions),
        out_shape=[
            jax.ShapeDtypeStruct((directions, groups, tile_rows, 8, 128), jnp.float32),
            jax.ShapeDtypeStruct((pairs, 8, 128), jnp.float32),
        ],
        in_specs=[SMEM] * 5 + [VMEM] * 4,
        out_specs=[VMEM] * 2,
        scratch_shapes=[
            pltpu.VMEM((stage * directions, 128), jnp.float32),
            pltpu.VMEM((stage * half, 128), jnp.float32),
            pltpu.VMEM((stage * half, 128), jnp.float32),
            pltpu.VMEM((8 * directions * tile_rows, 128), jnp.float32),
        ],
        compiler_params=params(12),
        name="advect",
    )(
        lev.reshape(1),
        angles,
        courant,
        growth_rate,
        breaking,
        spectra.reshape(tiles, 8, 128),
        below.reshape(tiles // 2, 8, 128),
        above.reshape(tiles // 2, 8, 128),
        land_sea,
    )

    sources, winds = [source], [wind]
    bit = 0
    while 1 << bit < levs:
        sources = sources + [swapped(s, "lev", bit) for s in sources]
        winds = winds + [swapped(w, "lev", bit) for w in winds]
        bit += 1

    result, charnock = pl.pallas_call(
        functools.partial(result_kernel, directions, levs),
        out_shape=[
            jax.ShapeDtypeStruct((tiles * 8, 128), jnp.float32),
            jax.ShapeDtypeStruct((tile_rows, tile_cols), jnp.float32),
        ],
        in_specs=[SMEM] + [VMEM] * (2 + 2 * levs),
        out_specs=[pl.BlockSpec(memory_space=pl.ANY), VMEM],
        scratch_shapes=[
            pltpu.VMEM((stage * directions, 128), jnp.float32),
            pltpu.SemaphoreType.DMA((groups,)),
        ],
        compiler_params=params(8),
        name="result",
    )(growth_rate, damped, land_sea, *sources, *winds)
    return grid, result.reshape(freqs, directions, tile_rows, tile_cols), charnock


def solution(mesh):
    in_specs = (
        P("band", None, "lev", None, None),
        P("band", None, None),
        P("lev"),
        P("band", None),
        P("band", None),
        P("lev", None, "band", None),
        P("lev"),
        P("lev"),
        P("lev"),
    )
    out_specs = (P("band", "lev", None, None), P("lev", None, "band", None), P("band", None))
    return jax.shard_map(
        on_device_, mesh=mesh, in_specs=in_specs, out_specs=out_specs, check_vma=False
    )
```

```python
import functools
import math

import jax
import jax.numpy as jnp
from jax import lax
from jax.experimental import pallas as pl
from jax.experimental.pallas import tpu as pltpu
from jax.sharding import PartitionSpec as P


NLON = 5136
LON_W = 512
NF = 36
STEPS = 4
FIELDS = 3

VMEM = pl.BlockSpec(memory_space=pltpu.VMEM)
SMEM = pl.BlockSpec(memory_space=pltpu.SMEM)


def swapped(block, axis, apart):
    count = lax.axis_size(axis)
    return lax.ppermute(block, axis, [(i, i ^ (1 << apart)) for i in range(count)])


def bits_of(count):
    bits = count.bit_length() - 1
    return [*range(1, bits), 0] if bits else []


def angles_of(directions):
    return [2.0 * math.pi / directions * (d + 0.5) for d in range(directions)]


def halves(row_low, low, high):
    return jnp.where(row_low, low, high)


def params(mib):
    return pltpu.CompilerParams(vmem_limit_bytes=mib * 2**20)


def pack_kernel(band, spectra, low, high, buffer, sems):
    freqs, half = low.shape[:2]
    odd = band[0] % 2
    chunks = buffer.shape[1]
    span = freqs // chunks
    reads, writes = [], []
    for k, out in enumerate((low, high)):
        first = (odd if k == 0 else 1 - odd) * half
        for c in range(chunks):
            rows = pl.ds(c * span, span)
            held = buffer.at[k, c]
            reads.append(
                pltpu.make_async_copy(spectra.at[rows, pl.ds(first, half)], held, sems.at[0, k, c])
            )
            writes.append(pltpu.make_async_copy(held, out.at[rows], sems.at[1, k, c]))
    for copy in reads:
        copy.start()
    for read, write in zip(reads, writes):
        read.wait()
        write.start()
    for copy in writes:
        copy.wait()


def advect_kernel(
    directions, lev, band, courant, rate, breaking, spectra, low, high, land,
    damped, source, own, held, sems,
):
    freqs = courant.shape[0]
    pairs = directions // 2
    half = pairs // 2
    theta = angles_of(directions)
    odd = band[0] % 2
    chunks = sems.shape[1]
    span = freqs // chunks
    copies = []
    for k in range(chunks):
        whole, part = pl.ds(k * span * pairs, span * pairs), pl.ds(k * span * half, span * half)
        copies.append(
            [
                pltpu.make_async_copy(spectra.at[whole], own.at[whole], sems.at[0, k]),
                pltpu.make_async_copy(low.at[part], held.at[1 - odd, part], sems.at[1, k]),
                pltpu.make_async_copy(high.at[part], held.at[odd, part], sems.at[2, k]),
            ]
        )
        for copy in copies[-1]:
            copy.start()
    source[...] = jnp.zeros_like(source)
    row = lax.broadcasted_iota(jnp.int32, (8, 128), 0)
    row_low = row < 4
    inner_row = row % 4
    land4 = land[...].astype(jnp.float32)
    mask = jnp.concatenate([land4, land4], axis=0)

    def body(f, carry):
        speed = courant[f]
        damp = breaking[f]
        gain = (1.0 + 2.0 * (lev[0] * freqs + f).astype(jnp.float32) / (NF - 1)) * rate[f]
        for j in range(pairs):
            up = j < half
            inner = own[f * pairs + j].astype(jnp.float32)
            outer = held[0 if up else 1, f * half + j % half].astype(jnp.float32)
            cosines = [math.cos(theta[2 * j + k]) for k in range(2)]
            sines = [abs(math.sin(theta[2 * j + k])) for k in range(2)]
            b = speed * halves(row_low, abs(cosines[0]), abs(cosines[1]))
            c = speed * halves(row_low, sines[0], sines[1])
            a = 1.0 - b - c
            c2 = c * c
            weights = (4.0 * c, 6.0 * c2, 4.0 * c2 * c, c2 * c2)

            def west(tile):
                east_side = pltpu.roll(tile, 1, 1) if max(cosines) > 0 else None
                west_side = pltpu.roll(tile, 127, 1) if min(cosines) < 0 else None
                if east_side is None or west_side is None:
                    return west_side if east_side is None else east_side
                return (
                    halves(row_low, east_side, west_side)
                    if cosines[0] > 0
                    else halves(row_low, west_side, east_side)
                )

            state = inner
            for k in range(1, STEPS + 1):
                if k == 4:
                    shifted = outer
                elif up:
                    shifted = jnp.where(
                        inner_row >= k, pltpu.roll(inner, k, 0), pltpu.roll(outer, k + 4, 0)
                    )
                else:
                    shifted = jnp.where(
                        inner_row < 4 - k, pltpu.roll(inner, 8 - k, 0), pltpu.roll(outer, 4 - k, 0)
                    )
                state = a * state + b * west(state) + weights[k - 1] * shifted
            damped[f * pairs + j] = mask * state / (1.0 + damp * state)
            source[j] = source[j] + gain * state
        return carry

    for k in range(chunks):
        for copy in copies[k]:
            copy.wait()
        lax.fori_loop(k * span, (k + 1) * span, body, 0)


def build_basis(cosines, sines, cos_table, sin_table, wave_cos, wave_sin):
    waves = wave_cos.shape[0]
    blocks = cos_table.shape[0] // waves
    tens = waves // 8
    for j in range(tens):
        ca, sa = cosines[blocks + j : blocks + j + 1, :], sines[blocks + j : blocks + j + 1, :]
        cb, sb = cosines[blocks + tens :, :], sines[blocks + tens :, :]
        wave_cos[8 * j : 8 * j + 8, :] = ca * cb - sa * sb
        wave_sin[8 * j : 8 * j + 8, :] = sa * cb + ca * sb

    def body(q, carry):
        ca, sa = cosines[pl.ds(q, 1), :], sines[pl.ds(q, 1), :]
        for j in range(0, waves, 16):
            cb, sb = wave_cos[j : j + 16, :], wave_sin[j : j + 16, :]
            rows = pl.ds(pl.multiple_of(q * waves + j, 16), 16)
            cos_table[rows, :] = (ca * cb - sa * sb).astype(jnp.bfloat16)
            sin_table[rows, :] = -(sa * cb + ca * sb).astype(jnp.bfloat16)
        return carry

    lax.fori_loop(0, blocks, body, 0)


def lanes_of(cells):
    return jnp.concatenate([cells[r : r + 1, :] for r in range(cells.shape[0])], axis=1)


def one_hot(coupling, pick):
    longitude = lanes_of(coupling[...]) % LON_W
    columns = lax.broadcasted_iota(jnp.int32, pick.shape, 0)
    pick[...] = (columns == longitude).astype(jnp.float32).astype(jnp.bfloat16)


def turned(parts, hold):
    at = 0
    for part in parts:
        count = part.shape[0]
        hold[at : at + count, :] = part[...]
        at += count
    return hold[...].T


dot = functools.partial(jnp.dot, preferred_element_type=jnp.float32)


def real_sum(legs, cos_table, sin_table):
    rows = legs.shape[0] // 2
    return dot(legs[:rows], cos_table[...]) + dot(legs[rows:], sin_table[...])


def first_kernel(count, cosines, sines, coupling, *refs):
    parts = refs[:count]
    early, cos_table, sin_table, pick, legs, wave_cos, wave_sin = refs[count:]
    build_basis(cosines, sines, cos_table, sin_table, wave_cos, wave_sin)
    one_hot(coupling, pick)
    early[...] = real_sum(turned(parts, legs), cos_table, sin_table)


def sum_kernel(count, cos_table, sin_table, coupling, *refs):
    parts = refs[:count]
    early, pick, legs = refs[count:]
    one_hot(coupling, pick)
    early[...] = real_sum(turned(parts, legs), cos_table, sin_table)


def fourier_kernel(
    lats, share, band, level, early, last, phase_cos, phase_sin, cos_table, sin_table, pick, coupling,
    grid, wind, hold,
):
    legs = last[...].T
    rows = legs.shape[0] // 2
    by_cos = dot(legs, cos_table[...])
    by_sin = dot(legs, sin_table[...])
    real = by_cos[:rows] + by_sin[rows:]
    imag = by_cos[rows:] - by_sin[:rows]
    fields = early[...] + (phase_cos[...] * real - phase_sin[...] * imag)
    hold[...] = fields
    for f in range(FIELDS):
        grid[f] = hold[pl.ds(f * lats + band[0] * share, share), :]
    speed = fields[: 2 * lats] * level[0]
    top = speed.astype(jnp.bfloat16)
    low = (speed - top.astype(jnp.float32)).astype(jnp.bfloat16)
    found = dot(top, pick[...]) + dot(low, pick[...])
    latitude = lanes_of(coupling[...]) // LON_W
    here = lax.broadcasted_iota(jnp.int32, (lats, latitude.shape[1]), 0) == latitude
    for c in range(2):
        value = jnp.sum(
            jnp.where(here, found[c * lats : (c + 1) * lats], 0.0), axis=0, keepdims=True
        )
        for r in range(wind.shape[1]):
            wind[c, r : r + 1, :] = value[:, r * 128 : (r + 1) * 128]


def result_kernel(directions, parts, rate, damped, land, *refs):
    sources, winds = refs[:parts], refs[parts : 2 * parts]
    result, charnock, stage, sems = refs[2 * parts :]
    freqs = rate.shape[0]
    pairs = directions // 2
    chunks = sems.shape[0]
    span = freqs // chunks
    theta = angles_of(directions)
    row_low = lax.broadcasted_iota(jnp.int32, (8, 128), 0) < 4

    def total(parts_of, index):
        value = parts_of[0][index]
        for part in parts_of[1:]:
            value = value + part[index]
        return value

    east4 = total(winds, 0)
    north4 = total(winds, 1)
    east = jnp.concatenate([east4, east4], axis=0)
    north = jnp.concatenate([north4, north4], axis=0)
    pushes = []
    for j in range(pairs):
        cosines = halves(row_low, math.cos(theta[2 * j]), math.cos(theta[2 * j + 1]))
        sines = halves(row_low, math.sin(theta[2 * j]), math.sin(theta[2 * j + 1]))
        pushes.append(jnp.maximum(cosines * east + sines * north, 0.0))
    copies = []
    for chunk in range(chunks):
        for f in range(chunk * span, (chunk + 1) * span):
            for j in range(pairs):
                value = damped[f * pairs + j]
                stage[f * pairs + j] = value + value * (rate[f] * pushes[j])
        here = pl.ds(chunk * span * pairs, span * pairs)
        copies.append(pltpu.make_async_copy(stage.at[here], result.at[here], sems.at[chunk]))
        copies[-1].start()
    stress = jnp.zeros((8, 128), jnp.float32)
    for j in range(pairs):
        stress = stress + pushes[j] * total(sources, j)
    stress = (stress[0:4] + stress[4:8]) * (land[...].astype(jnp.float32) / (NF * directions))
    charnock[...] = 0.011 + 0.5 * stress / (
        stress + 0.05 * (1.0 + east4 * east4 + north4 * north4)
    )
    for copy in copies:
        copy.wait()


def trig(waves):
    columns = jnp.arange(LON_W, dtype=jnp.int32)
    remains = waves[:, None] * columns[None, :] % NLON
    angles = 2.0 * math.pi / NLON * remains.astype(jnp.float32)
    return jnp.cos(angles), jnp.sin(angles)


def on_device_(
    spectral, legendre, level_weights, coupling, land_sea, spectra, courant, growth_rate, breaking
):
    waves, lats, n_total = legendre.shape
    freqs, directions, tile_rows, tile_cols = spectra.shape
    bands = lax.axis_size("band")
    levs = lax.axis_size("lev")
    band = lax.axis_index("band")
    lev = lax.axis_index("lev")
    share = lats // bands
    pairs = directions // 2
    half = directions // 2

    hbm = pl.BlockSpec(memory_space=pltpu.MemorySpace.HBM)
    in_hbm = functools.partial(
        pltpu.with_memory_space_constraint, memory_space=pltpu.MemorySpace.HBM
    )
    half_shape = pltpu.MemorySpace.HBM((freqs, half, tile_rows, tile_cols), jnp.bfloat16)
    chunks = 3
    low, high = pl.pallas_call(
        pack_kernel,
        out_shape=[half_shape] * 2,
        in_specs=[SMEM, hbm],
        out_specs=[hbm] * 2,
        scratch_shapes=[
            pltpu.VMEM((2, chunks, freqs // chunks, half, tile_rows, tile_cols), jnp.bfloat16),
            pltpu.SemaphoreType.DMA((2, 2, chunks)),
        ],
        compiler_params=params(4),
        name="pack",
    )(band.reshape(1), in_hbm(spectra))
    low = lax.ppermute(low, "band", [(i, i ^ 1) for i in range(bands)])
    across = [(i, i + 1) for i in range(1, bands - 1, 2)]
    high = lax.ppermute(high, "band", across + [(j, i) for i, j in across])

    stacked = spectral.reshape(waves, 2 * FIELDS, n_total)
    legs = lax.dot_general(
        stacked, legendre, (((2,), (2,)), ((0,), (0,))), preferred_element_type=jnp.float32
    ).astype(jnp.bfloat16)
    numbers = band * waves + jnp.arange(waves, dtype=jnp.int32)
    legs = legs.reshape(waves, 2 * FIELDS * lats)
    legs = legs * jnp.where(numbers == 0, 1.0, 2.0).astype(jnp.bfloat16)[:, None]

    order = [0]
    parts = [legs]
    for bit in bits_of(bands):
        together = jnp.concatenate(parts, axis=0) if len(parts) > 1 else legs
        parts = parts + [swapped(together, "band", bit)]
        if bit:
            order = order + [q ^ (1 << bit) for q in order]
    blocks = band ^ jnp.asarray(order, dtype=jnp.int32)

    count = len(parts) - 1
    total = bands * waves // 2
    points = tile_rows * tile_cols
    columns = 2 * FIELDS * lats
    shift = waves * (1 - 2 * (band % 2))
    table = pltpu.VMEM((total, LON_W), jnp.bfloat16)
    pick_shape = jax.ShapeDtypeStruct((LON_W, points), jnp.bfloat16)
    fields_shape = jax.ShapeDtypeStruct((FIELDS * lats, LON_W), jnp.float32)
    legs_scratch = pltpu.VMEM((total, columns), jnp.bfloat16)
    size = 10 if lats <= 32 else 32
    if waves % 16 == 0:
        tens = waves // 8
        listed = [blocks * waves, 8 * jnp.arange(tens, dtype=jnp.int32)]
        cos_rows, sin_rows = trig(jnp.concatenate(listed + [jnp.arange(8, dtype=jnp.int32)]))
        early, cos_table, sin_table, pick = pl.pallas_call(
            functools.partial(first_kernel, count),
            out_shape=[fields_shape, table, table, pick_shape],
            in_specs=[VMEM] * (3 + count),
            out_specs=[VMEM] * 4,
            scratch_shapes=[legs_scratch] + [pltpu.VMEM((waves, LON_W), jnp.float32)] * 2,
            compiler_params=params(size),
            name="first",
        )(cos_rows, sin_rows, coupling, *parts[:-1])
    else:
        cos_table, sin_table = trig(
            (blocks[:, None] * waves + jnp.arange(waves, dtype=jnp.int32)).reshape(-1)
        )
        cos_table, sin_table = cos_table.astype(jnp.bfloat16), -sin_table.astype(jnp.bfloat16)
        early, pick = pl.pallas_call(
            functools.partial(sum_kernel, count),
            out_shape=[fields_shape, pick_shape],
            in_specs=[VMEM] * (3 + count),
            out_specs=[VMEM] * 2,
            scratch_shapes=[legs_scratch],
            compiler_params=params(size),
            name="first",
        )(cos_table, sin_table, coupling, *parts[:-1])
    phase_cos, phase_sin = trig(shift.reshape(1))
    grid, wind = pl.pallas_call(
        functools.partial(fourier_kernel, lats, share),
        out_shape=[
            jax.ShapeDtypeStruct((FIELDS, share, LON_W), jnp.float32),
            jax.ShapeDtypeStruct((2, tile_rows, tile_cols), jnp.float32),
        ],
        in_specs=[SMEM, SMEM] + [VMEM] * 8,
        out_specs=[VMEM] * 2,
        scratch_shapes=[pltpu.VMEM((FIELDS * lats, LON_W), jnp.float32)],
        compiler_params=params(size),
        name="fourier",
    )(
        band.reshape(1), level_weights, early, parts[-1], phase_cos, phase_sin, cos_table, sin_table,
        pick, coupling,
    )
    grid = jnp.transpose(grid, (1, 0, 2)).reshape(share, 1, FIELDS, LON_W)

    tiles = freqs * pairs
    damped, source = pl.pallas_call(
        functools.partial(advect_kernel, directions),
        out_shape=[
            pltpu.VMEM((tiles, 8, 128), jnp.float32),
            pltpu.VMEM((pairs, 8, 128), jnp.float32),
        ],
        in_specs=[SMEM] * 5 + [hbm] * 3 + [VMEM],
        out_specs=[VMEM] * 2,
        scratch_shapes=[
            pltpu.VMEM((tiles, 8, 128), jnp.bfloat16),
            pltpu.VMEM((2, tiles // 2, 8, 128), jnp.bfloat16),
            pltpu.SemaphoreType.DMA((3, chunks)),
        ],
        compiler_params=params(6),
        name="advect",
    )(
        lev.reshape(1),
        band.reshape(1),
        courant,
        growth_rate,
        breaking,
        in_hbm(spectra.reshape(tiles, 8, 128)),
        in_hbm(low.reshape(tiles // 2, 8, 128)),
        in_hbm(high.reshape(tiles // 2, 8, 128)),
        land_sea,
    )

    sources, winds = [source], [wind]
    bit = 0
    while 1 << bit < levs:
        sources = sources + [swapped(s, "lev", bit) for s in sources]
        winds = winds + [swapped(w, "lev", bit) for w in winds]
        bit += 1

    result, charnock = pl.pallas_call(
        functools.partial(result_kernel, directions, levs),
        out_shape=[
            jax.ShapeDtypeStruct((tiles, 8, 128), jnp.float32),
            jax.ShapeDtypeStruct((tile_rows, tile_cols), jnp.float32),
        ],
        in_specs=[SMEM] + [VMEM] * (2 + 2 * levs),
        out_specs=[hbm, VMEM],
        scratch_shapes=[
            pltpu.VMEM((tiles, 8, 128), jnp.float32),
            pltpu.SemaphoreType.DMA((chunks,)),
        ],
        compiler_params=params(6),
        name="result",
    )(growth_rate, damped, land_sea, *sources, *winds)
    return grid, result.reshape(freqs, directions, tile_rows, tile_cols), charnock


def solution(mesh):
    in_specs = (
        P("band", None, "lev", None, None),
        P("band", None, None),
        P("lev"),
        P("band", None),
        P("band", None),
        P("lev", None, "band", None),
        P("lev"),
        P("lev"),
        P("lev"),
    )
    out_specs = (P("band", "lev", None, None), P("lev", None, "band", None), P("band", None))
    return jax.shard_map(
        on_device_, mesh=mesh, in_specs=in_specs, out_specs=out_specs, check_vma=False
    )
```

```python
import functools
import math

import jax
import jax.numpy as jnp
from jax import lax
from jax.experimental import pallas as pl
from jax.experimental.pallas import tpu as pltpu
from jax.sharding import PartitionSpec as P


NLON = 5136
LON_W = 512
NF = 36
STEPS = 4
FIELDS = 3

VMEM = pl.BlockSpec(memory_space=pltpu.VMEM)
SMEM = pl.BlockSpec(memory_space=pltpu.SMEM)


def swapped(block, axis, apart):
    count = lax.axis_size(axis)
    return lax.ppermute(block, axis, [(i, i ^ (1 << apart)) for i in range(count)])


def bits_of(count):
    return list(range(count.bit_length() - 1))


def angles_of(directions):
    return [2.0 * math.pi / directions * (d + 0.5) for d in range(directions)]


def halves(row_low, low, high):
    return jnp.where(row_low, low, high)


def params(mib):
    return pltpu.CompilerParams(vmem_limit_bytes=mib * 2**20)


def pack_kernel(band, spectra, low, high, buffer, sems):
    freqs, half = low.shape[:2]
    odd = band[0] % 2
    chunks = buffer.shape[1]
    span = freqs // chunks
    reads, writes = [], []
    for k, out in enumerate((low, high)):
        first = (odd if k == 0 else 1 - odd) * half
        for c in range(chunks):
            rows = pl.ds(c * span, span)
            held = buffer.at[k, c]
            reads.append(
                pltpu.make_async_copy(spectra.at[rows, pl.ds(first, half)], held, sems.at[0, k, c])
            )
            writes.append(pltpu.make_async_copy(held, out.at[rows], sems.at[1, k, c]))
    for copy in reads:
        copy.start()
    for read, write in zip(reads, writes):
        read.wait()
        write.start()
    for copy in writes:
        copy.wait()


def advect_kernel(
    directions, lev, up, courant, rate, breaking, spectra, halo, land, *refs
):
    (damped, source, own, outside, sems) = refs[-5:]
    freqs = courant.shape[0]
    half = directions // 4
    theta = angles_of(directions)
    chunks = sems.shape[1]
    span = freqs // chunks
    copies = []
    for k in range(chunks):
        rows = pl.ds(k * span, span)
        inside = spectra.at[rows, pl.ds((1 - up[0]) * half, half)]
        copies.append(
            [
                pltpu.make_async_copy(inside, own.at[rows], sems.at[0, k]),
                pltpu.make_async_copy(halo.at[rows], outside.at[rows], sems.at[1, k]),
            ]
        )
        for copy in copies[-1]:
            copy.start()
    row = lax.broadcasted_iota(jnp.int32, (8, 128), 0)
    row_low = row < 4
    inner_row = row % 4
    land4 = land[...].astype(jnp.float32)
    mask = jnp.concatenate([land4, land4], axis=0)
    source[...] = jnp.zeros_like(source)

    def body(f, carry, rising):
        speed = courant[f]
        damp = breaking[f]
        gain = (1.0 + 2.0 * (lev[0] * freqs + f).astype(jnp.float32) / (NF - 1)) * rate[f]
        for j in range(half):
            inner = own[f, j].astype(jnp.float32)
            outer = outside[f, j].astype(jnp.float32)
            signs = [1 if rising else -1] * 2
            cosines = [signs[k] * math.cos(theta[2 * j + k]) for k in range(2)]
            sines = [abs(math.sin(theta[2 * j + k])) for k in range(2)]
            b = speed * halves(row_low, abs(cosines[0]), abs(cosines[1]))
            c = speed * halves(row_low, sines[0], sines[1])
            a = 1.0 - b - c
            c2 = c * c
            weights = (4.0 * c, 6.0 * c2, 4.0 * c2 * c, c2 * c2)

            def upwind(tile):
                from_west = pltpu.roll(tile, 1, 1) if max(cosines) > 0 else None
                from_east = pltpu.roll(tile, 127, 1) if min(cosines) < 0 else None
                if from_west is None or from_east is None:
                    return from_east if from_west is None else from_west
                return (
                    halves(row_low, from_west, from_east)
                    if cosines[0] > 0
                    else halves(row_low, from_east, from_west)
                )

            state = inner
            for k in range(1, STEPS + 1):
                if k == 4:
                    shifted = outer
                elif rising:
                    shifted = jnp.where(
                        inner_row >= k, pltpu.roll(inner, k, 0), pltpu.roll(outer, k + 4, 0)
                    )
                else:
                    shifted = jnp.where(
                        inner_row < 4 - k, pltpu.roll(inner, 8 - k, 0), pltpu.roll(outer, 4 - k, 0)
                    )
                state = a * state + b * upwind(state) + weights[k - 1] * shifted
            damped[f, j] = mask * state / (1.0 + damp * state)
            source[j] = source[j] + gain * state
        return carry

    for k in range(chunks):
        for copy in copies[k]:
            copy.wait()
        for rising in (True, False):

            @pl.when(up[0] == int(rising))
            def _(k=k, rising=rising):
                lax.fori_loop(
                    k * span, (k + 1) * span, functools.partial(body, rising=rising), 0
                )


def build_basis(cosines, sines, cos_table, sin_table, wave_cos, wave_sin):
    waves = wave_cos.shape[0]
    blocks = cos_table.shape[0] // waves
    tens = waves // 8
    for j in range(tens):
        ca, sa = cosines[blocks + j : blocks + j + 1, :], sines[blocks + j : blocks + j + 1, :]
        cb, sb = cosines[blocks + tens :, :], sines[blocks + tens :, :]
        wave_cos[8 * j : 8 * j + 8, :] = ca * cb - sa * sb
        wave_sin[8 * j : 8 * j + 8, :] = sa * cb + ca * sb

    def body(q, carry):
        ca, sa = cosines[pl.ds(q, 1), :], sines[pl.ds(q, 1), :]
        for j in range(0, waves, 16):
            cb, sb = wave_cos[j : j + 16, :], wave_sin[j : j + 16, :]
            rows = pl.ds(pl.multiple_of(q * waves + j, 16), 16)
            cos_table[rows, :] = (ca * cb - sa * sb).astype(jnp.bfloat16)
            sin_table[rows, :] = -(sa * cb + ca * sb).astype(jnp.bfloat16)
        return carry

    lax.fori_loop(0, blocks, body, 0)


def lanes_of(cells):
    return jnp.concatenate([cells[r : r + 1, :] for r in range(cells.shape[0])], axis=1)


def one_hot(coupling, pick):
    longitude = lanes_of(coupling[...]) % LON_W
    columns = lax.broadcasted_iota(jnp.int32, pick.shape, 0)
    pick[...] = (columns == longitude).astype(jnp.float32).astype(jnp.bfloat16)


def turned(parts, hold):
    at = 0
    for part in parts:
        count = part.shape[0]
        hold[at : at + count, :] = part[...]
        at += count
    return hold[...].T


dot = functools.partial(jnp.dot, preferred_element_type=jnp.float32)


def real_sum(legs, cos_table, sin_table):
    rows = legs.shape[0] // 2
    return dot(legs[:rows], cos_table[...]) + dot(legs[rows:], sin_table[...])


def first_kernel(count, cosines, sines, coupling, *refs):
    parts = refs[:count]
    early, cos_table, sin_table, pick, legs, wave_cos, wave_sin = refs[count:]
    build_basis(cosines, sines, cos_table, sin_table, wave_cos, wave_sin)
    one_hot(coupling, pick)
    early[...] = real_sum(turned(parts, legs), cos_table, sin_table)


def sum_kernel(count, cos_table, sin_table, coupling, *refs):
    parts = refs[:count]
    early, pick, legs = refs[count:]
    one_hot(coupling, pick)
    early[...] = real_sum(turned(parts, legs), cos_table, sin_table)


def fourier_kernel(
    lats, share, band, level, early, last, phase_cos, phase_sin, cos_table, sin_table, pick, coupling,
    grid, wind, hold,
):
    legs = last[...].T
    rows = legs.shape[0] // 2
    by_cos = dot(legs, cos_table[...])
    by_sin = dot(legs, sin_table[...])
    real = by_cos[:rows] + by_sin[rows:]
    imag = by_cos[rows:] - by_sin[:rows]
    fields = early[...] + (phase_cos[...] * real - phase_sin[...] * imag)
    hold[...] = fields
    for f in range(FIELDS):
        grid[f] = hold[pl.ds(f * lats + band[0] * share, share), :]
    speed = fields[: 2 * lats] * level[0]
    top = speed.astype(jnp.bfloat16)
    low = (speed - top.astype(jnp.float32)).astype(jnp.bfloat16)
    found = dot(top, pick[...]) + dot(low, pick[...])
    latitude = lanes_of(coupling[...]) // LON_W
    here = lax.broadcasted_iota(jnp.int32, (lats, latitude.shape[1]), 0) == latitude
    for c in range(2):
        value = jnp.sum(
            jnp.where(here, found[c * lats : (c + 1) * lats], 0.0), axis=0, keepdims=True
        )
        for r in range(wind.shape[1]):
            wind[c, r : r + 1, :] = value[:, r * 128 : (r + 1) * 128]


def total(parts, index):
    value = parts[0][index]
    for part in parts[1:]:
        value = value + part[index]
    return value


def pushes_of(directions, winds, sign):
    half = directions // 4
    theta = angles_of(directions)
    row_low = lax.broadcasted_iota(jnp.int32, (8, 128), 0) < 4
    east4 = total(winds, 0)
    north4 = total(winds, 1)
    east = sign * jnp.concatenate([east4, east4], axis=0)
    north = sign * jnp.concatenate([north4, north4], axis=0)
    pushes = []
    for j in range(half):
        cosines = halves(row_low, math.cos(theta[2 * j]), math.cos(theta[2 * j + 1]))
        sines = halves(row_low, math.sin(theta[2 * j]), math.sin(theta[2 * j + 1]))
        pushes.append(jnp.maximum(cosines * east + sines * north, 0.0))
    return pushes, east4, north4


def sign_of(up):
    return (2 * up - 1).astype(jnp.float32)


def result_kernel(directions, parts, up, rate, damped, *refs):
    winds = refs[:parts]
    result, stage, sems = refs[-3:]
    half = directions // 4
    chunks = sems.shape[0]
    span = rate.shape[0] // chunks
    pushes, _, _ = pushes_of(directions, winds, sign_of(up[0]))
    copies = []
    for chunk in range(chunks):
        for f in range(chunk * span, (chunk + 1) * span):
            for j in range(half):
                value = damped[f, j]
                stage[f, j] = value + value * (rate[f] * pushes[j])
        rows = pl.ds(chunk * span, span)
        there = result.at[rows, pl.ds((1 - up[0]) * half, half)]
        copies.append(pltpu.make_async_copy(stage.at[rows], there, sems.at[chunk]))
        copies[-1].start()
    for copy in copies:
        copy.wait()


def charnock_kernel(directions, parts, up, land, *refs):
    winds, first, second, charnock = (
        refs[:parts], refs[parts : 2 * parts], refs[2 * parts : 3 * parts], refs[3 * parts],
    )
    sign = sign_of(up[0])
    stress = jnp.zeros((8, 128), jnp.float32)
    for sources, way in ((first, sign), (second, -sign)):
        pushes, east, north = pushes_of(directions, winds, way)
        for j, push in enumerate(pushes):
            stress = stress + push * total(sources, j)
    stress = (stress[0:4] + stress[4:8]) * (land[...].astype(jnp.float32) / (NF * directions))
    charnock[...] = 0.011 + 0.5 * stress / (
        stress + 0.05 * (1.0 + east * east + north * north)
    )


def trig(waves):
    columns = jnp.arange(LON_W, dtype=jnp.int32)
    remains = waves[:, None] * columns[None, :] % NLON
    angles = 2.0 * math.pi / NLON * remains.astype(jnp.float32)
    return jnp.cos(angles), jnp.sin(angles)


def on_device_(
    spectral, legendre, level_weights, coupling, land_sea, spectra, courant, growth_rate, breaking
):
    waves, lats, n_total = legendre.shape
    freqs, directions, tile_rows, tile_cols = spectra.shape
    bands = lax.axis_size("band")
    levs = lax.axis_size("lev")
    band = lax.axis_index("band")
    lev = lax.axis_index("lev")
    share = lats // bands
    pairs = directions // 2
    half = directions // 2

    hbm = pl.BlockSpec(memory_space=pltpu.MemorySpace.HBM)
    in_hbm = functools.partial(
        pltpu.with_memory_space_constraint, memory_space=pltpu.MemorySpace.HBM
    )
    half_shape = pltpu.MemorySpace.HBM((freqs, half, tile_rows, tile_cols), jnp.bfloat16)
    chunks = 3
    low, high = pl.pallas_call(
        pack_kernel,
        out_shape=[half_shape] * 2,
        in_specs=[SMEM, hbm],
        out_specs=[hbm] * 2,
        scratch_shapes=[
            pltpu.VMEM((2, chunks, freqs // chunks, half, tile_rows, tile_cols), jnp.bfloat16),
            pltpu.SemaphoreType.DMA((2, 2, chunks)),
        ],
        compiler_params=params(4),
        name="pack",
    )(band.reshape(1), in_hbm(spectra))
    low = lax.ppermute(low, "band", [(i, i ^ 1) for i in range(bands)])
    across = [(i, i + 1) for i in range(1, bands - 1, 2)]
    high = lax.ppermute(high, "band", across + [(j, i) for i, j in across])

    stacked = spectral.reshape(waves, 2 * FIELDS, n_total)
    legs = lax.dot_general(
        stacked, legendre, (((2,), (2,)), ((0,), (0,))), preferred_element_type=jnp.float32
    ).astype(jnp.bfloat16)
    numbers = band * waves + jnp.arange(waves, dtype=jnp.int32)
    legs = legs.reshape(waves, 2 * FIELDS * lats)
    legs = legs * jnp.where(numbers == 0, 1.0, 2.0).astype(jnp.bfloat16)[:, None]

    order = [0]
    parts = [legs]
    for bit in bits_of(bands):
        together = jnp.concatenate(parts, axis=0) if len(parts) > 1 else legs
        parts = parts + [swapped(together, "band", bit)]
        if 2 << bit < bands:
            order = order + [q ^ (1 << bit) for q in order]
    blocks = band ^ jnp.asarray(order, dtype=jnp.int32)

    count = len(parts) - 1
    total = bands * waves // 2
    points = tile_rows * tile_cols
    columns = 2 * FIELDS * lats
    shift = total * (1 - 2 * (band // (bands // 2)))
    table = pltpu.VMEM((total, LON_W), jnp.bfloat16)
    pick_shape = jax.ShapeDtypeStruct((LON_W, points), jnp.bfloat16)
    fields_shape = jax.ShapeDtypeStruct((FIELDS * lats, LON_W), jnp.float32)
    legs_scratch = pltpu.VMEM((total, columns), jnp.bfloat16)
    size = 10 if lats <= 32 else 32
    if waves % 16 == 0:
        tens = waves // 8
        listed = [blocks * waves, 8 * jnp.arange(tens, dtype=jnp.int32)]
        cos_rows, sin_rows = trig(jnp.concatenate(listed + [jnp.arange(8, dtype=jnp.int32)]))
        early, cos_table, sin_table, pick = pl.pallas_call(
            functools.partial(first_kernel, count),
            out_shape=[fields_shape, table, table, pick_shape],
            in_specs=[VMEM] * (3 + count),
            out_specs=[VMEM] * 4,
            scratch_shapes=[legs_scratch] + [pltpu.VMEM((waves, LON_W), jnp.float32)] * 2,
            compiler_params=params(size),
            name="first",
        )(cos_rows, sin_rows, coupling, *parts[:-1])
    else:
        cos_table, sin_table = trig(
            (blocks[:, None] * waves + jnp.arange(waves, dtype=jnp.int32)).reshape(-1)
        )
        cos_table, sin_table = cos_table.astype(jnp.bfloat16), -sin_table.astype(jnp.bfloat16)
        early, pick = pl.pallas_call(
            functools.partial(sum_kernel, count),
            out_shape=[fields_shape, pick_shape],
            in_specs=[VMEM] * (3 + count),
            out_specs=[VMEM] * 2,
            scratch_shapes=[legs_scratch],
            compiler_params=params(size),
            name="first",
        )(cos_table, sin_table, coupling, *parts[:-1])
    phase_cos, phase_sin = trig(shift.reshape(1))
    grid, wind = pl.pallas_call(
        functools.partial(fourier_kernel, lats, share),
        out_shape=[
            jax.ShapeDtypeStruct((FIELDS, share, LON_W), jnp.float32),
            jax.ShapeDtypeStruct((2, tile_rows, tile_cols), jnp.float32),
        ],
        in_specs=[SMEM, SMEM] + [VMEM] * 8,
        out_specs=[VMEM] * 2,
        scratch_shapes=[pltpu.VMEM((FIELDS * lats, LON_W), jnp.float32)],
        compiler_params=params(size),
        name="fourier",
    )(
        band.reshape(1), level_weights, early, parts[-1], phase_cos, phase_sin, cos_table, sin_table,
        pick, coupling,
    )
    grid = jnp.transpose(grid, (1, 0, 2)).reshape(share, 1, FIELDS, LON_W)

    quarter = pairs // 2
    odd = band % 2
    levels = lev.reshape(1)
    own = in_hbm(spectra.reshape(freqs, pairs, 8, 128))
    half_state = pltpu.VMEM((freqs, quarter, 8, 128), jnp.float32)

    def advected(halo, up):
        return pl.pallas_call(
            functools.partial(advect_kernel, directions),
            out_shape=[half_state, pltpu.VMEM((quarter, 8, 128), jnp.float32)],
            in_specs=[SMEM] * 5 + [hbm] * 2 + [VMEM],
            out_specs=[VMEM] * 2,
            scratch_shapes=[
                pltpu.VMEM((freqs, quarter, 8, 128), jnp.bfloat16),
                pltpu.VMEM((freqs, quarter, 8, 128), jnp.bfloat16),
                pltpu.SemaphoreType.DMA((2, chunks)),
            ],
            compiler_params=params(4),
        )(
            levels, up, courant, growth_rate, breaking, own,
            in_hbm(halo.reshape(freqs, quarter, 8, 128)), land_sea,
        )

    def over_lev(value):
        parts = [value]
        bit = 0
        while 1 << bit < levs:
            parts = parts + [swapped(part, "lev", bit) for part in parts]
            bit += 1
        return parts

    def forced(damped, up, *earlier):
        return pl.pallas_call(
            functools.partial(result_kernel, directions, levs),
            out_shape=pltpu.MemorySpace.HBM((freqs, pairs, 8, 128), jnp.float32),
            in_specs=[SMEM] * 2 + [VMEM] * (1 + levs) + [hbm] * len(earlier),
            out_specs=hbm,
            scratch_shapes=[
                pltpu.VMEM((freqs, quarter, 8, 128), jnp.float32),
                pltpu.SemaphoreType.DMA((chunks,)),
            ],
            input_output_aliases={3 + levs: 0} if earlier else {},
            compiler_params=params(4),
        )(up, growth_rate, damped, *winds, *earlier)

    near_up, far_up = odd.reshape(1), (1 - odd).reshape(1)
    winds = over_lev(wind)
    damped, source = advected(low, near_up)
    near_sources = over_lev(source)
    result = forced(damped, near_up)
    damped, source = advected(high, far_up)
    far_sources = over_lev(source)
    result = forced(damped, far_up, result)
    charnock = pl.pallas_call(
        functools.partial(charnock_kernel, directions, levs),
        out_shape=jax.ShapeDtypeStruct((tile_rows, tile_cols), jnp.float32),
        in_specs=[SMEM] + [VMEM] * (1 + 3 * levs),
        out_specs=VMEM,
        compiler_params=params(2),
        name="charnock",
    )(near_up, land_sea, *winds, *near_sources, *far_sources)
    return grid, result.reshape(freqs, directions, tile_rows, tile_cols), charnock


def solution(mesh):
    in_specs = (
        P("band", None, "lev", None, None),
        P("band", None, None),
        P("lev"),
        P("band", None),
        P("band", None),
        P("lev", None, "band", None),
        P("lev"),
        P("lev"),
        P("lev"),
    )
    out_specs = (P("band", "lev", None, None), P("lev", None, "band", None), P("band", None))
    return jax.shard_map(
        on_device_, mesh=mesh, in_specs=in_specs, out_specs=out_specs, check_vma=False
    )
```

```python
import functools
import math

import jax
import jax.numpy as jnp
from jax import lax
from jax.experimental import pallas as pl
from jax.experimental.pallas import tpu as pltpu
from jax.sharding import PartitionSpec as P


NLON = 5136
LON_W = 512
NF = 36
STEPS = 4
FIELDS = 3

VMEM = pl.BlockSpec(memory_space=pltpu.VMEM)
SMEM = pl.BlockSpec(memory_space=pltpu.SMEM)


def swapped(block, axis, apart):
    count = lax.axis_size(axis)
    return lax.ppermute(block, axis, [(i, i ^ (1 << apart)) for i in range(count)])


def bits_of(count):
    bits = count.bit_length() - 1
    return [0, *range(bits - 1, 0, -1)][:bits]


def angles_of(directions):
    return [2.0 * math.pi / directions * (d + 0.5) for d in range(directions)]


dot = functools.partial(jnp.dot, preferred_element_type=jnp.float32)


def halves(row_low, low, high):
    return jnp.where(row_low, low, high)


def params(mib):
    return pltpu.CompilerParams(vmem_limit_bytes=mib * 2**20)


def pack_kernel(band, spectra, low, high, buffer, sems):
    freqs, half = low.shape[:2]
    odd = band[0] % 2
    chunks = buffer.shape[1]
    span = freqs // chunks
    reads, writes = [], []
    for k, out in enumerate((low, high)):
        first = (odd if k == 0 else 1 - odd) * half
        for c in range(chunks):
            rows = pl.ds(c * span, span)
            held = buffer.at[k, c]
            reads.append(
                pltpu.make_async_copy(spectra.at[rows, pl.ds(first, half)], held, sems.at[0, k, c])
            )
            writes.append(pltpu.make_async_copy(held, out.at[rows], sems.at[1, k, c]))
    for copy in reads:
        copy.start()
    for read, write in zip(reads, writes):
        read.wait()
        write.start()
    for copy in writes:
        copy.wait()


def advect_kernel(directions, lev, up, courant, rate, breaking, spectra, halo, land, *refs):
    whole = spectra.shape[1] > halo.shape[1]
    if whole:
        damped, source, other, own, terms, moved, kept, shifts, sems = refs
    else:
        damped, source, terms, moved, kept, shifts = refs
        own = spectra
    freqs = courant.shape[0]
    half = directions // 4
    tiles = -(-half // 2)
    theta = angles_of(directions)
    if whole:
        copies = []
        for k, (first, dst) in enumerate((((1 - up[0]) * half, own), (up[0] * half, other))):
            copies.append(pltpu.make_async_copy(spectra.at[:, pl.ds(first, half)], dst, sems.at[k]))
            copies[-1].start()

    sign = 2 * up[0] - 1
    row = lax.broadcasted_iota(jnp.int32, (128, 128), 0)
    column = lax.broadcasted_iota(jnp.int32, (128, 128), 1)
    for i in range(STEPS):
        for k in range(2):
            move = (1 - 2 * k) * sign * (i + 1)
            hit = (row - column + move + 256) % 128 == 0
            shifts[128 * i : 128 * i + 128, 128 * k : 128 * k + 128] = hit.astype(
                jnp.float32
            ).astype(jnp.bfloat16)

    row = lax.broadcasted_iota(jnp.int32, (8, 128), 0)
    row_low = row < 4
    inner_row = row % 4
    land4 = land[...].astype(jnp.float32)
    mask = jnp.concatenate([land4, land4], axis=0)
    source[...] = jnp.zeros_like(source)
    if whole:
        for copy in copies:
            copy.wait()

    def powers(f, carry, rising):
        speed = courant[f]
        inside = inner_row >= 1 if rising else inner_row <= 2
        step = 1 if rising else 7
        held = []
        for j in range(half):
            cosines = [abs(math.cos(theta[2 * j + k])) for k in range(2)]
            sines = [abs(math.sin(theta[2 * j + k])) for k in range(2)]

            def both(power):
                return halves(row_low, power(cosines[0], sines[0]), power(cosines[1], sines[1]))

            def swapped_both(power):
                return halves(row_low, power(cosines[1], sines[1]), power(cosines[0], sines[0]))

            c = speed * both(lambda x, y: y)
            a = 1.0 - speed * both(lambda x, y: x + y)
            c_outer = speed * swapped_both(lambda x, y: y)
            a_outer = 1.0 - speed * swapped_both(lambda x, y: x + y)
            inner = own[f, j].astype(jnp.float32)
            outer = pltpu.roll(halo[f, j].astype(jnp.float32), 4, 0)
            states = [inner]
            for k in range(STEPS):
                from_outer = pltpu.roll(outer, step, 0)
                inner = a * inner + c * jnp.where(inside, pltpu.roll(inner, step, 0), from_outer)
                states.append(inner)
                if k < STEPS - 1:
                    outer = a_outer * outer + c_outer * from_outer
            kept[f, j] = states[STEPS]
            factors = (
                4.0 * speed, 6.0 * speed * speed, 4.0 * speed * speed * speed,
                speed * speed * speed * speed,
            )
            held.append(
                [
                    (factors[i] * both(lambda x, y, i=i: x ** (i + 1))) * states[STEPS - 1 - i]
                    for i in range(STEPS)
                ]
            )
            if j % 2 or j == half - 1:
                first = held[-2] if j % 2 else held[-1]
                at = pl.ds(pl.multiple_of(f * (16 * tiles) + 16 * (j // 2), 16), 16)
                for i in range(STEPS):
                    tile = jnp.concatenate([first[i], held[-1][i]], axis=0)
                    terms[at, 128 * i : 128 * i + 128] = tile.astype(jnp.bfloat16)
        return carry

    for rising in (True, False):

        @pl.when(up[0] == int(rising))
        def _(rising=rising):
            lax.fori_loop(0, freqs, functools.partial(powers, rising=rising), 0)

    moved[...] = dot(terms[...], shifts[...])

    def finish(f, carry):
        damp = breaking[f]
        gain = (1.0 + 2.0 * (lev[0] * freqs + f).astype(jnp.float32) / (NF - 1)) * rate[f]
        for j in range(half):
            at = pl.ds(pl.multiple_of(f * (16 * tiles) + 8 * j, 8), 8)
            east = [math.cos(theta[2 * j + k]) > 0 for k in range(2)]
            if east[0] == east[1]:
                shifted = moved[at, 0:128] if east[0] else moved[at, 128:256]
            else:
                shifted = halves(row_low, moved[at, 0:128], moved[at, 128:256])
            state = kept[f, j] + shifted
            damped[f, j] = mask * state / (1.0 + damp * state)
            source[j] = source[j] + gain * state
        return carry

    lax.fori_loop(0, freqs, finish, 0)


def build_basis(cosines, sines, cos_table, sin_table, wave_cos, wave_sin):
    waves = wave_cos.shape[0]
    blocks = cos_table.shape[0] // waves
    tens = waves // 8
    for j in range(tens):
        ca, sa = cosines[blocks + j : blocks + j + 1, :], sines[blocks + j : blocks + j + 1, :]
        cb, sb = cosines[blocks + tens :, :], sines[blocks + tens :, :]
        wave_cos[8 * j : 8 * j + 8, :] = ca * cb - sa * sb
        wave_sin[8 * j : 8 * j + 8, :] = sa * cb + ca * sb

    def body(q, carry):
        ca, sa = cosines[pl.ds(q, 1), :], sines[pl.ds(q, 1), :]
        for j in range(0, waves, 16):
            cb, sb = wave_cos[j : j + 16, :], wave_sin[j : j + 16, :]
            rows = pl.ds(pl.multiple_of(q * waves + j, 16), 16)
            cos_table[rows, :] = (ca * cb - sa * sb).astype(jnp.bfloat16)
            sin_table[rows, :] = -(sa * cb + ca * sb).astype(jnp.bfloat16)
        return carry

    lax.fori_loop(0, blocks, body, 0)


def lanes_of(cells):
    return jnp.concatenate([cells[r : r + 1, :] for r in range(cells.shape[0])], axis=1)


def one_hot(coupling, pick):
    longitude = lanes_of(coupling[...]) % LON_W
    columns = lax.broadcasted_iota(jnp.int32, pick.shape, 0)
    pick[...] = (columns == longitude).astype(jnp.float32).astype(jnp.bfloat16)


def turned(parts, hold):
    at = 0
    for part in parts:
        count = part.shape[0]
        hold[at : at + count, :] = part[...]
        at += count
    return hold[...].T


def real_sum(legs, cos_table, sin_table):
    rows = legs.shape[0] // 2
    return dot(legs[:rows], cos_table[...]) + dot(legs[rows:], sin_table[...])


def first_kernel(count, cosines, sines, coupling, *refs):
    parts = refs[:count]
    early, cos_table, sin_table, pick, legs, wave_cos, wave_sin = refs[count:]
    build_basis(cosines, sines, cos_table, sin_table, wave_cos, wave_sin)
    one_hot(coupling, pick)
    early[...] = real_sum(turned(parts, legs), cos_table, sin_table)


def sum_kernel(count, cos_table, sin_table, coupling, *refs):
    parts = refs[:count]
    early, pick, legs = refs[count:]
    one_hot(coupling, pick)
    early[...] = real_sum(turned(parts, legs), cos_table, sin_table)


def fourier_kernel(
    lats, share, band, level, early, last, phase_cos, phase_sin, cos_table, sin_table, pick, coupling,
    grid, wind, hold,
):
    legs = last[...].T
    rows = legs.shape[0] // 2
    by_cos = dot(legs, cos_table[...])
    by_sin = dot(legs, sin_table[...])
    real = by_cos[:rows] + by_sin[rows:]
    imag = by_cos[rows:] - by_sin[:rows]
    fields = early[...] + (phase_cos[...] * real - phase_sin[...] * imag)
    hold[...] = fields
    for f in range(FIELDS):
        grid[f] = hold[pl.ds(f * lats + band[0] * share, share), :]
    speed = fields[: 2 * lats] * level[0]
    top = speed.astype(jnp.bfloat16)
    low = (speed - top.astype(jnp.float32)).astype(jnp.bfloat16)
    found = dot(top, pick[...]) + dot(low, pick[...])
    latitude = lanes_of(coupling[...]) // LON_W
    here = lax.broadcasted_iota(jnp.int32, (lats, latitude.shape[1]), 0) == latitude
    for c in range(2):
        value = jnp.sum(
            jnp.where(here, found[c * lats : (c + 1) * lats], 0.0), axis=0, keepdims=True
        )
        for r in range(wind.shape[1]):
            wind[c, r : r + 1, :] = value[:, r * 128 : (r + 1) * 128]


def total(parts, index):
    value = parts[0][index]
    for part in parts[1:]:
        value = value + part[index]
    return value


def pushes_of(directions, winds, sign):
    half = directions // 4
    theta = angles_of(directions)
    row_low = lax.broadcasted_iota(jnp.int32, (8, 128), 0) < 4
    east4 = total(winds, 0)
    north4 = total(winds, 1)
    east = sign * jnp.concatenate([east4, east4], axis=0)
    north = sign * jnp.concatenate([north4, north4], axis=0)
    pushes = []
    for j in range(half):
        cosines = halves(row_low, math.cos(theta[2 * j]), math.cos(theta[2 * j + 1]))
        sines = halves(row_low, math.sin(theta[2 * j]), math.sin(theta[2 * j + 1]))
        pushes.append(jnp.maximum(cosines * east + sines * north, 0.0))
    return pushes, east4, north4


def sign_of(up):
    return (2 * up - 1).astype(jnp.float32)


def result_kernel(directions, parts, up, rate, damped, *refs):
    winds = refs[:parts]
    result, stage, sems = refs[-3:]
    half = directions // 4
    chunks = sems.shape[0]
    span = rate.shape[0] // chunks
    pushes, _, _ = pushes_of(directions, winds, sign_of(up[0]))
    copies = []
    for chunk in range(chunks):
        for f in range(chunk * span, (chunk + 1) * span):
            for j in range(half):
                value = damped[f, j]
                stage[f, j] = value + value * (rate[f] * pushes[j])
        rows = pl.ds(chunk * span, span)
        there = result.at[rows, pl.ds((1 - up[0]) * half, half)]
        copies.append(pltpu.make_async_copy(stage.at[rows], there, sems.at[chunk]))
        copies[-1].start()
    for copy in copies:
        copy.wait()


def charnock_kernel(directions, parts, up, land, *refs):
    winds, first, second, charnock = (
        refs[:parts], refs[parts : 2 * parts], refs[2 * parts : 3 * parts], refs[3 * parts],
    )
    sign = sign_of(up[0])
    stress = jnp.zeros((8, 128), jnp.float32)
    for sources, way in ((first, sign), (second, -sign)):
        pushes, east, north = pushes_of(directions, winds, way)
        for j, push in enumerate(pushes):
            stress = stress + push * total(sources, j)
    stress = (stress[0:4] + stress[4:8]) * (land[...].astype(jnp.float32) / (NF * directions))
    charnock[...] = 0.011 + 0.5 * stress / (
        stress + 0.05 * (1.0 + east * east + north * north)
    )


def trig(waves):
    columns = jnp.arange(LON_W, dtype=jnp.int32)
    remains = waves[:, None] * columns[None, :] % NLON
    angles = 2.0 * math.pi / NLON * remains.astype(jnp.float32)
    return jnp.cos(angles), jnp.sin(angles)


def on_device_(
    spectral, legendre, level_weights, coupling, land_sea, spectra, courant, growth_rate, breaking
):
    waves, lats, n_total = legendre.shape
    freqs, directions, tile_rows, tile_cols = spectra.shape
    bands = lax.axis_size("band")
    levs = lax.axis_size("lev")
    band = lax.axis_index("band")
    lev = lax.axis_index("lev")
    share = lats // bands
    pairs = directions // 2
    half = directions // 2

    hbm = pl.BlockSpec(memory_space=pltpu.MemorySpace.HBM)
    in_hbm = functools.partial(
        pltpu.with_memory_space_constraint, memory_space=pltpu.MemorySpace.HBM
    )
    in_vmem = functools.partial(
        pltpu.with_memory_space_constraint, memory_space=pltpu.MemorySpace.VMEM
    )
    half_shape = pltpu.MemorySpace.HBM((freqs, half, tile_rows, tile_cols), jnp.bfloat16)
    chunks = 3
    low, high = pl.pallas_call(
        pack_kernel,
        out_shape=[half_shape] * 2,
        in_specs=[SMEM, hbm],
        out_specs=[hbm] * 2,
        scratch_shapes=[
            pltpu.VMEM((2, chunks, freqs // chunks, half, tile_rows, tile_cols), jnp.bfloat16),
            pltpu.SemaphoreType.DMA((2, 2, chunks)),
        ],
        compiler_params=params(4),
        name="pack",
    )(band.reshape(1), in_hbm(spectra))
    low = lax.ppermute(low, "band", [(i, i ^ 1) for i in range(bands)])
    across = [(i, i + 1) for i in range(1, bands - 1, 2)]
    high = lax.ppermute(high, "band", across + [(j, i) for i, j in across])

    stacked = spectral.reshape(waves, 2 * FIELDS, n_total)
    legs = lax.dot_general(
        stacked, legendre, (((2,), (2,)), ((0,), (0,))), preferred_element_type=jnp.float32
    ).astype(jnp.bfloat16)
    numbers = band * waves + jnp.arange(waves, dtype=jnp.int32)
    legs = legs.reshape(waves, 2 * FIELDS * lats)
    legs = legs * jnp.where(numbers == 0, 1.0, 2.0).astype(jnp.bfloat16)[:, None]

    order = [0]
    parts = [legs]
    for bit in bits_of(bands):
        together = jnp.concatenate(parts, axis=0) if len(parts) > 1 else legs
        parts = parts + [swapped(together, "band", bit)]
        if len(parts) <= bands.bit_length() - 1:
            order = order + [q ^ (1 << bit) for q in order]
    blocks = band ^ jnp.asarray(order, dtype=jnp.int32)

    count = len(parts) - 1
    total = bands * waves // 2
    points = tile_rows * tile_cols
    columns = 2 * FIELDS * lats
    last = bits_of(bands)[-1]
    shift = (waves << last) * (1 - 2 * (jnp.right_shift(band, last) % 2))
    table = pltpu.VMEM((total, LON_W), jnp.bfloat16)
    pick_shape = jax.ShapeDtypeStruct((LON_W, points), jnp.bfloat16)
    fields_shape = jax.ShapeDtypeStruct((FIELDS * lats, LON_W), jnp.float32)
    legs_scratch = pltpu.VMEM((total, columns), jnp.bfloat16)
    size = 10 if lats <= 32 else 32
    if waves % 16 == 0:
        tens = waves // 8
        listed = [blocks * waves, 8 * jnp.arange(tens, dtype=jnp.int32)]
        cos_rows, sin_rows = trig(jnp.concatenate(listed + [jnp.arange(8, dtype=jnp.int32)]))
        early, cos_table, sin_table, pick = pl.pallas_call(
            functools.partial(first_kernel, count),
            out_shape=[fields_shape, table, table, pick_shape],
            in_specs=[VMEM] * (3 + count),
            out_specs=[VMEM] * 4,
            scratch_shapes=[legs_scratch] + [pltpu.VMEM((waves, LON_W), jnp.float32)] * 2,
            compiler_params=params(size),
            name="first",
        )(cos_rows, sin_rows, coupling, *parts[:-1])
    else:
        cos_table, sin_table = trig(
            (blocks[:, None] * waves + jnp.arange(waves, dtype=jnp.int32)).reshape(-1)
        )
        cos_table, sin_table = cos_table.astype(jnp.bfloat16), -sin_table.astype(jnp.bfloat16)
        early, pick = pl.pallas_call(
            functools.partial(sum_kernel, count),
            out_shape=[fields_shape, pick_shape],
            in_specs=[VMEM] * (3 + count),
            out_specs=[VMEM] * 2,
            scratch_shapes=[legs_scratch],
            compiler_params=params(size),
            name="first",
        )(cos_table, sin_table, coupling, *parts[:-1])
    phase_cos, phase_sin = trig(shift.reshape(1))
    grid, wind = pl.pallas_call(
        functools.partial(fourier_kernel, lats, share),
        out_shape=[
            jax.ShapeDtypeStruct((FIELDS, share, LON_W), jnp.float32),
            jax.ShapeDtypeStruct((2, tile_rows, tile_cols), jnp.float32),
        ],
        in_specs=[SMEM, SMEM] + [VMEM] * 8,
        out_specs=[VMEM] * 2,
        scratch_shapes=[pltpu.VMEM((FIELDS * lats, LON_W), jnp.float32)],
        compiler_params=params(size),
        name="fourier",
    )(
        band.reshape(1), level_weights, early, parts[-1], phase_cos, phase_sin, cos_table, sin_table,
        pick, coupling,
    )
    grid = jnp.transpose(grid, (1, 0, 2)).reshape(share, 1, FIELDS, LON_W)

    quarter = pairs // 2
    odd = band % 2
    levels = lev.reshape(1)
    own = in_hbm(spectra.reshape(freqs, pairs, 8, 128))
    half_state = pltpu.VMEM((freqs, quarter, 8, 128), jnp.float32)

    def advected(spectra_of, halo, up):
        whole = spectra_of.shape[1] == pairs
        part = pltpu.VMEM((freqs, quarter, 8, 128), jnp.bfloat16)
        tall = 16 * -(-quarter // 2) * freqs
        return pl.pallas_call(
            functools.partial(advect_kernel, directions),
            out_shape=[half_state, pltpu.VMEM((quarter, 8, 128), jnp.float32)] + [part] * whole,
            in_specs=[SMEM] * 5 + [hbm if whole else VMEM, VMEM, VMEM],
            out_specs=[VMEM] * (2 + whole),
            scratch_shapes=[part] * whole
            + [
                pltpu.VMEM((tall, STEPS * 128), jnp.bfloat16),
                pltpu.VMEM((tall, 256), jnp.float32),
                pltpu.VMEM((freqs, quarter, 8, 128), jnp.float32),
                pltpu.VMEM((STEPS * 128, 256), jnp.bfloat16),
            ]
            + [pltpu.SemaphoreType.DMA((2,))] * whole,
            compiler_params=params(12),
        )(
            levels, up, courant, growth_rate, breaking, spectra_of,
            in_vmem(halo.reshape(freqs, quarter, 8, 128)), land_sea,
        )

    def over_lev(value):
        parts = [value]
        bit = 0
        while 1 << bit < levs:
            parts = parts + [swapped(part, "lev", bit) for part in parts]
            bit += 1
        return parts

    def forced(damped, up, *earlier):
        return pl.pallas_call(
            functools.partial(result_kernel, directions, levs),
            out_shape=pltpu.MemorySpace.HBM((freqs, pairs, 8, 128), jnp.float32),
            in_specs=[SMEM] * 2 + [VMEM] * (1 + levs) + [hbm] * len(earlier),
            out_specs=hbm,
            scratch_shapes=[
                pltpu.VMEM((freqs, quarter, 8, 128), jnp.float32),
                pltpu.SemaphoreType.DMA((chunks,)),
            ],
            input_output_aliases={3 + levs: 0} if earlier else {},
            compiler_params=params(4),
        )(up, growth_rate, damped, *winds, *earlier)

    near_up, far_up = odd.reshape(1), (1 - odd).reshape(1)
    winds = over_lev(wind)
    damped, source, own = advected(own, low, near_up)
    near_sources = over_lev(source)
    result = forced(damped, near_up)
    damped, source = advected(own, high, far_up)
    far_sources = over_lev(source)
    result = forced(damped, far_up, result)
    charnock = pl.pallas_call(
        functools.partial(charnock_kernel, directions, levs),
        out_shape=jax.ShapeDtypeStruct((tile_rows, tile_cols), jnp.float32),
        in_specs=[SMEM] + [VMEM] * (1 + 3 * levs),
        out_specs=VMEM,
        compiler_params=params(2),
        name="charnock",
    )(near_up, land_sea, *winds, *near_sources, *far_sources)
    return grid, result.reshape(freqs, directions, tile_rows, tile_cols), charnock


def solution(mesh):
    in_specs = (
        P("band", None, "lev", None, None),
        P("band", None, None),
        P("lev"),
        P("band", None),
        P("band", None),
        P("lev", None, "band", None),
        P("lev"),
        P("lev"),
        P("lev"),
    )
    out_specs = (P("band", "lev", None, None), P("lev", None, "band", None), P("band", None))
    return jax.shard_map(
        on_device_, mesh=mesh, in_specs=in_specs, out_specs=out_specs, check_vma=False
    )
```

```python
import functools
import math

import jax
import jax.numpy as jnp
from jax import lax
from jax.experimental import pallas as pl
from jax.experimental.pallas import tpu as pltpu
from jax.sharding import PartitionSpec as P


NLON = 5136
LON_W = 512
NF = 36
STEPS = 4
FIELDS = 3

VMEM = pl.BlockSpec(memory_space=pltpu.VMEM)
SMEM = pl.BlockSpec(memory_space=pltpu.SMEM)


def swapped(block, axis, apart):
    count = lax.axis_size(axis)
    return lax.ppermute(block, axis, [(i, i ^ (1 << apart)) for i in range(count)])


def bits_of(count):
    bits = count.bit_length() - 1
    return [0, *range(bits - 1, 0, -1)][:bits]


def angles_of(directions):
    return [2.0 * math.pi / directions * (d + 0.5) for d in range(directions)]


dot = functools.partial(jnp.dot, preferred_element_type=jnp.float32)


def halves(row_low, low, high):
    return jnp.where(row_low, low, high)


def params(mib):
    return pltpu.CompilerParams(vmem_limit_bytes=mib * 2**20)


def pack_kernel(band, spectra, low, high, buffer, sems):
    freqs, half = low.shape[:2]
    odd = band[0] % 2
    chunks = buffer.shape[1]
    span = freqs // chunks
    reads, writes = [], []
    for k, out in enumerate((low, high)):
        first = (odd if k == 0 else 1 - odd) * half
        for c in range(chunks):
            rows = pl.ds(c * span, span)
            held = buffer.at[k, c]
            reads.append(
                pltpu.make_async_copy(spectra.at[rows, pl.ds(first, half)], held, sems.at[0, k, c])
            )
            writes.append(pltpu.make_async_copy(held, out.at[rows], sems.at[1, k, c]))
    for copy in reads:
        copy.start()
    for read, write in zip(reads, writes):
        read.wait()
        write.start()
    for copy in writes:
        copy.wait()


def advect_kernel(directions, lev, up, courant, rate, breaking, spectra, halo, land, *refs):
    whole = spectra.shape[1] > halo.shape[1]
    if whole:
        damped, source, other, own, terms, moved, kept, shifts, sems = refs
    else:
        damped, source, terms, moved, kept, shifts = refs
        own = spectra
    freqs = courant.shape[0]
    half = directions // 4
    tiles = -(-half // 2)
    theta = angles_of(directions)
    if whole:
        copies = []
        for k, (first, dst) in enumerate((((1 - up[0]) * half, own), (up[0] * half, other))):
            copies.append(pltpu.make_async_copy(spectra.at[:, pl.ds(first, half)], dst, sems.at[k]))
            copies[-1].start()

    sign = 2 * up[0] - 1
    row = lax.broadcasted_iota(jnp.int32, (128, 128), 0)
    column = lax.broadcasted_iota(jnp.int32, (128, 128), 1)
    for i in range(STEPS):
        for k in range(2):
            move = (1 - 2 * k) * sign * (i + 1)
            hit = (row - column + move + 256) % 128 == 0
            shifts[128 * i : 128 * i + 128, 128 * k : 128 * k + 128] = hit.astype(
                jnp.float32
            ).astype(jnp.bfloat16)

    row = lax.broadcasted_iota(jnp.int32, (8, 128), 0)
    row_low = row < 4
    inner_row = row % 4
    land4 = land[...].astype(jnp.float32)
    mask = jnp.concatenate([land4, land4], axis=0)
    source[...] = jnp.zeros_like(source)
    if whole:
        for copy in copies:
            copy.wait()

    def powers(f, carry, rising):
        speed = courant[f]
        inside = inner_row >= 1 if rising else inner_row <= 2
        step = 1 if rising else 7
        held = []
        for j in range(half):
            cosines = [abs(math.cos(theta[2 * j + k])) for k in range(2)]
            sines = [abs(math.sin(theta[2 * j + k])) for k in range(2)]

            def both(power):
                return halves(row_low, power(cosines[0], sines[0]), power(cosines[1], sines[1]))

            def swapped_both(power):
                return halves(row_low, power(cosines[1], sines[1]), power(cosines[0], sines[0]))

            c = speed * both(lambda x, y: y)
            a = 1.0 - speed * both(lambda x, y: x + y)
            c_outer = speed * swapped_both(lambda x, y: y)
            a_outer = 1.0 - speed * swapped_both(lambda x, y: x + y)
            inner = own[f, j].astype(jnp.float32)
            outer = pltpu.roll(halo[f, j].astype(jnp.float32), 4, 0)
            states = [inner]
            for k in range(STEPS):
                from_outer = pltpu.roll(outer, step, 0)
                inner = a * inner + c * jnp.where(inside, pltpu.roll(inner, step, 0), from_outer)
                states.append(inner)
                if k < STEPS - 1:
                    outer = a_outer * outer + c_outer * from_outer
            kept[f, j] = states[STEPS]
            factors = (
                4.0 * speed, 6.0 * speed * speed, 4.0 * speed * speed * speed,
                speed * speed * speed * speed,
            )
            held.append(
                [
                    (factors[i] * both(lambda x, y, i=i: x ** (i + 1))) * states[STEPS - 1 - i]
                    for i in range(STEPS)
                ]
            )
            if j % 2 or j == half - 1:
                first = held[-2] if j % 2 else held[-1]
                at = pl.ds(pl.multiple_of(f * (16 * tiles) + 16 * (j // 2), 16), 16)
                for i in range(STEPS):
                    tile = jnp.concatenate([first[i], held[-1][i]], axis=0)
                    terms[at, 128 * i : 128 * i + 128] = tile.astype(jnp.bfloat16)
        return carry

    for rising in (True, False):

        @pl.when(up[0] == int(rising))
        def _(rising=rising):
            lax.fori_loop(0, freqs, functools.partial(powers, rising=rising), 0)

    moved[...] = dot(terms[...], shifts[...])

    def finish(f, carry):
        damp = breaking[f]
        gain = (1.0 + 2.0 * (lev[0] * freqs + f).astype(jnp.float32) / (NF - 1)) * rate[f]
        for j in range(half):
            at = pl.ds(pl.multiple_of(f * (16 * tiles) + 8 * j, 8), 8)
            east = [math.cos(theta[2 * j + k]) > 0 for k in range(2)]
            if east[0] == east[1]:
                shifted = moved[at, 0:128] if east[0] else moved[at, 128:256]
            else:
                shifted = halves(row_low, moved[at, 0:128], moved[at, 128:256])
            state = kept[f, j] + shifted
            damped[f, j] = mask * state / (1.0 + damp * state)
            source[j] = source[j] + gain * state
        return carry

    lax.fori_loop(0, freqs, finish, 0)


def build_basis(cosines, sines, cos_table, sin_table, wave_cos, wave_sin):
    waves = wave_cos.shape[0]
    blocks = cos_table.shape[0] // waves
    tens = waves // 8
    for j in range(tens):
        ca, sa = cosines[blocks + j : blocks + j + 1, :], sines[blocks + j : blocks + j + 1, :]
        cb, sb = cosines[blocks + tens :, :], sines[blocks + tens :, :]
        wave_cos[8 * j : 8 * j + 8, :] = ca * cb - sa * sb
        wave_sin[8 * j : 8 * j + 8, :] = sa * cb + ca * sb

    def body(q, carry):
        ca, sa = cosines[pl.ds(q, 1), :], sines[pl.ds(q, 1), :]
        for j in range(0, waves, 16):
            cb, sb = wave_cos[j : j + 16, :], wave_sin[j : j + 16, :]
            rows = pl.ds(pl.multiple_of(q * waves + j, 16), 16)
            cos_table[rows, :] = (ca * cb - sa * sb).astype(jnp.bfloat16)
            sin_table[rows, :] = -(sa * cb + ca * sb).astype(jnp.bfloat16)
        return carry

    lax.fori_loop(0, blocks, body, 0)


def lanes_of(cells):
    return jnp.concatenate([cells[r : r + 1, :] for r in range(cells.shape[0])], axis=1)


def one_hot(coupling, pick):
    longitude = lanes_of(coupling[...]) % LON_W
    columns = lax.broadcasted_iota(jnp.int32, pick.shape, 0)
    pick[...] = (columns == longitude).astype(jnp.float32).astype(jnp.bfloat16)


def turned(parts, hold):
    at = 0
    for part in parts:
        count = part.shape[0]
        hold[at : at + count, :] = part[...]
        at += count
    return hold[...].T


def real_sum(legs, cos_table, sin_table):
    rows = legs.shape[0] // 2
    return dot(legs[:rows], cos_table[...]) + dot(legs[rows:], sin_table[...])


def first_kernel(count, cosines, sines, coupling, *refs):
    parts = refs[:count]
    early, cos_table, sin_table, pick, legs, wave_cos, wave_sin = refs[count:]
    build_basis(cosines, sines, cos_table, sin_table, wave_cos, wave_sin)
    one_hot(coupling, pick)
    early[...] = real_sum(turned(parts, legs), cos_table, sin_table)


def sum_kernel(count, cos_table, sin_table, coupling, *refs):
    parts = refs[:count]
    early, pick, legs = refs[count:]
    one_hot(coupling, pick)
    early[...] = real_sum(turned(parts, legs), cos_table, sin_table)


def fourier_kernel(
    lats, share, band, level, early, last, phase_cos, phase_sin, cos_table, sin_table, pick, coupling,
    grid, wind, hold,
):
    legs = last[...].T
    rows = legs.shape[0] // 2
    by_cos = dot(legs, cos_table[...])
    by_sin = dot(legs, sin_table[...])
    real = by_cos[:rows] + by_sin[rows:]
    imag = by_cos[rows:] - by_sin[:rows]
    fields = early[...] + (phase_cos[...] * real - phase_sin[...] * imag)
    hold[...] = fields
    for f in range(FIELDS):
        grid[f] = hold[pl.ds(f * lats + band[0] * share, share), :]
    speed = fields[: 2 * lats] * level[0]
    top = speed.astype(jnp.bfloat16)
    low = (speed - top.astype(jnp.float32)).astype(jnp.bfloat16)
    found = dot(top, pick[...]) + dot(low, pick[...])
    latitude = lanes_of(coupling[...]) // LON_W
    here = lax.broadcasted_iota(jnp.int32, (lats, latitude.shape[1]), 0) == latitude
    for c in range(2):
        value = jnp.sum(
            jnp.where(here, found[c * lats : (c + 1) * lats], 0.0), axis=0, keepdims=True
        )
        for r in range(wind.shape[1]):
            wind[c, r : r + 1, :] = value[:, r * 128 : (r + 1) * 128]


def total(parts, index):
    value = parts[0][index]
    for part in parts[1:]:
        value = value + part[index]
    return value


def pushes_of(directions, winds, sign):
    half = directions // 4
    theta = angles_of(directions)
    row_low = lax.broadcasted_iota(jnp.int32, (8, 128), 0) < 4
    east4 = total(winds, 0)
    north4 = total(winds, 1)
    east = sign * jnp.concatenate([east4, east4], axis=0)
    north = sign * jnp.concatenate([north4, north4], axis=0)
    pushes = []
    for j in range(half):
        cosines = halves(row_low, math.cos(theta[2 * j]), math.cos(theta[2 * j + 1]))
        sines = halves(row_low, math.sin(theta[2 * j]), math.sin(theta[2 * j + 1]))
        pushes.append(jnp.maximum(cosines * east + sines * north, 0.0))
    return pushes, east4, north4


def sign_of(up):
    return (2 * up - 1).astype(jnp.float32)


def result_kernel(directions, parts, up, rate, near, far, *refs):
    winds = refs[:parts]
    result, stage, sems = refs[-3:]
    half = directions // 4
    chunks = sems.shape[0]
    span = rate.shape[0] // chunks
    sign = sign_of(up[0])
    sides = [
        (near, (1 - up[0]) * half, pushes_of(directions, winds, sign)[0]),
        (far, up[0] * half, pushes_of(directions, winds, -sign)[0]),
    ]
    copies = []
    for chunk in range(chunks):
        for f in range(chunk * span, (chunk + 1) * span):
            for damped, first, pushes in sides:
                for j in range(half):
                    value = damped[f, j]
                    stage[f, first + j] = value + value * (rate[f] * pushes[j])
        rows = pl.ds(chunk * span, span)
        copies.append(pltpu.make_async_copy(stage.at[rows], result.at[rows], sems.at[chunk]))
        copies[-1].start()
    for copy in copies:
        copy.wait()


def charnock_kernel(directions, parts, up, land, *refs):
    winds, first, second, charnock = (
        refs[:parts], refs[parts : 2 * parts], refs[2 * parts : 3 * parts], refs[3 * parts],
    )
    sign = sign_of(up[0])
    stress = jnp.zeros((8, 128), jnp.float32)
    for sources, way in ((first, sign), (second, -sign)):
        pushes, east, north = pushes_of(directions, winds, way)
        for j, push in enumerate(pushes):
            stress = stress + push * total(sources, j)
    stress = (stress[0:4] + stress[4:8]) * (land[...].astype(jnp.float32) / (NF * directions))
    charnock[...] = 0.011 + 0.5 * stress / (
        stress + 0.05 * (1.0 + east * east + north * north)
    )


def trig(waves):
    columns = jnp.arange(LON_W, dtype=jnp.int32)
    remains = waves[:, None] * columns[None, :] % NLON
    angles = 2.0 * math.pi / NLON * remains.astype(jnp.float32)
    return jnp.cos(angles), jnp.sin(angles)


def on_device_(
    spectral, legendre, level_weights, coupling, land_sea, spectra, courant, growth_rate, breaking
):
    waves, lats, n_total = legendre.shape
    freqs, directions, tile_rows, tile_cols = spectra.shape
    bands = lax.axis_size("band")
    levs = lax.axis_size("lev")
    band = lax.axis_index("band")
    lev = lax.axis_index("lev")
    share = lats // bands
    pairs = directions // 2
    half = directions // 2

    hbm = pl.BlockSpec(memory_space=pltpu.MemorySpace.HBM)
    in_hbm = functools.partial(
        pltpu.with_memory_space_constraint, memory_space=pltpu.MemorySpace.HBM
    )
    in_vmem = functools.partial(
        pltpu.with_memory_space_constraint, memory_space=pltpu.MemorySpace.VMEM
    )
    half_shape = pltpu.MemorySpace.HBM((freqs, half, tile_rows, tile_cols), jnp.bfloat16)
    chunks = 3
    low, high = pl.pallas_call(
        pack_kernel,
        out_shape=[half_shape] * 2,
        in_specs=[SMEM, hbm],
        out_specs=[hbm] * 2,
        scratch_shapes=[
            pltpu.VMEM((2, chunks, freqs // chunks, half, tile_rows, tile_cols), jnp.bfloat16),
            pltpu.SemaphoreType.DMA((2, 2, chunks)),
        ],
        compiler_params=params(4),
        name="pack",
    )(band.reshape(1), in_hbm(spectra))
    low = lax.ppermute(low, "band", [(i, i ^ 1) for i in range(bands)])
    across = [(i, i + 1) for i in range(1, bands - 1, 2)]
    high = lax.ppermute(high, "band", across + [(j, i) for i, j in across])

    stacked = spectral.reshape(waves, 2 * FIELDS, n_total)
    legs = lax.dot_general(
        stacked, legendre, (((2,), (2,)), ((0,), (0,))), preferred_element_type=jnp.float32
    ).astype(jnp.bfloat16)
    numbers = band * waves + jnp.arange(waves, dtype=jnp.int32)
    legs = legs.reshape(waves, 2 * FIELDS * lats)
    legs = legs * jnp.where(numbers == 0, 1.0, 2.0).astype(jnp.bfloat16)[:, None]

    order = [0]
    parts = [legs]
    for bit in bits_of(bands):
        together = jnp.concatenate(parts, axis=0) if len(parts) > 1 else legs
        parts = parts + [swapped(together, "band", bit)]
        if len(parts) <= bands.bit_length() - 1:
            order = order + [q ^ (1 << bit) for q in order]
    blocks = band ^ jnp.asarray(order, dtype=jnp.int32)

    count = len(parts) - 1
    total = bands * waves // 2
    points = tile_rows * tile_cols
    columns = 2 * FIELDS * lats
    last = bits_of(bands)[-1]
    shift = (waves << last) * (1 - 2 * (jnp.right_shift(band, last) % 2))
    table = pltpu.VMEM((total, LON_W), jnp.bfloat16)
    pick_shape = jax.ShapeDtypeStruct((LON_W, points), jnp.bfloat16)
    fields_shape = jax.ShapeDtypeStruct((FIELDS * lats, LON_W), jnp.float32)
    legs_scratch = pltpu.VMEM((total, columns), jnp.bfloat16)
    size = 10 if lats <= 32 else 32
    if waves % 16 == 0:
        tens = waves // 8
        listed = [blocks * waves, 8 * jnp.arange(tens, dtype=jnp.int32)]
        cos_rows, sin_rows = trig(jnp.concatenate(listed + [jnp.arange(8, dtype=jnp.int32)]))
        early, cos_table, sin_table, pick = pl.pallas_call(
            functools.partial(first_kernel, count),
            out_shape=[fields_shape, table, table, pick_shape],
            in_specs=[VMEM] * (3 + count),
            out_specs=[VMEM] * 4,
            scratch_shapes=[legs_scratch] + [pltpu.VMEM((waves, LON_W), jnp.float32)] * 2,
            compiler_params=params(size),
            name="first",
        )(cos_rows, sin_rows, coupling, *parts[:-1])
    else:
        cos_table, sin_table = trig(
            (blocks[:, None] * waves + jnp.arange(waves, dtype=jnp.int32)).reshape(-1)
        )
        cos_table, sin_table = cos_table.astype(jnp.bfloat16), -sin_table.astype(jnp.bfloat16)
        early, pick = pl.pallas_call(
            functools.partial(sum_kernel, count),
            out_shape=[fields_shape, pick_shape],
            in_specs=[VMEM] * (3 + count),
            out_specs=[VMEM] * 2,
            scratch_shapes=[legs_scratch],
            compiler_params=params(size),
            name="first",
        )(cos_table, sin_table, coupling, *parts[:-1])
    phase_cos, phase_sin = trig(shift.reshape(1))
    grid, wind = pl.pallas_call(
        functools.partial(fourier_kernel, lats, share),
        out_shape=[
            jax.ShapeDtypeStruct((FIELDS, share, LON_W), jnp.float32),
            jax.ShapeDtypeStruct((2, tile_rows, tile_cols), jnp.float32),
        ],
        in_specs=[SMEM, SMEM] + [VMEM] * 8,
        out_specs=[VMEM] * 2,
        scratch_shapes=[pltpu.VMEM((FIELDS * lats, LON_W), jnp.float32)],
        compiler_params=params(size),
        name="fourier",
    )(
        band.reshape(1), level_weights, early, parts[-1], phase_cos, phase_sin, cos_table, sin_table,
        pick, coupling,
    )
    grid = jnp.transpose(grid, (1, 0, 2)).reshape(share, 1, FIELDS, LON_W)

    quarter = pairs // 2
    odd = band % 2
    levels = lev.reshape(1)
    own = in_hbm(spectra.reshape(freqs, pairs, 8, 128))
    half_state = pltpu.VMEM((freqs, quarter, 8, 128), jnp.float32)

    def advected(spectra_of, halo, up):
        whole = spectra_of.shape[1] == pairs
        part = pltpu.VMEM((freqs, quarter, 8, 128), jnp.bfloat16)
        tall = 16 * -(-quarter // 2) * freqs
        return pl.pallas_call(
            functools.partial(advect_kernel, directions),
            out_shape=[half_state, pltpu.VMEM((quarter, 8, 128), jnp.float32)] + [part] * whole,
            in_specs=[SMEM] * 5 + [hbm if whole else VMEM, VMEM, VMEM],
            out_specs=[VMEM] * (2 + whole),
            scratch_shapes=[part] * whole
            + [
                pltpu.VMEM((tall, STEPS * 128), jnp.bfloat16),
                pltpu.VMEM((tall, 256), jnp.float32),
                pltpu.VMEM((freqs, quarter, 8, 128), jnp.float32),
                pltpu.VMEM((STEPS * 128, 256), jnp.bfloat16),
            ]
            + [pltpu.SemaphoreType.DMA((2,))] * whole,
            compiler_params=params(12),
        )(
            levels, up, courant, growth_rate, breaking, spectra_of,
            in_vmem(halo.reshape(freqs, quarter, 8, 128)), land_sea,
        )

    def over_lev(value):
        parts = [value]
        bit = 0
        while 1 << bit < levs:
            parts = parts + [swapped(part, "lev", bit) for part in parts]
            bit += 1
        return parts

    near_up, far_up = odd.reshape(1), (1 - odd).reshape(1)
    winds = over_lev(wind)
    near_damped, source, own = advected(own, low, near_up)
    near_sources = over_lev(source)
    far_damped, source = advected(own, high, far_up)
    far_sources = over_lev(source)
    result = pl.pallas_call(
        functools.partial(result_kernel, directions, levs),
        out_shape=pltpu.MemorySpace.HBM((freqs, pairs, 8, 128), jnp.float32),
        in_specs=[SMEM] * 2 + [VMEM] * (2 + levs),
        out_specs=hbm,
        scratch_shapes=[
            pltpu.VMEM((freqs, pairs, 8, 128), jnp.float32),
            pltpu.SemaphoreType.DMA((chunks,)),
        ],
        compiler_params=params(6),
        name="result",
    )(near_up, growth_rate, near_damped, far_damped, *winds)
    charnock = pl.pallas_call(
        functools.partial(charnock_kernel, directions, levs),
        out_shape=jax.ShapeDtypeStruct((tile_rows, tile_cols), jnp.float32),
        in_specs=[SMEM] + [VMEM] * (1 + 3 * levs),
        out_specs=VMEM,
        compiler_params=params(2),
        name="charnock",
    )(near_up, land_sea, *winds, *near_sources, *far_sources)
    return grid, result.reshape(freqs, directions, tile_rows, tile_cols), charnock


def solution(mesh):
    in_specs = (
        P("band", None, "lev", None, None),
        P("band", None, None),
        P("lev"),
        P("band", None),
        P("band", None),
        P("lev", None, "band", None),
        P("lev"),
        P("lev"),
        P("lev"),
    )
    out_specs = (P("band", "lev", None, None), P("lev", None, "band", None), P("band", None))
    return jax.shard_map(
        on_device_, mesh=mesh, in_specs=in_specs, out_specs=out_specs, check_vma=False
    )
```

```python
import functools
import math

import jax
import jax.numpy as jnp
from jax import lax
from jax.experimental import pallas as pl
from jax.experimental.pallas import tpu as pltpu
from jax.sharding import PartitionSpec as P


NLON = 5136
LON_W = 512
NF = 36
STEPS = 4
FIELDS = 3

VMEM = pl.BlockSpec(memory_space=pltpu.VMEM)
SMEM = pl.BlockSpec(memory_space=pltpu.SMEM)


def swapped(block, axis, apart):
    count = lax.axis_size(axis)
    return lax.ppermute(block, axis, [(i, i ^ (1 << apart)) for i in range(count)])


def bits_of(count):
    bits = count.bit_length() - 1
    return [0, *range(bits - 1, 0, -1)][:bits]


def angles_of(directions):
    return [2.0 * math.pi / directions * (d + 0.5) for d in range(directions)]


dot = functools.partial(jnp.dot, preferred_element_type=jnp.float32)


def halves(row_low, low, high):
    return jnp.where(row_low, low, high)


def params(mib):
    return pltpu.CompilerParams(vmem_limit_bytes=mib * 2**20)


def join_kernel(*refs):
    at = 0
    for part in refs[:-1]:
        refs[-1][at : at + part.shape[0], :] = part[...]
        at += part.shape[0]


def pack_kernel(band, spectra, low, high, buffer, sems):
    freqs, half = low.shape[:2]
    odd = band[0] % 2
    chunks = buffer.shape[1]
    span = freqs // chunks
    reads, writes = [], []
    for k, out in enumerate((low, high)):
        first = (odd if k == 0 else 1 - odd) * half
        for c in range(chunks):
            rows = pl.ds(c * span, span)
            held = buffer.at[k, c]
            reads.append(
                pltpu.make_async_copy(spectra.at[rows, pl.ds(first, half)], held, sems.at[0, k, c])
            )
            writes.append(pltpu.make_async_copy(held, out.at[rows], sems.at[1, k, c]))
    for copy in reads:
        copy.start()
    for read, write in zip(reads, writes):
        read.wait()
        write.start()
    for copy in writes:
        copy.wait()


def advect_kernel(directions, lev, up, courant, rate, breaking, spectra, halo, land, *refs):
    whole = spectra.shape[1] > halo.shape[1]
    if whole:
        damped, source, other, own, terms, moved, kept, shifts, sems = refs
    else:
        damped, source, terms, moved, kept, shifts = refs
        own = spectra
    freqs = courant.shape[0]
    half = directions // 4
    tiles = -(-half // 2)
    theta = angles_of(directions)
    if whole:
        copies = []
        for k, (first, dst) in enumerate((((1 - up[0]) * half, own), (up[0] * half, other))):
            copies.append(pltpu.make_async_copy(spectra.at[:, pl.ds(first, half)], dst, sems.at[k]))
            copies[-1].start()

    sign = 2 * up[0] - 1
    row = lax.broadcasted_iota(jnp.int32, (128, 128), 0)
    column = lax.broadcasted_iota(jnp.int32, (128, 128), 1)
    for i in range(STEPS):
        for k in range(2):
            move = (1 - 2 * k) * sign * (i + 1)
            hit = (row - column + move + 256) % 128 == 0
            shifts[128 * i : 128 * i + 128, 128 * k : 128 * k + 128] = hit.astype(
                jnp.float32
            ).astype(jnp.bfloat16)

    row = lax.broadcasted_iota(jnp.int32, (8, 128), 0)
    row_low = row < 4
    inner_row = row % 4
    land4 = land[...].astype(jnp.float32)
    mask = jnp.concatenate([land4, land4], axis=0)
    source[...] = jnp.zeros_like(source)
    if whole:
        for copy in copies:
            copy.wait()

    def powers(f, carry, rising):
        speed = courant[f]
        inside = inner_row >= 1 if rising else inner_row <= 2
        step = 1 if rising else 7
        held = []
        for j in range(half):
            cosines = [abs(math.cos(theta[2 * j + k])) for k in range(2)]
            sines = [abs(math.sin(theta[2 * j + k])) for k in range(2)]

            def both(power):
                return halves(row_low, power(cosines[0], sines[0]), power(cosines[1], sines[1]))

            def swapped_both(power):
                return halves(row_low, power(cosines[1], sines[1]), power(cosines[0], sines[0]))

            c = speed * both(lambda x, y: y)
            a = 1.0 - speed * both(lambda x, y: x + y)
            c_outer = speed * swapped_both(lambda x, y: y)
            a_outer = 1.0 - speed * swapped_both(lambda x, y: x + y)
            inner = own[f, j].astype(jnp.float32)
            outer = pltpu.roll(halo[f, j].astype(jnp.float32), 4, 0)
            states = [inner]
            for k in range(STEPS):
                from_outer = pltpu.roll(outer, step, 0)
                inner = a * inner + c * jnp.where(inside, pltpu.roll(inner, step, 0), from_outer)
                states.append(inner)
                if k < STEPS - 1:
                    outer = a_outer * outer + c_outer * from_outer
            kept[f, j] = states[STEPS]
            factors = (
                4.0 * speed, 6.0 * speed * speed, 4.0 * speed * speed * speed,
                speed * speed * speed * speed,
            )
            held.append(
                [
                    (factors[i] * both(lambda x, y, i=i: x ** (i + 1))) * states[STEPS - 1 - i]
                    for i in range(STEPS)
                ]
            )
            if j % 2 or j == half - 1:
                first = held[-2] if j % 2 else held[-1]
                at = pl.ds(pl.multiple_of(f * (16 * tiles) + 16 * (j // 2), 16), 16)
                for i in range(STEPS):
                    tile = jnp.concatenate([first[i], held[-1][i]], axis=0)
                    terms[at, 128 * i : 128 * i + 128] = tile.astype(jnp.bfloat16)
        return carry

    for rising in (True, False):

        @pl.when(up[0] == int(rising))
        def _(rising=rising):
            lax.fori_loop(0, freqs, functools.partial(powers, rising=rising), 0)

    moved[...] = dot(terms[...], shifts[...])

    def finish(f, carry):
        damp = breaking[f]
        gain = (1.0 + 2.0 * (lev[0] * freqs + f).astype(jnp.float32) / (NF - 1)) * rate[f]
        for j in range(half):
            at = pl.ds(pl.multiple_of(f * (16 * tiles) + 8 * j, 8), 8)
            east = [math.cos(theta[2 * j + k]) > 0 for k in range(2)]
            if east[0] == east[1]:
                shifted = moved[at, 0:128] if east[0] else moved[at, 128:256]
            else:
                shifted = halves(row_low, moved[at, 0:128], moved[at, 128:256])
            state = kept[f, j] + shifted
            damped[f, j] = mask * state / (1.0 + damp * state)
            source[j] = source[j] + gain * state
        return carry

    lax.fori_loop(0, freqs, finish, 0)


def build_basis(cosines, sines, cos_table, sin_table, wave_cos, wave_sin):
    waves = wave_cos.shape[0]
    blocks = cos_table.shape[0] // waves
    tens = waves // 8
    units = slice(blocks + tens, blocks + tens + 8)
    for j in range(tens):
        ca, sa = cosines[blocks + j : blocks + j + 1, :], sines[blocks + j : blocks + j + 1, :]
        cb, sb = cosines[units, :], sines[units, :]
        wave_cos[8 * j : 8 * j + 8, :] = ca * cb - sa * sb
        wave_sin[8 * j : 8 * j + 8, :] = sa * cb + ca * sb

    def body(q, carry):
        ca, sa = cosines[pl.ds(q, 1), :], sines[pl.ds(q, 1), :]
        for j in range(0, waves, 16):
            cb, sb = wave_cos[j : j + 16, :], wave_sin[j : j + 16, :]
            rows = pl.ds(pl.multiple_of(q * waves + j, 16), 16)
            cos_table[rows, :] = (ca * cb - sa * sb).astype(jnp.bfloat16)
            sin_table[rows, :] = -(sa * cb + ca * sb).astype(jnp.bfloat16)
        return carry

    lax.fori_loop(0, blocks, body, 0)


def lanes_of(cells):
    return jnp.concatenate([cells[r : r + 1, :] for r in range(cells.shape[0])], axis=1)


def one_hot(coupling, pick):
    longitude = lanes_of(coupling[...]) % 128
    columns = lax.broadcasted_iota(jnp.int32, pick.shape, 0)
    pick[...] = (columns == longitude).astype(jnp.float32).astype(jnp.bfloat16)


def synthesis(groups, phases, cosines, sines, cos_table, sin_table):
    stacked = jnp.concatenate(groups, axis=0) if len(groups) > 1 else groups[0]
    by_cos = dot(stacked, cos_table[...])
    by_sin = dot(stacked, sin_table[...])
    rows = groups[0].shape[0] // 2
    result = None
    for g, phase in enumerate(phases):
        first, middle, end = 2 * g * rows, (2 * g + 1) * rows, (2 * g + 2) * rows
        value = by_cos[first:middle] + by_sin[middle:end]
        if phase:
            at = cosines.shape[0] - 4 + phase
            imag = by_cos[middle:end] - by_sin[first:middle]
            value = cosines[at : at + 1, :] * value - sines[at : at + 1, :] * imag
        result = value if result is None else result + value
    return result


def first_kernel(count, built, cosines, sines, coupling, *refs):
    if built:
        parts, (early, cos_table, sin_table, pick, legs, wave_cos, wave_sin) = (
            refs[:count], refs[count:],
        )
        build_basis(cosines, sines, cos_table, sin_table, wave_cos, wave_sin)
    else:
        cos_table, sin_table = refs[:2]
        parts, (early, pick, legs) = refs[2 : 2 + count], refs[2 + count :]
    one_hot(coupling, pick)
    at = 0
    for part in parts[:-1]:
        legs[at : at + part.shape[0], :] = part[...]
        at += part.shape[0]
    groups = [legs[...].T, parts[-1][...].T]
    early[...] = synthesis(groups, (0, 1), cosines, sines, cos_table, sin_table)


def fourier_kernel(
    lats, share, band, level, early, last, cosines, sines, cos_table, sin_table, pick, coupling,
    grid, wind, hold,
):
    legs = last[...].T
    middle = legs.shape[1] // 2
    groups = [legs[:, :middle], legs[:, middle:]]
    fields = early[...] + synthesis(groups, (2, 3), cosines, sines, cos_table, sin_table)
    hold[...] = fields
    for f in range(FIELDS):
        grid[f] = hold[pl.ds(f * lats + band[0] * share, share), :]
    speed = fields[: 2 * lats] * level[0]
    top = speed.astype(jnp.bfloat16)
    low = (speed - top.astype(jnp.float32)).astype(jnp.bfloat16)
    pieces = [part[:, at : at + 128] for part in (top, low) for at in range(0, LON_W, 128)]
    found = dot(jnp.concatenate(pieces, axis=0), pick[...])
    where = lanes_of(coupling[...])
    latitude = where // LON_W
    group = where % LON_W // 128
    count = LON_W // 128
    row = lax.broadcasted_iota(jnp.int32, (lats, where.shape[1]), 0)
    values = [None, None]
    for a in range(count):
        here = (row == latitude) & (group == a)
        for c in range(2):
            first = (2 * a + c) * lats
            second = (2 * (count + a) + c) * lats
            part = found[first : first + lats] + found[second : second + lats]
            part = jnp.where(here, part, 0.0)
            values[c] = part if a == 0 else values[c] + part
    for c in range(2):
        value = jnp.sum(values[c], axis=0, keepdims=True)
        for r in range(wind.shape[1]):
            wind[c, r : r + 1, :] = value[:, r * 128 : (r + 1) * 128]


def total(parts, index):
    value = parts[0][index]
    for part in parts[1:]:
        value = value + part[index]
    return value


def pushes_of(directions, winds, sign):
    half = directions // 4
    theta = angles_of(directions)
    row_low = lax.broadcasted_iota(jnp.int32, (8, 128), 0) < 4
    east4 = total(winds, 0)
    north4 = total(winds, 1)
    east = sign * jnp.concatenate([east4, east4], axis=0)
    north = sign * jnp.concatenate([north4, north4], axis=0)
    pushes = []
    for j in range(half):
        cosines = halves(row_low, math.cos(theta[2 * j]), math.cos(theta[2 * j + 1]))
        sines = halves(row_low, math.sin(theta[2 * j]), math.sin(theta[2 * j + 1]))
        pushes.append(jnp.maximum(cosines * east + sines * north, 0.0))
    return pushes, east4, north4


def sign_of(up):
    return (2 * up - 1).astype(jnp.float32)


def result_kernel(directions, parts, up, rate, near, far, *refs):
    winds = refs[:parts]
    result, stage, sems = refs[-3:]
    half = directions // 4
    chunks = sems.shape[0]
    span = rate.shape[0] // chunks
    sign = sign_of(up[0])
    sides = [
        (near, (1 - up[0]) * half, pushes_of(directions, winds, sign)[0]),
        (far, up[0] * half, pushes_of(directions, winds, -sign)[0]),
    ]
    copies = []
    for chunk in range(chunks):
        for f in range(chunk * span, (chunk + 1) * span):
            for damped, first, pushes in sides:
                for j in range(half):
                    value = damped[f, j]
                    stage[f, first + j] = value + value * (rate[f] * pushes[j])
        rows = pl.ds(chunk * span, span)
        copies.append(pltpu.make_async_copy(stage.at[rows], result.at[rows], sems.at[chunk]))
        copies[-1].start()
    for copy in copies:
        copy.wait()


def charnock_kernel(directions, parts, up, land, *refs):
    winds, first, second, charnock = (
        refs[:parts], refs[parts : 2 * parts], refs[2 * parts : 3 * parts], refs[3 * parts],
    )
    sign = sign_of(up[0])
    stress = jnp.zeros((8, 128), jnp.float32)
    for sources, way in ((first, sign), (second, -sign)):
        pushes, east, north = pushes_of(directions, winds, way)
        for j, push in enumerate(pushes):
            stress = stress + push * total(sources, j)
    stress = (stress[0:4] + stress[4:8]) * (land[...].astype(jnp.float32) / (NF * directions))
    charnock[...] = 0.011 + 0.5 * stress / (
        stress + 0.05 * (1.0 + east * east + north * north)
    )


def trig(waves):
    columns = jnp.arange(LON_W, dtype=jnp.int32)
    remains = waves[:, None] * columns[None, :] % NLON
    angles = 2.0 * math.pi / NLON * remains.astype(jnp.float32)
    return jnp.cos(angles), jnp.sin(angles)


def on_device_(
    spectral, legendre, level_weights, coupling, land_sea, spectra, courant, growth_rate, breaking
):
    waves, lats, n_total = legendre.shape
    freqs, directions, tile_rows, tile_cols = spectra.shape
    bands = lax.axis_size("band")
    levs = lax.axis_size("lev")
    band = lax.axis_index("band")
    lev = lax.axis_index("lev")
    share = lats // bands
    pairs = directions // 2
    half = directions // 2

    hbm = pl.BlockSpec(memory_space=pltpu.MemorySpace.HBM)
    in_hbm = functools.partial(
        pltpu.with_memory_space_constraint, memory_space=pltpu.MemorySpace.HBM
    )
    in_vmem = functools.partial(
        pltpu.with_memory_space_constraint, memory_space=pltpu.MemorySpace.VMEM
    )
    half_shape = pltpu.MemorySpace.HBM((freqs, half, tile_rows, tile_cols), jnp.bfloat16)
    chunks = 3
    low, high = pl.pallas_call(
        pack_kernel,
        out_shape=[half_shape] * 2,
        in_specs=[SMEM, hbm],
        out_specs=[hbm] * 2,
        scratch_shapes=[
            pltpu.VMEM((2, chunks, freqs // chunks, half, tile_rows, tile_cols), jnp.bfloat16),
            pltpu.SemaphoreType.DMA((2, 2, chunks)),
        ],
        compiler_params=params(4),
        name="pack",
    )(band.reshape(1), in_hbm(spectra))
    low = lax.ppermute(low, "band", [(i, i ^ 1) for i in range(bands)])
    across = [(i, i + 1) for i in range(1, bands - 1, 2)]
    high = lax.ppermute(high, "band", across + [(j, i) for i, j in across])

    stacked = spectral.reshape(waves, 2 * FIELDS, n_total)
    legs = lax.dot_general(
        stacked, legendre, (((2,), (2,)), ((0,), (0,))), preferred_element_type=jnp.float32
    ).astype(jnp.bfloat16)
    numbers = band * waves + jnp.arange(waves, dtype=jnp.int32)
    legs = legs.reshape(waves, 2 * FIELDS * lats)
    legs = legs * jnp.where(numbers == 0, 1.0, 2.0).astype(jnp.bfloat16)[:, None]

    order = [0]
    parts = [legs]
    bits = bits_of(bands)
    small = lats <= 32
    for bit in bits:
        if len(parts) == len(bits) and small:
            rows = sum(part.shape[0] for part in parts)
            together = pl.pallas_call(
                join_kernel,
                out_shape=pltpu.VMEM((rows, legs.shape[1]), jnp.bfloat16),
                in_specs=[VMEM] * len(parts),
                out_specs=VMEM,
                compiler_params=params(2),
                name="join",
            )(*parts)
        else:
            together = jnp.concatenate(parts, axis=0) if len(parts) > 1 else legs
        parts = parts + [swapped(together, "band", bit)]
        if len(parts) < len(bits):
            order = order + [q ^ (1 << bit) for q in order]

    def flipped(bit):
        return (waves << bit) * (1 - 2 * (jnp.right_shift(band, bit) % 2))

    count = len(parts) - 1
    total_rows = bands * waves // 4
    points = tile_rows * tile_cols
    columns = 2 * FIELDS * lats
    table = pltpu.VMEM((total_rows, LON_W), jnp.bfloat16)
    pick_shape = jax.ShapeDtypeStruct((128, points), jnp.bfloat16)
    fields_shape = jax.ShapeDtypeStruct((FIELDS * lats, LON_W), jnp.float32)
    legs_scratch = pltpu.VMEM((total_rows, columns), jnp.bfloat16)
    size = 10 if small else 36
    built = waves % 16 == 0
    blocks = band ^ jnp.asarray(order, dtype=jnp.int32)
    one, two = flipped(bits[-2]), flipped(bits[-1])
    listed = [jnp.stack([one, two, one + two])]
    if built:
        units = jnp.arange(8, dtype=jnp.int32)
        listed = [blocks * waves, 8 * jnp.arange(waves // 8, dtype=jnp.int32), units] + listed
    cos_rows, sin_rows = trig(jnp.concatenate(listed))
    tables = []
    if not built:
        cos_table, sin_table = trig(
            (blocks[:, None] * waves + jnp.arange(waves, dtype=jnp.int32)).reshape(-1)
        )
        tables = [cos_table.astype(jnp.bfloat16), -sin_table.astype(jnp.bfloat16)]
    outs = pl.pallas_call(
        functools.partial(first_kernel, count, built),
        out_shape=[fields_shape] + [table, table] * built + [pick_shape],
        in_specs=[VMEM] * (3 + len(tables) + count),
        out_specs=[VMEM] * (2 + 2 * built),
        scratch_shapes=[legs_scratch] + [pltpu.VMEM((waves, LON_W), jnp.float32)] * (2 * built),
        compiler_params=params(size),
        name="first",
    )(cos_rows, sin_rows, coupling, *tables, *parts[:-1])
    early, pick = outs[0], outs[-1]
    tables = tables or outs[1:3]
    grid, wind = pl.pallas_call(
        functools.partial(fourier_kernel, lats, share),
        out_shape=[
            jax.ShapeDtypeStruct((FIELDS, share, LON_W), jnp.float32),
            jax.ShapeDtypeStruct((2, tile_rows, tile_cols), jnp.float32),
        ],
        in_specs=[SMEM, SMEM] + [VMEM] * 8,
        out_specs=[VMEM] * 2,
        scratch_shapes=[pltpu.VMEM((FIELDS * lats, LON_W), jnp.float32)],
        compiler_params=params(size),
        name="fourier",
    )(
        band.reshape(1), level_weights, early, in_vmem(parts[-1]) if small else parts[-1], cos_rows, sin_rows, *tables, pick, coupling
    )
    grid = jnp.transpose(grid, (1, 0, 2)).reshape(share, 1, FIELDS, LON_W)

    quarter = pairs // 2
    odd = band % 2
    levels = lev.reshape(1)
    own = in_hbm(spectra.reshape(freqs, pairs, 8, 128))
    half_state = pltpu.VMEM((freqs, quarter, 8, 128), jnp.float32)

    def advected(spectra_of, halo, up):
        whole = spectra_of.shape[1] == pairs
        part = pltpu.VMEM((freqs, quarter, 8, 128), jnp.bfloat16)
        tall = 16 * -(-quarter // 2) * freqs
        return pl.pallas_call(
            functools.partial(advect_kernel, directions),
            out_shape=[half_state, pltpu.VMEM((quarter, 8, 128), jnp.float32)] + [part] * whole,
            in_specs=[SMEM] * 5 + [hbm if whole else VMEM, VMEM, VMEM],
            out_specs=[VMEM] * (2 + whole),
            scratch_shapes=[part] * whole
            + [
                pltpu.VMEM((tall, STEPS * 128), jnp.bfloat16),
                pltpu.VMEM((tall, 256), jnp.float32),
                pltpu.VMEM((freqs, quarter, 8, 128), jnp.float32),
                pltpu.VMEM((STEPS * 128, 256), jnp.bfloat16),
            ]
            + [pltpu.SemaphoreType.DMA((2,))] * whole,
            compiler_params=params(12),
        )(
            levels, up, courant, growth_rate, breaking, spectra_of,
            in_vmem(halo.reshape(freqs, quarter, 8, 128)), land_sea,
        )

    def over_lev(value):
        parts = [value]
        bit = 0
        while 1 << bit < levs:
            parts = parts + [swapped(part, "lev", bit) for part in parts]
            bit += 1
        return parts

    near_up, far_up = odd.reshape(1), (1 - odd).reshape(1)
    winds = over_lev(wind)
    near_damped, source, own = advected(own, low, near_up)
    near_sources = over_lev(source)
    far_damped, source = advected(own, high, far_up)
    far_sources = over_lev(source)
    result = pl.pallas_call(
        functools.partial(result_kernel, directions, levs),
        out_shape=pltpu.MemorySpace.HBM((freqs, pairs, 8, 128), jnp.float32),
        in_specs=[SMEM] * 2 + [VMEM] * (2 + levs),
        out_specs=hbm,
        scratch_shapes=[
            pltpu.VMEM((freqs, pairs, 8, 128), jnp.float32),
            pltpu.SemaphoreType.DMA((chunks,)),
        ],
        compiler_params=params(6),
        name="result",
    )(near_up, growth_rate, near_damped, far_damped, *winds)
    charnock = pl.pallas_call(
        functools.partial(charnock_kernel, directions, levs),
        out_shape=jax.ShapeDtypeStruct((tile_rows, tile_cols), jnp.float32),
        in_specs=[SMEM] + [VMEM] * (1 + 3 * levs),
        out_specs=VMEM,
        compiler_params=params(2),
        name="charnock",
    )(near_up, land_sea, *winds, *near_sources, *far_sources)
    return grid, result.reshape(freqs, directions, tile_rows, tile_cols), charnock


def solution(mesh):
    in_specs = (
        P("band", None, "lev", None, None),
        P("band", None, None),
        P("lev"),
        P("band", None),
        P("band", None),
        P("lev", None, "band", None),
        P("lev"),
        P("lev"),
        P("lev"),
    )
    out_specs = (P("band", "lev", None, None), P("lev", None, "band", None), P("band", None))
    return jax.shard_map(
        on_device_, mesh=mesh, in_specs=in_specs, out_specs=out_specs, check_vma=False
    )
```

```python
import functools
import math

import jax
import jax.numpy as jnp
import numpy as np
from jax import lax
from jax.experimental import pallas as pl
from jax.experimental.pallas import tpu as pltpu
from jax.sharding import PartitionSpec as P


NLON = 5136
LON_W = 512
NF = 36
STEPS = 4
FIELDS = 3

VMEM = pl.BlockSpec(memory_space=pltpu.VMEM)
SMEM = pl.BlockSpec(memory_space=pltpu.SMEM)


def swapped(block, axis, apart):
    count = lax.axis_size(axis)
    return lax.ppermute(block, axis, [(i, i ^ (1 << apart)) for i in range(count)])


def bits_of(count):
    bits = count.bit_length() - 1
    return [0, *range(bits - 1, 0, -1)][:bits]


def angles_of(directions):
    return [2.0 * math.pi / directions * (d + 0.5) for d in range(directions)]


dot = functools.partial(jnp.dot, preferred_element_type=jnp.float32)


def halves(row_low, low, high):
    return jnp.where(row_low, low, high)


def params(mib):
    return pltpu.CompilerParams(vmem_limit_bytes=mib * 2**20)


def join_kernel(*refs):
    at = 0
    for part in refs[:-1]:
        refs[-1][at : at + part.shape[0], :] = part[...]
        at += part.shape[0]


def pack_kernel(band, lev, spectra, low, high, buffer, sems):
    freqs, half = low.shape[:2]
    odd = band[0] & 1
    chunks = buffer.shape[1]
    span = freqs // chunks
    reads, writes = [], []
    for k, out in enumerate((low, high)):
        first = (odd if k == 0 else 1 - odd) * half
        for c in range(chunks):
            rows = pl.ds(c * span, span)
            held = buffer.at[k, c]
            reads.append(
                pltpu.make_async_copy(spectra.at[rows, pl.ds(first, half)], held, sems.at[0, k, c])
            )
            writes.append(pltpu.make_async_copy(held, out.at[rows], sems.at[1, k, c]))
    for copy in reads:
        copy.start()
    for read, write in zip(reads, writes):
        read.wait()
        write.start()
    for copy in writes:
        copy.wait()


def shift_matrix():
    table = np.zeros((STEPS * 128, 256), np.float32)
    x = np.arange(128)
    for i in range(STEPS):
        table[128 * i + (x - i - 1) % 128, x] = 1.0
        table[128 * i + (x + i + 1) % 128, 128 + x] = 1.0
    return jnp.asarray(table, jnp.bfloat16)


def advect_kernel(
    directions, flip, lev, band, courant, rate, breaking, spectra, halo, land, shift_table, *refs
):
    whole = spectra.shape[1] > halo.shape[1]
    if whole:
        damped, source, other, own, terms, moved, kept, shifts, sems = refs
    else:
        damped, source, terms, moved, kept, shifts, sems = refs
        own = spectra
    up = (band[0] & 1) ^ flip
    freqs = courant.shape[0]
    half = directions // 4
    tiles = -(-half // 2)
    theta = angles_of(directions)
    shift_copy = pltpu.make_async_copy(shift_table, shifts, sems.at[0])
    shift_copy.start()
    if whole:
        copies = []
        for k, (first, dst) in enumerate((((1 - up) * half, own), (up * half, other))):
            copies.append(pltpu.make_async_copy(spectra.at[:, pl.ds(first, half)], dst, sems.at[1 + k]))
            copies[-1].start()

    row = lax.broadcasted_iota(jnp.int32, (8, 128), 0)
    row_low = row < 4
    inner_row = row % 4
    land4 = land[...].astype(jnp.float32)
    mask = jnp.concatenate([land4, land4], axis=0)
    source[...] = jnp.zeros_like(source)
    if whole:
        for copy in copies:
            copy.wait()

    def powers(f, carry, rising):
        speed = courant[f]
        inside = inner_row >= 1 if rising else inner_row <= 2
        step = 1 if rising else 7
        held = []
        for j in range(half):
            cosines = [abs(math.cos(theta[2 * j + k])) for k in range(2)]
            sines = [abs(math.sin(theta[2 * j + k])) for k in range(2)]

            def both(power):
                return halves(row_low, power(cosines[0], sines[0]), power(cosines[1], sines[1]))

            def swapped_both(power):
                return halves(row_low, power(cosines[1], sines[1]), power(cosines[0], sines[0]))

            c = speed * both(lambda x, y: y)
            a = 1.0 - speed * both(lambda x, y: x + y)
            c_outer = speed * swapped_both(lambda x, y: y)
            a_outer = 1.0 - speed * swapped_both(lambda x, y: x + y)
            inner = own[f, j].astype(jnp.float32)
            outer = pltpu.roll(halo[f, j].astype(jnp.float32), 4, 0)
            states = [inner]
            for k in range(STEPS):
                from_outer = pltpu.roll(outer, step, 0)
                inner = a * inner + c * jnp.where(inside, pltpu.roll(inner, step, 0), from_outer)
                states.append(inner)
                if k < STEPS - 1:
                    outer = a_outer * outer + c_outer * from_outer
            kept[f, j] = states[STEPS]
            factors = (
                4.0 * speed, 6.0 * speed * speed, 4.0 * speed * speed * speed,
                speed * speed * speed * speed,
            )
            held.append(
                [
                    (factors[i] * both(lambda x, y, i=i: x ** (i + 1))) * states[STEPS - 1 - i]
                    for i in range(STEPS)
                ]
            )
            if j % 2 or j == half - 1:
                lower = held[-2] if j % 2 else held[-1]
                at = pl.ds(pl.multiple_of(f * (16 * tiles) + 16 * (j // 2), 16), 16)
                for i in range(STEPS):
                    tile = jnp.concatenate([lower[i], held[-1][i]], axis=0)
                    terms[at, 128 * i : 128 * i + 128] = tile.astype(jnp.bfloat16)
        return carry

    for rising in (True, False):

        @pl.when(up == int(rising))
        def _(rising=rising):
            lax.fori_loop(0, freqs, functools.partial(powers, rising=rising), 0)

    shift_copy.wait()
    moved[...] = dot(terms[...], shifts[...])

    first = pl.multiple_of((1 - up) * 128, 128)

    def finish(f, carry):
        damp = breaking[f]
        gain = (1.0 + 2.0 * (lev[0] * freqs + f).astype(jnp.float32) / (NF - 1)) * rate[f]
        for j in range(half):
            at = pl.ds(pl.multiple_of(f * (16 * tiles) + 8 * j, 8), 8)
            east = [math.cos(theta[2 * j + k]) > 0 for k in range(2)]
            sides = [moved[at, pl.ds(first if way else 128 - first, 128)] for way in east]
            shifted = sides[0] if east[0] == east[1] else halves(row_low, *sides)
            state = kept[f, j] + shifted
            damped[f, j] = mask * state / (1.0 + damp * state)
            source[j] = source[j] + gain * state
        return carry

    lax.fori_loop(0, freqs, finish, 0)


def build_basis(cosines, sines, cos_table, sin_table, wave_cos, wave_sin):
    waves = wave_cos.shape[0]
    blocks = cos_table.shape[0] // waves
    tens = waves // 8
    units = slice(blocks + tens, blocks + tens + 8)
    for j in range(tens):
        ca, sa = cosines[blocks + j : blocks + j + 1, :], sines[blocks + j : blocks + j + 1, :]
        cb, sb = cosines[units, :], sines[units, :]
        wave_cos[8 * j : 8 * j + 8, :] = ca * cb - sa * sb
        wave_sin[8 * j : 8 * j + 8, :] = sa * cb + ca * sb

    def body(q, carry):
        ca, sa = cosines[pl.ds(q, 1), :], sines[pl.ds(q, 1), :]
        for j in range(0, waves, 16):
            cb, sb = wave_cos[j : j + 16, :], wave_sin[j : j + 16, :]
            rows = pl.ds(pl.multiple_of(q * waves + j, 16), 16)
            cos_table[rows, :] = (ca * cb - sa * sb).astype(jnp.bfloat16)
            sin_table[rows, :] = -(sa * cb + ca * sb).astype(jnp.bfloat16)
        return carry

    lax.fori_loop(0, blocks, body, 0)


def lanes_of(cells):
    return jnp.concatenate([cells[r : r + 1, :] for r in range(cells.shape[0])], axis=1)


def one_hot(coupling, pick):
    longitude = lanes_of(coupling[...]) % 128
    columns = lax.broadcasted_iota(jnp.int32, pick.shape, 0)
    pick[...] = (columns == longitude).astype(jnp.float32).astype(jnp.bfloat16)


def synthesis(groups, phases, cosines, sines, cos_table, sin_table):
    stacked = jnp.concatenate(groups, axis=0) if len(groups) > 1 else groups[0]
    by_cos = dot(stacked, cos_table[...])
    by_sin = dot(stacked, sin_table[...])
    rows = groups[0].shape[0] // 2
    result = None
    for g, phase in enumerate(phases):
        first, middle, end = 2 * g * rows, (2 * g + 1) * rows, (2 * g + 2) * rows
        value = by_cos[first:middle] + by_sin[middle:end]
        if phase:
            at = cosines.shape[0] - 4 + phase
            imag = by_cos[middle:end] - by_sin[first:middle]
            value = cosines[at : at + 1, :] * value - sines[at : at + 1, :] * imag
        result = value if result is None else result + value
    return result


def first_kernel(count, built, cosines, sines, coupling, *refs):
    if built:
        parts, (early, cos_table, sin_table, pick, legs, wave_cos, wave_sin) = (
            refs[:count], refs[count:],
        )
        build_basis(cosines, sines, cos_table, sin_table, wave_cos, wave_sin)
    else:
        cos_table, sin_table = refs[:2]
        parts, (early, pick, legs) = refs[2 : 2 + count], refs[2 + count :]
    one_hot(coupling, pick)
    at = 0
    for part in parts[:-1]:
        legs[at : at + part.shape[0], :] = part[...]
        at += part.shape[0]
    groups = [legs[...].T, parts[-1][...].T]
    early[...] = synthesis(groups, (0, 1), cosines, sines, cos_table, sin_table)


def fourier_kernel(
    lats, share, band, level, early, last, cosines, sines, cos_table, sin_table, pick, coupling,
    grid, wind, hold,
):
    legs = last[...].T
    middle = legs.shape[1] // 2
    groups = [legs[:, :middle], legs[:, middle:]]
    fields = early[...] + synthesis(groups, (2, 3), cosines, sines, cos_table, sin_table)
    hold[...] = fields
    for f in range(FIELDS):
        grid[f] = hold[pl.ds(f * lats + band[0] * share, share), :]
    speed = fields[: 2 * lats] * level[0]
    top = speed.astype(jnp.bfloat16)
    low = (speed - top.astype(jnp.float32)).astype(jnp.bfloat16)
    pieces = [part[:, at : at + 128] for part in (top, low) for at in range(0, LON_W, 128)]
    found = dot(jnp.concatenate(pieces, axis=0), pick[...])
    where = lanes_of(coupling[...])
    latitude = where // LON_W
    group = where % LON_W // 128
    count = LON_W // 128
    row = lax.broadcasted_iota(jnp.int32, (lats, where.shape[1]), 0)
    values = [None, None]
    for a in range(count):
        here = (row == latitude) & (group == a)
        for c in range(2):
            first = (2 * a + c) * lats
            second = (2 * (count + a) + c) * lats
            part = found[first : first + lats] + found[second : second + lats]
            part = jnp.where(here, part, 0.0)
            values[c] = part if a == 0 else values[c] + part
    for c in range(2):
        value = jnp.sum(values[c], axis=0, keepdims=True)
        for r in range(wind.shape[1]):
            wind[c, r : r + 1, :] = value[:, r * 128 : (r + 1) * 128]


def total(parts, index):
    value = parts[0][index]
    for part in parts[1:]:
        value = value + part[index]
    return value


def pushes_of(directions, winds, sign):
    half = directions // 4
    theta = angles_of(directions)
    row_low = lax.broadcasted_iota(jnp.int32, (8, 128), 0) < 4
    east4 = total(winds, 0)
    north4 = total(winds, 1)
    east = sign * jnp.concatenate([east4, east4], axis=0)
    north = sign * jnp.concatenate([north4, north4], axis=0)
    pushes = []
    for j in range(half):
        cosines = halves(row_low, math.cos(theta[2 * j]), math.cos(theta[2 * j + 1]))
        sines = halves(row_low, math.sin(theta[2 * j]), math.sin(theta[2 * j + 1]))
        pushes.append(jnp.maximum(cosines * east + sines * north, 0.0))
    return pushes, east4, north4


def result_kernel(directions, parts, band, rate, near, far, *refs):
    winds = refs[:parts]
    result, stage, sems = refs[-3:]
    half = directions // 4
    chunks = sems.shape[0]
    span = rate.shape[0] // chunks
    up = band[0] & 1
    sign = (2 * up - 1).astype(jnp.float32)
    sides = [
        (near, (1 - up) * half, pushes_of(directions, winds, sign)[0]),
        (far, up * half, pushes_of(directions, winds, -sign)[0]),
    ]
    copies = []
    for chunk in range(chunks):
        for f in range(chunk * span, (chunk + 1) * span):
            for damped, first, pushes in sides:
                for j in range(half):
                    value = damped[f, j]
                    stage[f, first + j] = value + value * (rate[f] * pushes[j])
        rows = pl.ds(chunk * span, span)
        copies.append(pltpu.make_async_copy(stage.at[rows], result.at[rows], sems.at[chunk]))
        copies[-1].start()
    for copy in copies:
        copy.wait()


def charnock_kernel(directions, parts, band, land, *refs):
    winds, first, second, charnock = (
        refs[:parts], refs[parts : 2 * parts], refs[2 * parts : 3 * parts], refs[3 * parts],
    )
    up = band[0] & 1
    sign = (2 * up - 1).astype(jnp.float32)
    stress = jnp.zeros((8, 128), jnp.float32)
    for sources, way in ((first, sign), (second, -sign)):
        pushes, east, north = pushes_of(directions, winds, way)
        for j, push in enumerate(pushes):
            stress = stress + push * total(sources, j)
    stress = (stress[0:4] + stress[4:8]) * (land[...].astype(jnp.float32) / (NF * directions))
    charnock[...] = 0.011 + 0.5 * stress / (
        stress + 0.05 * (1.0 + east * east + north * north)
    )


def trig(waves):
    columns = jnp.arange(LON_W, dtype=jnp.int32)
    remains = waves[:, None] * columns[None, :] % NLON
    angles = 2.0 * math.pi / NLON * remains.astype(jnp.float32)
    return jnp.cos(angles), jnp.sin(angles)


def on_device_(
    spectral, legendre, level_weights, coupling, land_sea, spectra, courant, growth_rate, breaking
):
    waves, lats, n_total = legendre.shape
    freqs, directions, tile_rows, tile_cols = spectra.shape
    bands = lax.axis_size("band")
    levs = lax.axis_size("lev")
    band = lax.axis_index("band")
    lev = lax.axis_index("lev")
    share = lats // bands
    pairs = directions // 2
    half = directions // 2

    hbm = pl.BlockSpec(memory_space=pltpu.MemorySpace.HBM)
    in_hbm = functools.partial(
        pltpu.with_memory_space_constraint, memory_space=pltpu.MemorySpace.HBM
    )
    in_vmem = functools.partial(
        pltpu.with_memory_space_constraint, memory_space=pltpu.MemorySpace.VMEM
    )
    half_shape = pltpu.MemorySpace.HBM((freqs, half, tile_rows, tile_cols), jnp.bfloat16)
    chunks = 3
    low, high = pl.pallas_call(
        pack_kernel,
        out_shape=[half_shape] * 2,
        in_specs=[SMEM, SMEM, hbm],
        out_specs=[hbm] * 2,
        scratch_shapes=[
            pltpu.VMEM((2, chunks, freqs // chunks, half, tile_rows, tile_cols), jnp.bfloat16),
            pltpu.SemaphoreType.DMA((2, 2, chunks)),
        ],
        compiler_params=params(4),
        name="pack",
    )(band.reshape(1), lev.reshape(1), in_hbm(spectra))
    low = lax.ppermute(low, "band", [(i, i ^ 1) for i in range(bands)])
    across = [(i, i + 1) for i in range(1, bands - 1, 2)]
    high = lax.ppermute(high, "band", across + [(j, i) for i, j in across])

    stacked = spectral.reshape(waves, 2 * FIELDS, n_total)
    legs = lax.dot_general(
        stacked, legendre, (((2,), (2,)), ((0,), (0,))), preferred_element_type=jnp.float32
    ).astype(jnp.bfloat16)
    numbers = band * waves + jnp.arange(waves, dtype=jnp.int32)
    legs = legs.reshape(waves, 2 * FIELDS * lats)
    legs = legs * jnp.where(numbers == 0, 1.0, 2.0).astype(jnp.bfloat16)[:, None]

    order = [0]
    parts = [legs]
    bits = bits_of(bands)
    small = lats <= 32
    for bit in bits:
        if len(parts) == len(bits) and small:
            rows = sum(part.shape[0] for part in parts)
            together = pl.pallas_call(
                join_kernel,
                out_shape=pltpu.VMEM((rows, legs.shape[1]), jnp.bfloat16),
                in_specs=[VMEM] * len(parts),
                out_specs=VMEM,
                compiler_params=params(2),
                name="join",
            )(*parts)
        else:
            together = jnp.concatenate(parts, axis=0) if len(parts) > 1 else legs
        parts = parts + [swapped(together, "band", bit)]
        if len(parts) < len(bits):
            order = order + [q ^ (1 << bit) for q in order]

    def flipped(bit):
        return (waves << bit) * (1 - 2 * (jnp.right_shift(band, bit) & 1))

    count = len(parts) - 1
    total_rows = bands * waves // 4
    points = tile_rows * tile_cols
    columns = 2 * FIELDS * lats
    table = pltpu.VMEM((total_rows, LON_W), jnp.bfloat16)
    pick_shape = jax.ShapeDtypeStruct((128, points), jnp.bfloat16)
    fields_shape = jax.ShapeDtypeStruct((FIELDS * lats, LON_W), jnp.float32)
    legs_scratch = pltpu.VMEM((total_rows, columns), jnp.bfloat16)
    size = 10 if small else 36
    built = waves % 16 == 0
    blocks = band ^ jnp.asarray(order, dtype=jnp.int32)
    one, two = flipped(bits[-2]), flipped(bits[-1])
    listed = [jnp.stack([one, two, one + two])]
    if built:
        units = jnp.arange(8, dtype=jnp.int32)
        listed = [blocks * waves, 8 * jnp.arange(waves // 8, dtype=jnp.int32), units] + listed
    cos_rows, sin_rows = trig(jnp.concatenate(listed))
    tables = []
    if not built:
        cos_table, sin_table = trig(
            (blocks[:, None] * waves + jnp.arange(waves, dtype=jnp.int32)).reshape(-1)
        )
        tables = [cos_table.astype(jnp.bfloat16), -sin_table.astype(jnp.bfloat16)]
    outs = pl.pallas_call(
        functools.partial(first_kernel, count, built),
        out_shape=[fields_shape] + [table, table] * built + [pick_shape],
        in_specs=[VMEM] * (3 + len(tables) + count),
        out_specs=[VMEM] * (2 + 2 * built),
        scratch_shapes=[legs_scratch] + [pltpu.VMEM((waves, LON_W), jnp.float32)] * (2 * built),
        compiler_params=params(size),
        name="first",
    )(cos_rows, sin_rows, coupling, *tables, *parts[:-1])
    early, pick = outs[0], outs[-1]
    tables = tables or outs[1:3]
    grid, wind = pl.pallas_call(
        functools.partial(fourier_kernel, lats, share),
        out_shape=[
            jax.ShapeDtypeStruct((FIELDS, share, LON_W), jnp.float32),
            jax.ShapeDtypeStruct((2, tile_rows, tile_cols), jnp.float32),
        ],
        in_specs=[SMEM, SMEM] + [VMEM] * 8,
        out_specs=[VMEM] * 2,
        scratch_shapes=[pltpu.VMEM((FIELDS * lats, LON_W), jnp.float32)],
        compiler_params=params(size),
        name="fourier",
    )(
        band.reshape(1), level_weights, early, in_vmem(parts[-1]) if small else parts[-1], cos_rows, sin_rows, *tables, pick, coupling
    )
    grid = jnp.transpose(grid, (1, 0, 2)).reshape(share, 1, FIELDS, LON_W)

    quarter = pairs // 2
    levels, here = lev.reshape(1), band.reshape(1)
    own = in_hbm(spectra.reshape(freqs, pairs, 8, 128))
    half_state = pltpu.VMEM((freqs, quarter, 8, 128), jnp.float32)

    shifts = in_hbm(shift_matrix())

    def advected(spectra_of, halo, flip):
        whole = spectra_of.shape[1] == pairs
        part = pltpu.VMEM((freqs, quarter, 8, 128), jnp.bfloat16)
        tall = 16 * -(-quarter // 2) * freqs
        return pl.pallas_call(
            functools.partial(advect_kernel, directions, flip),
            out_shape=[half_state, pltpu.VMEM((quarter, 8, 128), jnp.float32)] + [part] * whole,
            in_specs=[SMEM] * 5 + [hbm if whole else VMEM] + [VMEM] * 2 + [hbm],
            out_specs=[VMEM] * (2 + whole),
            scratch_shapes=[part] * whole
            + [
                pltpu.VMEM((tall, STEPS * 128), jnp.bfloat16),
                pltpu.VMEM((tall, 256), jnp.float32),
                pltpu.VMEM((freqs, quarter, 8, 128), jnp.float32),
                pltpu.VMEM(shifts.shape, shifts.dtype),
                pltpu.SemaphoreType.DMA((3,)),
            ],
            compiler_params=params(12),
        )(
            levels, here, courant, growth_rate, breaking, spectra_of,
            in_vmem(halo.reshape(freqs, quarter, 8, 128)), land_sea, shifts,
        )

    def over_lev(value):
        parts = [value]
        bit = 0
        while 1 << bit < levs:
            parts = parts + [swapped(part, "lev", bit) for part in parts]
            bit += 1
        return parts

    winds = over_lev(wind)
    near_damped, source, own = advected(own, low, 0)
    near_sources = over_lev(source)
    far_damped, source = advected(own, high, 1)
    far_sources = over_lev(source)
    result = pl.pallas_call(
        functools.partial(result_kernel, directions, levs),
        out_shape=pltpu.MemorySpace.HBM((freqs, pairs, 8, 128), jnp.float32),
        in_specs=[SMEM] * 2 + [VMEM] * (2 + levs),
        out_specs=hbm,
        scratch_shapes=[
            pltpu.VMEM((freqs, pairs, 8, 128), jnp.float32),
            pltpu.SemaphoreType.DMA((chunks,)),
        ],
        compiler_params=params(6),
        name="result",
    )(here, growth_rate, near_damped, far_damped, *winds)
    charnock = pl.pallas_call(
        functools.partial(charnock_kernel, directions, levs),
        out_shape=jax.ShapeDtypeStruct((tile_rows, tile_cols), jnp.float32),
        in_specs=[SMEM] + [VMEM] * (1 + 3 * levs),
        out_specs=VMEM,
        compiler_params=params(2),
        name="charnock",
    )(here, land_sea, *winds, *near_sources, *far_sources)
    return grid, result.reshape(freqs, directions, tile_rows, tile_cols), charnock


def solution(mesh):
    in_specs = (
        P("band", None, "lev", None, None),
        P("band", None, None),
        P("lev"),
        P("band", None),
        P("band", None),
        P("lev", None, "band", None),
        P("lev"),
        P("lev"),
        P("lev"),
    )
    out_specs = (P("band", "lev", None, None), P("lev", None, "band", None), P("band", None))
    return jax.shard_map(
        on_device_, mesh=mesh, in_specs=in_specs, out_specs=out_specs, check_vma=False
    )
```

```python
import functools
import math

import jax
import jax.numpy as jnp
import numpy as np
from jax import lax
from jax.experimental import pallas as pl
from jax.experimental.pallas import tpu as pltpu
from jax.sharding import PartitionSpec as P


NLON = 5136
LON_W = 512
NF = 36
STEPS = 4
FIELDS = 3

VMEM = pl.BlockSpec(memory_space=pltpu.VMEM)
SMEM = pl.BlockSpec(memory_space=pltpu.SMEM)


def swapped(block, axis, apart):
    count = lax.axis_size(axis)
    return lax.ppermute(block, axis, [(i, i ^ (1 << apart)) for i in range(count)])


def bits_of(count):
    bits = count.bit_length() - 1
    return [0, *range(bits - 1, 0, -1)][:bits]


def angles_of(directions):
    return [2.0 * math.pi / directions * (d + 0.5) for d in range(directions)]


dot = functools.partial(jnp.dot, preferred_element_type=jnp.float32)


def halves(row_low, low, high):
    return jnp.where(row_low, low, high)


def params(mib):
    return pltpu.CompilerParams(vmem_limit_bytes=mib * 2**20)


def pack_kernel(band, lev, spectra, low, high, buffer, sems):
    freqs, half = low.shape[:2]
    odd = band[0] & 1
    chunks = sems.shape[2]
    span = freqs // chunks
    reads, writes = [], []
    for k, out in enumerate((low, high)):
        held = buffer.at[k]
        first = (odd if k == 0 else 1 - odd) * half
        for c in range(chunks):
            rows = pl.ds(c * span, span)
            inside = spectra.at[rows, pl.ds(first, half)]
            reads.append(pltpu.make_async_copy(inside, held.at[rows], sems.at[0, k, c]))
            writes.append(pltpu.make_async_copy(held.at[rows], out.at[rows], sems.at[1, k, c]))
    for copy in reads:
        copy.start()
    for read, write in zip(reads, writes):
        read.wait()
        write.start()
    for copy in writes:
        copy.wait()


def shift_matrix():
    table = np.zeros((STEPS * 128, 256), np.float32)
    x = np.arange(128)
    for i in range(STEPS):
        table[128 * i + (x - i - 1) % 128, x] = 1.0
        table[128 * i + (x + i + 1) % 128, 128 + x] = 1.0
    return jnp.asarray(table, jnp.bfloat16)


def advect_kernel(
    directions, flip, lev, band, courant, rate, breaking, own, halo, land, shift_table,
    damped, source, terms, moved, kept, shifts, sems,
):
    up = (band[0] & 1) ^ flip
    freqs = courant.shape[0]
    half = directions // 4
    tiles = -(-half // 2)
    theta = angles_of(directions)
    shift_copy = pltpu.make_async_copy(shift_table, shifts, sems.at[0])
    shift_copy.start()
    row = lax.broadcasted_iota(jnp.int32, (8, 128), 0)
    row_low = row < 4
    inner_row = row % 4
    land4 = land[...].astype(jnp.float32)
    mask = jnp.concatenate([land4, land4], axis=0)
    source[...] = jnp.zeros_like(source)

    def powers(f, carry, rising):
        speed = courant[f]
        inside = inner_row >= 1 if rising else inner_row <= 2
        step = 1 if rising else 7
        held = []
        for j in range(half):
            cosines = [abs(math.cos(theta[2 * j + k])) for k in range(2)]
            sines = [abs(math.sin(theta[2 * j + k])) for k in range(2)]

            def both(power):
                return halves(row_low, power(cosines[0], sines[0]), power(cosines[1], sines[1]))

            def swapped_both(power):
                return halves(row_low, power(cosines[1], sines[1]), power(cosines[0], sines[0]))

            c = speed * both(lambda x, y: y)
            a = 1.0 - speed * both(lambda x, y: x + y)
            c_outer = speed * swapped_both(lambda x, y: y)
            a_outer = 1.0 - speed * swapped_both(lambda x, y: x + y)
            inner = own[f, j].astype(jnp.float32)
            outer = pltpu.roll(halo[f, j].astype(jnp.float32), 4, 0)
            states = [inner]
            for k in range(STEPS):
                from_outer = pltpu.roll(outer, step, 0)
                inner = a * inner + c * jnp.where(inside, pltpu.roll(inner, step, 0), from_outer)
                states.append(inner)
                if k < STEPS - 1:
                    outer = a_outer * outer + c_outer * from_outer
            kept[f, j] = states[STEPS]
            factors = (
                4.0 * speed, 6.0 * speed * speed, 4.0 * speed * speed * speed,
                speed * speed * speed * speed,
            )
            held.append(
                [
                    (factors[i] * both(lambda x, y, i=i: x ** (i + 1))) * states[STEPS - 1 - i]
                    for i in range(STEPS)
                ]
            )
            if j % 2 or j == half - 1:
                lower = held[-2] if j % 2 else held[-1]
                at = pl.ds(pl.multiple_of(f * (16 * tiles) + 16 * (j // 2), 16), 16)
                for i in range(STEPS):
                    tile = jnp.concatenate([lower[i], held[-1][i]], axis=0)
                    terms[at, 128 * i : 128 * i + 128] = tile.astype(jnp.bfloat16)
        return carry

    for rising in (True, False):

        @pl.when(up == int(rising))
        def _(rising=rising):
            lax.fori_loop(0, freqs, functools.partial(powers, rising=rising), 0)

    shift_copy.wait()
    moved[...] = dot(terms[...], shifts[...])

    first = pl.multiple_of((1 - up) * 128, 128)

    def finish(f, carry):
        damp = breaking[f]
        gain = (1.0 + 2.0 * (lev[0] * freqs + f).astype(jnp.float32) / (NF - 1)) * rate[f]
        for j in range(half):
            at = pl.ds(pl.multiple_of(f * (16 * tiles) + 8 * j, 8), 8)
            east = [math.cos(theta[2 * j + k]) > 0 for k in range(2)]
            sides = [moved[at, pl.ds(first if way else 128 - first, 128)] for way in east]
            shifted = sides[0] if east[0] == east[1] else halves(row_low, *sides)
            state = kept[f, j] + shifted
            damped[f, j] = mask * state / (1.0 + damp * state)
            source[j] = source[j] + gain * state
        return carry

    lax.fori_loop(0, freqs, finish, 0)


def basis_kernel(cosines, sines, coupling, cos_table, sin_table, pick, wave_cos, wave_sin):
    waves = wave_cos.shape[0]
    blocks = cos_table.shape[0] // waves
    tens = waves // 8
    units = slice(blocks + tens, blocks + tens + 8)
    for j in range(tens):
        ca, sa = cosines[blocks + j : blocks + j + 1, :], sines[blocks + j : blocks + j + 1, :]
        cb, sb = cosines[units, :], sines[units, :]
        wave_cos[8 * j : 8 * j + 8, :] = ca * cb - sa * sb
        wave_sin[8 * j : 8 * j + 8, :] = sa * cb + ca * sb

    def body(q, carry):
        ca, sa = cosines[pl.ds(q, 1), :], sines[pl.ds(q, 1), :]
        for j in range(0, waves, 16):
            cb, sb = wave_cos[j : j + 16, :], wave_sin[j : j + 16, :]
            rows = pl.ds(pl.multiple_of(q * waves + j, 16), 16)
            cos_table[rows, :] = (ca * cb - sa * sb).astype(jnp.bfloat16)
            sin_table[rows, :] = -(sa * cb + ca * sb).astype(jnp.bfloat16)
        return carry

    lax.fori_loop(0, blocks, body, 0)
    one_hot(coupling, pick)


def lanes_of(cells):
    return jnp.concatenate([cells[r : r + 1, :] for r in range(cells.shape[0])], axis=1)


def one_hot(coupling, pick):
    longitude = lanes_of(coupling[...]) % 128
    columns = lax.broadcasted_iota(jnp.int32, pick.shape, 0)
    pick[...] = (columns == longitude).astype(jnp.float32).astype(jnp.bfloat16)


def synthesis(groups, phases, cosines, sines, cos_table, sin_table):
    stacked = jnp.concatenate(groups, axis=0) if len(groups) > 1 else groups[0]
    by_cos = dot(stacked, cos_table[...])
    by_sin = dot(stacked, sin_table[...])
    rows = groups[0].shape[0] // 2
    result = None
    for g, phase in enumerate(phases):
        first, middle, end = 2 * g * rows, (2 * g + 1) * rows, (2 * g + 2) * rows
        value = by_cos[first:middle] + by_sin[middle:end]
        if phase:
            at = cosines.shape[0] - 1
            imag = by_cos[middle:end] - by_sin[first:middle]
            value = cosines[at : at + 1, :] * value - sines[at : at + 1, :] * imag
        result = value if result is None else result + value
    return result


def first_kernel(
    count, lats, share, last, band, cosines, sines, cos_table, sin_table, *refs
):
    parts, (early, outgoing, legs) = refs[:count], refs[count:]
    at = 0
    for part in parts[:-1]:
        legs[at : at + part.shape[0], :] = part[...]
        at += part.shape[0]
    groups = [legs[...].T, parts[-1][...].T]
    early[...] = synthesis(groups, (0, 1), cosines, sines, cos_table, sin_table)
    outgoing[: 2 * lats, :] = early[: 2 * lats, :]
    theirs = (band[0] ^ (1 << last)) * share
    outgoing[2 * lats :, :] = jnp.zeros_like(outgoing[2 * lats :, :])
    outgoing[2 * lats : 2 * lats + share, :] = early[pl.ds(2 * lats + theirs, share), :]


def fourier_kernel(
    lats, share, band, level, early, incoming, pick, coupling, grid, wind, hold
):
    fields = early[: 2 * lats, :] + incoming[: 2 * lats, :]
    mine = band[0] * share
    grid[2] = early[pl.ds(2 * lats + mine, share), :] + incoming[2 * lats : 2 * lats + share, :]
    hold[...] = fields
    for f in range(2):
        grid[f] = hold[pl.ds(f * lats + mine, share), :]
    speed = fields * level[0]
    top = speed.astype(jnp.bfloat16)
    low = (speed - top.astype(jnp.float32)).astype(jnp.bfloat16)
    pieces = [part[:, at : at + 128] for part in (top, low) for at in range(0, LON_W, 128)]
    found = dot(jnp.concatenate(pieces, axis=0), pick[...])
    where = lanes_of(coupling[...])
    latitude = where // LON_W
    group = where % LON_W // 128
    count = LON_W // 128
    row = lax.broadcasted_iota(jnp.int32, (lats, where.shape[1]), 0)
    values = [None, None]
    for a in range(count):
        here = (row == latitude) & (group == a)
        for c in range(2):
            first = (2 * a + c) * lats
            second = (2 * (count + a) + c) * lats
            part = found[first : first + lats] + found[second : second + lats]
            part = jnp.where(here, part, 0.0)
            values[c] = part if a == 0 else values[c] + part
    for c in range(2):
        value = jnp.sum(values[c], axis=0, keepdims=True)
        for r in range(wind.shape[1]):
            wind[c, r : r + 1, :] = value[:, r * 128 : (r + 1) * 128]


def total(parts, index):
    value = parts[0][index]
    for part in parts[1:]:
        value = value + part[index]
    return value


def pushes_of(directions, winds, sign):
    half = directions // 4
    theta = angles_of(directions)
    row_low = lax.broadcasted_iota(jnp.int32, (8, 128), 0) < 4
    east4 = total(winds, 0)
    north4 = total(winds, 1)
    east = sign * jnp.concatenate([east4, east4], axis=0)
    north = sign * jnp.concatenate([north4, north4], axis=0)
    pushes = []
    for j in range(half):
        cosines = halves(row_low, math.cos(theta[2 * j]), math.cos(theta[2 * j + 1]))
        sines = halves(row_low, math.sin(theta[2 * j]), math.sin(theta[2 * j + 1]))
        pushes.append(jnp.maximum(cosines * east + sines * north, 0.0))
    return pushes, east4, north4


def result_kernel(directions, parts, band, rate, near, far, *refs):
    winds = refs[:parts]
    result, stage, sems = refs[-3:]
    half = directions // 4
    chunks = sems.shape[0]
    span = rate.shape[0] // chunks
    up = band[0] & 1
    sign = (2 * up - 1).astype(jnp.float32)
    sides = [
        (near, (1 - up) * half, pushes_of(directions, winds, sign)[0]),
        (far, up * half, pushes_of(directions, winds, -sign)[0]),
    ]
    copies = []
    for chunk in range(chunks):
        for f in range(chunk * span, (chunk + 1) * span):
            for damped, first, pushes in sides:
                for j in range(half):
                    value = damped[f, j]
                    stage[f, first + j] = value + value * (rate[f] * pushes[j])
        rows = pl.ds(chunk * span, span)
        copies.append(pltpu.make_async_copy(stage.at[rows], result.at[rows], sems.at[chunk]))
        copies[-1].start()
    for copy in copies:
        copy.wait()


def charnock_kernel(directions, parts, band, land, *refs):
    winds, first, second, charnock = (
        refs[:parts], refs[parts : 2 * parts], refs[2 * parts : 3 * parts], refs[3 * parts],
    )
    up = band[0] & 1
    sign = (2 * up - 1).astype(jnp.float32)
    stress = jnp.zeros((8, 128), jnp.float32)
    for sources, way in ((first, sign), (second, -sign)):
        pushes, east, north = pushes_of(directions, winds, way)
        for j, push in enumerate(pushes):
            stress = stress + push * total(sources, j)
    stress = (stress[0:4] + stress[4:8]) * (land[...].astype(jnp.float32) / (NF * directions))
    charnock[...] = 0.011 + 0.5 * stress / (
        stress + 0.05 * (1.0 + east * east + north * north)
    )


def trig(waves):
    columns = jnp.arange(LON_W, dtype=jnp.int32)
    remains = waves[:, None] * columns[None, :] % NLON
    angles = 2.0 * math.pi / NLON * remains.astype(jnp.float32)
    return jnp.cos(angles), jnp.sin(angles)


def on_device_(
    spectral, legendre, level_weights, coupling, land_sea, spectra, courant, growth_rate, breaking
):
    waves, lats, n_total = legendre.shape
    freqs, directions, tile_rows, tile_cols = spectra.shape
    bands = lax.axis_size("band")
    levs = lax.axis_size("lev")
    band = lax.axis_index("band")
    lev = lax.axis_index("lev")
    share = lats // bands
    pairs = directions // 2
    half = directions // 2

    hbm = pl.BlockSpec(memory_space=pltpu.MemorySpace.HBM)
    in_hbm = functools.partial(
        pltpu.with_memory_space_constraint, memory_space=pltpu.MemorySpace.HBM
    )
    half_shape = pltpu.MemorySpace.HBM((freqs, half, tile_rows, tile_cols), jnp.bfloat16)
    chunks = 3
    far_own, near_own = pl.pallas_call(
        pack_kernel,
        out_shape=[half_shape] * 2,
        in_specs=[SMEM, SMEM, hbm],
        out_specs=[hbm] * 2,
        scratch_shapes=[
            pltpu.VMEM((2, freqs, half, tile_rows, tile_cols), jnp.bfloat16),
            pltpu.SemaphoreType.DMA((2, 2, chunks)),
        ],
        compiler_params=params(4),
        name="pack",
    )(band.reshape(1), lev.reshape(1), in_hbm(spectra))
    low = lax.ppermute(far_own, "band", [(i, i ^ 1) for i in range(bands)])
    across = [(i, i + 1) for i in range(1, bands - 1, 2)]
    high = lax.ppermute(near_own, "band", across + [(j, i) for i, j in across])

    stacked = spectral.reshape(waves, 2 * FIELDS, n_total)
    legs = lax.dot_general(
        stacked, legendre, (((2,), (2,)), ((0,), (0,))), preferred_element_type=jnp.float32
    ).astype(jnp.bfloat16)
    numbers = band * waves + jnp.arange(waves, dtype=jnp.int32)
    legs = legs.reshape(waves, 2 * FIELDS * lats)
    legs = legs * jnp.where(numbers == 0, 1.0, 2.0).astype(jnp.bfloat16)[:, None]

    order = [0]
    parts = [legs]
    bits = bits_of(bands)
    for bit in bits[:-1]:
        together = jnp.concatenate(parts, axis=0) if len(parts) > 1 else legs
        parts = parts + [swapped(together, "band", bit)]
        if len(parts) < len(bits):
            order = order + [q ^ (1 << bit) for q in order]

    count = len(parts)
    total_rows = bands * waves // 4
    points = tile_rows * tile_cols
    columns = 2 * FIELDS * lats
    table = pltpu.VMEM((total_rows, LON_W), jnp.bfloat16)
    pick_shape = pltpu.VMEM((128, points), jnp.bfloat16)
    size = 10 if lats <= 32 else 36
    blocks = band ^ jnp.asarray(order, dtype=jnp.int32)
    listed = [((waves << bits[-2]) * (1 - 2 * (jnp.right_shift(band, bits[-2]) & 1))).reshape(1)]
    if waves % 16 == 0:
        units = jnp.arange(8, dtype=jnp.int32)
        listed = [blocks * waves, 8 * jnp.arange(waves // 8, dtype=jnp.int32), units] + listed
    cos_rows, sin_rows = trig(jnp.concatenate(listed))
    if waves % 16 == 0:
        cos_table, sin_table, pick = pl.pallas_call(
            basis_kernel,
            out_shape=[table, table, pick_shape],
            in_specs=[VMEM] * 3,
            out_specs=[VMEM] * 3,
            scratch_shapes=[pltpu.VMEM((waves, LON_W), jnp.float32)] * 2,
            compiler_params=params(4),
            name="basis",
        )(cos_rows, sin_rows, coupling)
    else:
        cos_table, sin_table = trig(
            (blocks[:, None] * waves + jnp.arange(waves, dtype=jnp.int32)).reshape(-1)
        )
        cos_table, sin_table = cos_table.astype(jnp.bfloat16), -sin_table.astype(jnp.bfloat16)
        pick = pl.pallas_call(
            one_hot, out_shape=pick_shape, in_specs=[VMEM], out_specs=VMEM, name="pick"
        )(coupling)
    sent = -(-(2 * lats + share) // 8) * 8
    early, outgoing = pl.pallas_call(
        functools.partial(first_kernel, count, lats, share, bits[-1]),
        out_shape=[
            pltpu.VMEM((FIELDS * lats, LON_W), jnp.float32),
            pltpu.VMEM((sent, LON_W), jnp.float32),
        ],
        in_specs=[SMEM] + [VMEM] * (4 + count),
        out_specs=[VMEM] * 2,
        scratch_shapes=[pltpu.VMEM((total_rows, columns), jnp.bfloat16)],
        compiler_params=params(size),
        name="first",
    )(band.reshape(1), cos_rows, sin_rows, cos_table, sin_table, *parts)
    incoming = swapped(outgoing, "band", bits[-1])
    grid, wind = pl.pallas_call(
        functools.partial(fourier_kernel, lats, share),
        out_shape=[
            jax.ShapeDtypeStruct((FIELDS, share, LON_W), jnp.float32),
            jax.ShapeDtypeStruct((2, tile_rows, tile_cols), jnp.float32),
        ],
        in_specs=[SMEM, SMEM] + [VMEM] * 4,
        out_specs=[VMEM] * 2,
        scratch_shapes=[pltpu.VMEM((2 * lats, LON_W), jnp.float32)],
        compiler_params=params(size),
        name="fourier",
    )(band.reshape(1), level_weights, early, incoming, pick, coupling)
    grid = jnp.transpose(grid, (1, 0, 2)).reshape(share, 1, FIELDS, LON_W)

    quarter = pairs // 2
    levels, here = lev.reshape(1), band.reshape(1)
    half_state = pltpu.VMEM((freqs, quarter, 8, 128), jnp.float32)
    shifts = in_hbm(shift_matrix())

    def advected(own, halo, flip):
        tall = 16 * -(-quarter // 2) * freqs
        return pl.pallas_call(
            functools.partial(advect_kernel, directions, flip),
            out_shape=[half_state, pltpu.VMEM((quarter, 8, 128), jnp.float32)],
            in_specs=[SMEM] * 5 + [VMEM] * 3 + [hbm],
            out_specs=[VMEM] * 2,
            scratch_shapes=[
                pltpu.VMEM((tall, STEPS * 128), jnp.bfloat16),
                pltpu.VMEM((tall, 256), jnp.float32),
                pltpu.VMEM((freqs, quarter, 8, 128), jnp.float32),
                pltpu.VMEM(shifts.shape, shifts.dtype),
                pltpu.SemaphoreType.DMA((1,)),
            ],
            compiler_params=params(12),
        )(
            levels, here, courant, growth_rate, breaking,
            own.reshape(freqs, quarter, 8, 128), halo.reshape(freqs, quarter, 8, 128),
            land_sea, shifts,
        )

    def over_lev(value):
        parts = [value]
        bit = 0
        while 1 << bit < levs:
            parts = parts + [swapped(part, "lev", bit) for part in parts]
            bit += 1
        return parts

    winds = over_lev(wind)
    near_damped, source = advected(near_own, low, 0)
    near_sources = over_lev(source)
    far_damped, source = advected(far_own, high, 1)
    far_sources = over_lev(source)
    result = pl.pallas_call(
        functools.partial(result_kernel, directions, levs),
        out_shape=pltpu.MemorySpace.HBM((freqs, pairs, 8, 128), jnp.float32),
        in_specs=[SMEM] * 2 + [VMEM] * (2 + levs),
        out_specs=hbm,
        scratch_shapes=[
            pltpu.VMEM((freqs, pairs, 8, 128), jnp.float32),
            pltpu.SemaphoreType.DMA((chunks,)),
        ],
        compiler_params=params(6),
        name="result",
    )(here, growth_rate, near_damped, far_damped, *winds)
    charnock = pl.pallas_call(
        functools.partial(charnock_kernel, directions, levs),
        out_shape=jax.ShapeDtypeStruct((tile_rows, tile_cols), jnp.float32),
        in_specs=[SMEM] + [VMEM] * (1 + 3 * levs),
        out_specs=VMEM,
        compiler_params=params(2),
        name="charnock",
    )(here, land_sea, *winds, *near_sources, *far_sources)
    return grid, result.reshape(freqs, directions, tile_rows, tile_cols), charnock


def solution(mesh):
    in_specs = (
        P("band", None, "lev", None, None),
        P("band", None, None),
        P("lev"),
        P("band", None),
        P("band", None),
        P("lev", None, "band", None),
        P("lev"),
        P("lev"),
        P("lev"),
    )
    out_specs = (P("band", "lev", None, None), P("lev", None, "band", None), P("band", None))
    return jax.shard_map(
        on_device_, mesh=mesh, in_specs=in_specs, out_specs=out_specs, check_vma=False
    )
```

```python
import functools
import math

import jax
import jax.numpy as jnp
import numpy as np
from jax import lax
from jax.experimental import pallas as pl
from jax.experimental.pallas import tpu as pltpu
from jax.sharding import PartitionSpec as P


NLON = 5136
LON_W = 512
NF = 36
STEPS = 4
FIELDS = 3

VMEM = pl.BlockSpec(memory_space=pltpu.VMEM)
SMEM = pl.BlockSpec(memory_space=pltpu.SMEM)


def swapped(block, axis, apart):
    count = lax.axis_size(axis)
    return lax.ppermute(block, axis, [(i, i ^ (1 << apart)) for i in range(count)])


def bits_of(count):
    bits = count.bit_length() - 1
    return [*range(bits - 1, 1, -1), 0, 1][-bits:]


def angles_of(directions):
    return [2.0 * math.pi / directions * (d + 0.5) for d in range(directions)]


dot = functools.partial(jnp.dot, preferred_element_type=jnp.float32)


def halves(row_low, low, high):
    return jnp.where(row_low, low, high)


def params(mib):
    return pltpu.CompilerParams(vmem_limit_bytes=mib * 2**20)


def pack_kernel(band, lev, spectra, low, high, buffer, sems):
    freqs, half = low.shape[:2]
    odd = band[0] & 1
    chunks = sems.shape[2]
    span = freqs // chunks
    reads, writes = [], []
    for k, out in enumerate((low, high)):
        held = buffer.at[k]
        first = (odd if k == 0 else 1 - odd) * half
        for c in range(chunks):
            rows = pl.ds(c * span, span)
            inside = spectra.at[rows, pl.ds(first, half)]
            reads.append(pltpu.make_async_copy(inside, held.at[rows], sems.at[0, k, c]))
            writes.append(pltpu.make_async_copy(held.at[rows], out.at[rows], sems.at[1, k, c]))
    for copy in reads:
        copy.start()
    for read, write in zip(reads, writes):
        read.wait()
        write.start()
    for copy in writes:
        copy.wait()


def shift_matrix():
    table = np.zeros((STEPS * 128, 256), np.float32)
    x = np.arange(128)
    for i in range(STEPS):
        table[128 * i + (x - i - 1) % 128, x] = 1.0
        table[128 * i + (x + i + 1) % 128, 128 + x] = 1.0
    return jnp.asarray(table, jnp.bfloat16)


def advect_kernel(
    directions, flip, staged, lev, band, courant, rate, breaking, own_in, halo_in, land, shift_table,
    damped, source, terms, moved, kept, shifts, sems, *staging,
):
    up = (band[0] & 1) ^ flip
    freqs = courant.shape[0]
    half = directions // 4
    tiles = -(-half // 2)
    theta = angles_of(directions)
    shift_copy = pltpu.make_async_copy(shift_table, shifts, sems.at[0])
    shift_copy.start()
    own, halo = staging if staged else (own_in, halo_in)
    chunks = (sems.shape[0] - 1) // 2 if staged else 1
    span = freqs // chunks
    copies = []
    for k in range(chunks if staged else 0):
        part = pl.ds(k * span, span)
        for n, (src, dst) in enumerate(((own_in, own), (halo_in, halo))):
            copy = pltpu.make_async_copy(src.at[part], dst.at[part], sems.at[1 + 2 * k + n])
            copy.start()
            copies.append(copy)
    row = lax.broadcasted_iota(jnp.int32, (8, 128), 0)
    row_low = row < 4
    inner_row = row % 4
    land4 = land[...].astype(jnp.float32)
    mask = jnp.concatenate([land4, land4], axis=0)
    source[...] = jnp.zeros_like(source)

    def powers(f, carry, rising):
        speed = courant[f]
        inside = inner_row >= 1 if rising else inner_row <= 2
        step = 1 if rising else 7
        held = []
        for j in range(half):
            cosines = [abs(math.cos(theta[2 * j + k])) for k in range(2)]
            sines = [abs(math.sin(theta[2 * j + k])) for k in range(2)]

            def both(power):
                return halves(row_low, power(cosines[0], sines[0]), power(cosines[1], sines[1]))

            def swapped_both(power):
                return halves(row_low, power(cosines[1], sines[1]), power(cosines[0], sines[0]))

            c = speed * both(lambda x, y: y)
            a = 1.0 - speed * both(lambda x, y: x + y)
            c_outer = speed * swapped_both(lambda x, y: y)
            a_outer = 1.0 - speed * swapped_both(lambda x, y: x + y)
            inner = own[f, j].astype(jnp.float32)
            outer = pltpu.roll(halo[f, j].astype(jnp.float32), 4, 0)
            states = [inner]
            for k in range(STEPS):
                from_outer = pltpu.roll(outer, step, 0)
                inner = a * inner + c * jnp.where(inside, pltpu.roll(inner, step, 0), from_outer)
                states.append(inner)
                if k < STEPS - 1:
                    outer = a_outer * outer + c_outer * from_outer
            kept[f, j] = states[STEPS]
            factors = (
                4.0 * speed, 6.0 * speed * speed, 4.0 * speed * speed * speed,
                speed * speed * speed * speed,
            )
            held.append(
                [
                    (factors[i] * both(lambda x, y, i=i: x ** (i + 1))) * states[STEPS - 1 - i]
                    for i in range(STEPS)
                ]
            )
            if j % 2 or j == half - 1:
                lower = held[-2] if j % 2 else held[-1]
                at = pl.ds(pl.multiple_of(f * (16 * tiles) + 16 * (j // 2), 16), 16)
                for i in range(STEPS):
                    tile = jnp.concatenate([lower[i], held[-1][i]], axis=0)
                    terms[at, 128 * i : 128 * i + 128] = tile.astype(jnp.bfloat16)
        return carry

    for k in range(chunks):
        for copy in copies[2 * k : 2 * k + 2]:
            copy.wait()
        for rising in (True, False):

            @pl.when(up == int(rising))
            def _(k=k, rising=rising):
                lax.fori_loop(
                    k * span, (k + 1) * span, functools.partial(powers, rising=rising), 0
                )

    shift_copy.wait()
    moved[...] = dot(terms[...], shifts[...])

    first = pl.multiple_of((1 - up) * 128, 128)

    def finish(f, carry):
        damp = breaking[f]
        gain = (1.0 + 2.0 * (lev[0] * freqs + f).astype(jnp.float32) / (NF - 1)) * rate[f]
        for j in range(half):
            at = pl.ds(pl.multiple_of(f * (16 * tiles) + 8 * j, 8), 8)
            east = [math.cos(theta[2 * j + k]) > 0 for k in range(2)]
            sides = [moved[at, pl.ds(first if way else 128 - first, 128)] for way in east]
            shifted = sides[0] if east[0] == east[1] else halves(row_low, *sides)
            state = kept[f, j] + shifted
            damped[f, j] = mask * state / (1.0 + damp * state)
            source[j] = source[j] + gain * state
        return carry

    lax.fori_loop(0, freqs, finish, 0)


def basis_kernel(
    level, cosines, sines, coupling, cos_table, sin_table, pick, weight, wave_cos, wave_sin
):
    waves = wave_cos.shape[0]
    blocks = cos_table.shape[0] // waves
    tens = waves // 8
    units = slice(blocks + tens, blocks + tens + 8)
    for j in range(tens):
        ca, sa = cosines[blocks + j : blocks + j + 1, :], sines[blocks + j : blocks + j + 1, :]
        cb, sb = cosines[units, :], sines[units, :]
        wave_cos[8 * j : 8 * j + 8, :] = ca * cb - sa * sb
        wave_sin[8 * j : 8 * j + 8, :] = sa * cb + ca * sb

    def body(q, carry):
        ca, sa = cosines[pl.ds(q, 1), :], sines[pl.ds(q, 1), :]
        for j in range(0, waves, 16):
            cb, sb = wave_cos[j : j + 16, :], wave_sin[j : j + 16, :]
            rows = pl.ds(pl.multiple_of(q * waves + j, 16), 16)
            cos_table[rows, :] = (ca * cb - sa * sb).astype(jnp.bfloat16)
            sin_table[rows, :] = -(sa * cb + ca * sb).astype(jnp.bfloat16)
        return carry

    lax.fori_loop(0, blocks, body, 0)
    one_hot(coupling, pick)
    weight[...] = jnp.full(weight.shape, level[0], jnp.float32)


def lanes_of(cells):
    return jnp.concatenate([cells[r : r + 1, :] for r in range(cells.shape[0])], axis=1)


def one_hot(coupling, pick):
    longitude = lanes_of(coupling[...]) % 128
    columns = lax.broadcasted_iota(jnp.int32, pick.shape, 0)
    pick[...] = (columns == longitude).astype(jnp.float32).astype(jnp.bfloat16)


def synthesis(groups, phases, cosines, sines, cos_table, sin_table):
    stacked = jnp.concatenate(groups, axis=0) if len(groups) > 1 else groups[0]
    by_cos = dot(stacked, cos_table[...])
    by_sin = dot(stacked, sin_table[...])
    rows = groups[0].shape[0] // 2
    result = None
    for g, phase in enumerate(phases):
        first, middle, end = 2 * g * rows, (2 * g + 1) * rows, (2 * g + 2) * rows
        value = by_cos[first:middle] + by_sin[middle:end]
        if phase:
            at = cosines.shape[0] - 1
            imag = by_cos[middle:end] - by_sin[first:middle]
            value = cosines[at : at + 1, :] * value - sines[at : at + 1, :] * imag
        result = value if result is None else result + value
    return result


def first_kernel(
    count, lats, share, last, band, cosines, sines, cos_table, sin_table, *refs
):
    parts, (early, outgoing, legs) = refs[:count], refs[count:]
    at = 0
    for part in parts[:-1]:
        legs[at : at + part.shape[0], :] = part[...]
        at += part.shape[0]
    groups = [legs[...].T, parts[-1][...].T]
    early[...] = synthesis(groups, (0, 1), cosines, sines, cos_table, sin_table)
    outgoing[: 2 * lats, :] = early[: 2 * lats, :]
    theirs = (band[0] ^ (1 << last)) * share
    outgoing[2 * lats :, :] = jnp.zeros_like(outgoing[2 * lats :, :])
    outgoing[2 * lats : 2 * lats + share, :] = early[pl.ds(2 * lats + theirs, share), :]


def fourier_kernel(
    lats, share, band, level, early, incoming, pick, coupling, grid, wind, hold
):
    fields = early[: 2 * lats, :] + incoming[: 2 * lats, :]
    mine = band[0] * share
    grid[2] = early[pl.ds(2 * lats + mine, share), :] + incoming[2 * lats : 2 * lats + share, :]
    hold[...] = fields
    for f in range(2):
        grid[f] = hold[pl.ds(f * lats + mine, share), :]
    speed = fields * level[0:1, 0:1]
    top = speed.astype(jnp.bfloat16)
    low = (speed - top.astype(jnp.float32)).astype(jnp.bfloat16)
    pieces = [part[:, at : at + 128] for part in (top, low) for at in range(0, LON_W, 128)]
    found = dot(jnp.concatenate(pieces, axis=0), pick[...])
    where = lanes_of(coupling[...])
    latitude = where // LON_W
    group = where % LON_W // 128
    count = LON_W // 128
    row = lax.broadcasted_iota(jnp.int32, (lats, where.shape[1]), 0)
    values = [None, None]
    for a in range(count):
        here = (row == latitude) & (group == a)
        for c in range(2):
            first = (2 * a + c) * lats
            second = (2 * (count + a) + c) * lats
            part = found[first : first + lats] + found[second : second + lats]
            part = jnp.where(here, part, 0.0)
            values[c] = part if a == 0 else values[c] + part
    for c in range(2):
        value = jnp.sum(values[c], axis=0, keepdims=True)
        for r in range(wind.shape[1]):
            wind[c, r : r + 1, :] = value[:, r * 128 : (r + 1) * 128]


def total(parts, index):
    value = parts[0][index]
    for part in parts[1:]:
        value = value + part[index]
    return value


def pushes_of(directions, winds, sign):
    half = directions // 4
    theta = angles_of(directions)
    row_low = lax.broadcasted_iota(jnp.int32, (8, 128), 0) < 4
    east4 = total(winds, 0)
    north4 = total(winds, 1)
    east = sign * jnp.concatenate([east4, east4], axis=0)
    north = sign * jnp.concatenate([north4, north4], axis=0)
    pushes = []
    for j in range(half):
        cosines = halves(row_low, math.cos(theta[2 * j]), math.cos(theta[2 * j + 1]))
        sines = halves(row_low, math.sin(theta[2 * j]), math.sin(theta[2 * j + 1]))
        pushes.append(jnp.maximum(cosines * east + sines * north, 0.0))
    return pushes, east4, north4


def result_kernel(directions, parts, band, rate, near, far, *refs):
    winds = refs[:parts]
    result, stage, sems = refs[-3:]
    half = directions // 4
    chunks = sems.shape[0]
    span = rate.shape[0] // chunks
    up = band[0] & 1
    sign = (2 * up - 1).astype(jnp.float32)
    sides = [
        (near, (1 - up) * half, pushes_of(directions, winds, sign)[0]),
        (far, up * half, pushes_of(directions, winds, -sign)[0]),
    ]
    copies = []
    for chunk in range(chunks):
        for f in range(chunk * span, (chunk + 1) * span):
            for damped, first, pushes in sides:
                for j in range(half):
                    value = damped[f, j]
                    stage[f, first + j] = value + value * (rate[f] * pushes[j])
        rows = pl.ds(chunk * span, span)
        copies.append(pltpu.make_async_copy(stage.at[rows], result.at[rows], sems.at[chunk]))
        copies[-1].start()
    for copy in copies:
        copy.wait()


def charnock_kernel(directions, parts, band, land, *refs):
    winds, first, second, charnock = (
        refs[:parts], refs[parts : 2 * parts], refs[2 * parts : 3 * parts], refs[3 * parts],
    )
    up = band[0] & 1
    sign = (2 * up - 1).astype(jnp.float32)
    stress = jnp.zeros((8, 128), jnp.float32)
    for sources, way in ((first, sign), (second, -sign)):
        pushes, east, north = pushes_of(directions, winds, way)
        for j, push in enumerate(pushes):
            stress = stress + push * total(sources, j)
    stress = (stress[0:4] + stress[4:8]) * (land[...].astype(jnp.float32) / (NF * directions))
    charnock[...] = 0.011 + 0.5 * stress / (
        stress + 0.05 * (1.0 + east * east + north * north)
    )


def trig(waves):
    columns = jnp.arange(LON_W, dtype=jnp.int32)
    remains = waves[:, None] * columns[None, :] % NLON
    angles = 2.0 * math.pi / NLON * remains.astype(jnp.float32)
    return jnp.cos(angles), jnp.sin(angles)


def on_device_(
    spectral, legendre, level_weights, coupling, land_sea, spectra, courant, growth_rate, breaking
):
    waves, lats, n_total = legendre.shape
    freqs, directions, tile_rows, tile_cols = spectra.shape
    bands = lax.axis_size("band")
    levs = lax.axis_size("lev")
    band = lax.axis_index("band")
    lev = lax.axis_index("lev")
    share = lats // bands
    pairs = directions // 2
    half = directions // 2

    hbm = pl.BlockSpec(memory_space=pltpu.MemorySpace.HBM)
    in_hbm = functools.partial(
        pltpu.with_memory_space_constraint, memory_space=pltpu.MemorySpace.HBM
    )
    half_shape = pltpu.MemorySpace.HBM((freqs, half, tile_rows, tile_cols), jnp.bfloat16)
    chunks = 3
    far_own, near_own = pl.pallas_call(
        pack_kernel,
        out_shape=[half_shape] * 2,
        in_specs=[SMEM, SMEM, hbm],
        out_specs=[hbm] * 2,
        scratch_shapes=[
            pltpu.VMEM((2, freqs, half, tile_rows, tile_cols), jnp.bfloat16),
            pltpu.SemaphoreType.DMA((2, 2, chunks)),
        ],
        compiler_params=params(4),
        name="pack",
    )(band.reshape(1), lev.reshape(1), in_hbm(spectra))
    low = lax.ppermute(far_own, "band", [(i, i ^ 1) for i in range(bands)])
    across = [(i, i + 1) for i in range(1, bands - 1, 2)]
    high = lax.ppermute(near_own, "band", across + [(j, i) for i, j in across])

    stacked = spectral.reshape(waves, 2 * FIELDS, n_total)
    legs = lax.dot_general(
        stacked, legendre, (((2,), (2,)), ((0,), (0,))), preferred_element_type=jnp.float32
    ).astype(jnp.bfloat16)
    numbers = band * waves + jnp.arange(waves, dtype=jnp.int32)
    legs = legs.reshape(waves, 2 * FIELDS * lats)
    legs = legs * jnp.where(numbers == 0, 1.0, 2.0).astype(jnp.bfloat16)[:, None]

    order = [0]
    parts = [legs]
    bits = bits_of(bands)
    for bit in bits[:-1]:
        together = jnp.concatenate(parts, axis=0) if len(parts) > 1 else legs
        parts = parts + [swapped(together, "band", bit)]
        if len(parts) < len(bits):
            order = order + [q ^ (1 << bit) for q in order]

    count = len(parts)
    total_rows = bands * waves // 4
    points = tile_rows * tile_cols
    columns = 2 * FIELDS * lats
    table = pltpu.VMEM((total_rows, LON_W), jnp.bfloat16)
    pick_shape = pltpu.VMEM((128, points), jnp.bfloat16)
    size = 10 if lats <= 32 else 36
    blocks = band ^ jnp.asarray(order, dtype=jnp.int32)
    listed = [((waves << bits[-2]) * (1 - 2 * (jnp.right_shift(band, bits[-2]) & 1))).reshape(1)]
    if waves % 16 == 0:
        units = jnp.arange(8, dtype=jnp.int32)
        listed = [blocks * waves, 8 * jnp.arange(waves // 8, dtype=jnp.int32), units] + listed
    cos_rows, sin_rows = trig(jnp.concatenate(listed))
    if waves % 16 == 0:
        cos_table, sin_table, pick, weight = pl.pallas_call(
            basis_kernel,
            out_shape=[table, table, pick_shape, pltpu.VMEM((8, 128), jnp.float32)],
            in_specs=[SMEM] + [VMEM] * 3,
            out_specs=[VMEM] * 4,
            scratch_shapes=[pltpu.VMEM((waves, LON_W), jnp.float32)] * 2,
            compiler_params=params(4),
            name="basis",
        )(level_weights, cos_rows, sin_rows, coupling)
    else:
        weight = jnp.broadcast_to(level_weights, (8, 128))
        cos_table, sin_table = trig(
            (blocks[:, None] * waves + jnp.arange(waves, dtype=jnp.int32)).reshape(-1)
        )
        cos_table, sin_table = cos_table.astype(jnp.bfloat16), -sin_table.astype(jnp.bfloat16)
        pick = pl.pallas_call(
            one_hot, out_shape=pick_shape, in_specs=[VMEM], out_specs=VMEM, name="pick"
        )(coupling)
    sent = -(-(2 * lats + share) // 8) * 8
    early, outgoing = pl.pallas_call(
        functools.partial(first_kernel, count, lats, share, bits[-1]),
        out_shape=[
            pltpu.VMEM((FIELDS * lats, LON_W), jnp.float32),
            pltpu.VMEM((sent, LON_W), jnp.float32),
        ],
        in_specs=[SMEM] + [VMEM] * (4 + count),
        out_specs=[VMEM] * 2,
        scratch_shapes=[pltpu.VMEM((total_rows, columns), jnp.bfloat16)],
        compiler_params=params(size),
        name="first",
    )(band.reshape(1), cos_rows, sin_rows, cos_table, sin_table, *parts)
    incoming = swapped(outgoing, "band", bits[-1])
    grid, wind = pl.pallas_call(
        functools.partial(fourier_kernel, lats, share),
        out_shape=[
            jax.ShapeDtypeStruct((FIELDS, share, LON_W), jnp.float32),
            jax.ShapeDtypeStruct((2, tile_rows, tile_cols), jnp.float32),
        ],
        in_specs=[SMEM] + [VMEM] * 5,
        out_specs=[VMEM] * 2,
        scratch_shapes=[pltpu.VMEM((2 * lats, LON_W), jnp.float32)],
        compiler_params=params(size),
        name="fourier",
    )(band.reshape(1), weight, early, incoming, pick, coupling)
    grid = jnp.transpose(grid, (1, 0, 2)).reshape(share, 1, FIELDS, LON_W)

    quarter = pairs // 2
    levels, here = lev.reshape(1), band.reshape(1)
    half_state = pltpu.VMEM((freqs, quarter, 8, 128), jnp.float32)
    shifts = in_hbm(shift_matrix())

    def advected(own, halo, flip, staged):
        tall = 16 * -(-quarter // 2) * freqs
        part = (freqs, quarter, 8, 128)
        tiles = [own.reshape(part), halo.reshape(part)]
        return pl.pallas_call(
            functools.partial(advect_kernel, directions, flip, staged),
            out_shape=[half_state, pltpu.VMEM((quarter, 8, 128), jnp.float32)],
            in_specs=[SMEM] * 5 + [hbm if staged else VMEM] * 2 + [VMEM, hbm],
            out_specs=[VMEM] * 2,
            scratch_shapes=[
                pltpu.VMEM((tall, STEPS * 128), jnp.bfloat16),
                pltpu.VMEM((tall, 256), jnp.float32),
                pltpu.VMEM(part, jnp.float32),
                pltpu.VMEM(shifts.shape, shifts.dtype),
                pltpu.SemaphoreType.DMA((1 + 2 * chunks * staged,)),
            ]
            + [pltpu.VMEM(part, jnp.bfloat16)] * (2 * staged),
            compiler_params=params(12),
        )(
            levels, here, courant, growth_rate, breaking,
            *(map(in_hbm, tiles) if staged else tiles), land_sea, shifts,
        )

    def over_lev(value):
        parts = [value]
        bit = 0
        while 1 << bit < levs:
            parts = parts + [swapped(part, "lev", bit) for part in parts]
            bit += 1
        return parts

    winds = over_lev(wind)
    near_damped, source = advected(near_own, low, 0, True)
    near_sources = over_lev(source)
    far_damped, source = advected(far_own, high, 1, False)
    far_sources = over_lev(source)
    result = pl.pallas_call(
        functools.partial(result_kernel, directions, levs),
        out_shape=pltpu.MemorySpace.HBM((freqs, pairs, 8, 128), jnp.float32),
        in_specs=[SMEM] * 2 + [VMEM] * (2 + levs),
        out_specs=hbm,
        scratch_shapes=[
            pltpu.VMEM((freqs, pairs, 8, 128), jnp.float32),
            pltpu.SemaphoreType.DMA((2 * chunks if freqs % (2 * chunks) == 0 else chunks,)),
        ],
        compiler_params=params(6),
        name="result",
    )(here, growth_rate, near_damped, far_damped, *winds)
    charnock = pl.pallas_call(
        functools.partial(charnock_kernel, directions, levs),
        out_shape=jax.ShapeDtypeStruct((tile_rows, tile_cols), jnp.float32),
        in_specs=[SMEM] + [VMEM] * (1 + 3 * levs),
        out_specs=VMEM,
        compiler_params=params(2),
        name="charnock",
    )(here, land_sea, *winds, *near_sources, *far_sources)
    return grid, result.reshape(freqs, directions, tile_rows, tile_cols), charnock


def solution(mesh):
    in_specs = (
        P("band", None, "lev", None, None),
        P("band", None, None),
        P("lev"),
        P("band", None),
        P("band", None),
        P("lev", None, "band", None),
        P("lev"),
        P("lev"),
        P("lev"),
    )
    out_specs = (P("band", "lev", None, None), P("lev", None, "band", None), P("band", None))
    return jax.shard_map(
        on_device_, mesh=mesh, in_specs=in_specs, out_specs=out_specs, check_vma=False
    )
```
